32 devices in a mesh: dp: 8 (over y, x, core), tensor: 4 (over z).
Axes of the slice: x: 2, y: 2, z: 4, core: 2. Of those that a mesh axis runs over, the one named last changes fastest.
Arguments:
- tokens: bfloat16 [2, 8, 640, 2048], P(None, 'dp'), may hold values from -6 to 6
- cont_lengths: int32 [2, 8, 8], P(None, 'dp'), may hold values from 1 to 128, 512 in all within a row
- first_gain: bfloat16 [2048], P('dp'), may hold values from 0.25 to 1.75
- first_bias: bfloat16 [2048], P('dp'), may hold values from -4 to 4
- second_gain: bfloat16 [2048], P('dp'), may hold values from 0.25 to 1.75
- second_bias: bfloat16 [2048], P('dp'), may hold values from -4 to 4
- joined_weight: bfloat16 [2048, 6144], P('dp', 'tensor'), may hold values from -0.125 to 0.125
- joined_bias: bfloat16 [8, 768], P('tensor', 'dp'), may hold values from -4 to 4
- dense_weight: bfloat16 [2048, 2048], P('tensor', 'dp'), may hold values from -1 to 1
- dense_bias: bfloat16 [2048], P('dp'), may hold values from -4 to 4
- up_weight: bfloat16 [2048, 8192], P('dp', 'tensor'), may hold values from -0.125 to 0.125
- up_bias: bfloat16 [8, 1024], P('tensor', 'dp'), may hold values from -4 to 4
- down_weight: bfloat16 [8192, 2048], P('tensor', 'dp'), may hold values from -0.0625 to 0.0625
- down_bias: bfloat16 [2048], P('dp'), may hold values from -4 to 4
- cotangent: bfloat16 [2, 8, 640, 2048], P(None, 'dp'), may hold values from -6 to 6
Outputs:
- output: bfloat16 [2, 8, 640, 2048], P(None, 'dp')
- input_grad: bfloat16 [2, 8, 640, 2048], P(None, 'dp')
- first_gain_grad: float32 [2048], P('dp')
- first_bias_grad: float32 [2048], P('dp')
- second_gain_grad: float32 [2048], P('dp')
- second_bias_grad: float32 [2048], P('dp')
- joined_weight_grad: float32 [2048, 6144], P('dp', 'tensor')
- joined_bias_grad: float32 [8, 768], P('tensor', 'dp')
- dense_weight_grad: float32 [2048, 2048], P('tensor', 'dp')
- dense_bias_grad: float32 [2048], P('dp')
- up_weight_grad: float32 [2048, 8192], P('dp', 'tensor')
- up_bias_grad: float32 [8, 1024], P('tensor', 'dp')
- down_weight_grad: float32 [8192, 2048], P('tensor', 'dp')
- down_bias_grad: float32 [2048], P('dp')
The draws below stay inside these ranges and needn't reach their ends.
Inputs may be any that keep to these rules, and one draw needn't show every extreme that they name: `cont_lengths`: in each block the 8 lengths sum to 512; some continuation has exactly 128 tokens.
All inputs are finite; a program needn't handle non-finite values.
Results may differ from the reference program's by a relative error of at most 0.013.
Values may be sent and summed in bfloat16 or wider, within the bound.
No kernel may reach another device: no remote copies, remote signals or barrier semaphores. Data moves between devices by JAX's collectives and lax.ppermute only.
A program may use at most 256 MiB of HBM per device.

```python
import math
import jax
import jax.numpy as jnp
import numpy as np
from jax import lax

D = 2048
HEADS = 8
HEAD_DIM = 256
ROT_DIMS = 64
FF = 8192
PROMPT = 1024
CONT_LEN = 128
MICRO = 2
CT_DEV = 512
BLOCKS = 8
PROMPT_DEV = 128
ROWS = 640
CONT_DEV = 8


def block_levels(key, shape, shards, least, top_value):
    loudness, own = 1.0, jax.random.fold_in(key, 6)
    for dim, parts in shards:
        heights = jnp.exp(jax.random.uniform(jax.random.fold_in(own, dim), (parts,), jnp.float32, least / len(shards), top_value / len(shards)))
        loudness = loudness * jnp.repeat(heights, shape[dim] // parts).reshape([-1 if axis == dim else 1 for axis in range(len(shape))])
    return loudness


def split_up(number_of, total, reach, slope):
    weights = [(1 << 20) // math.isqrt(standing ** slope) + 1 for standing in range(2, number_of + 1)]
    surplus, holding = total - reach - (number_of - 1), [1] * (number_of - 1)
    while surplus > 0:
        movable = [i for i in range(number_of - 1) if holding[i] < reach]
        pool, left = sum([weights[i] for i in movable]), surplus
        for i in movable:
            addition = min(reach - holding[i], max(1, left * weights[i] // pool), surplus)
            holding[i] = holding[i] + addition
            surplus = surplus - addition
    return np.array([reach] + holding)


def uneven(stream_key, count, total, limit, lean):
    if count == 2:
        one = jax.random.randint(stream_key, (), max(1, total - limit), min(limit, total - 1) + 1)
        return jnp.stack([one, total - one])
    sizes = jnp.asarray(split_up(count, total, limit, lean), jnp.int32)
    twos = (count - 1) // 2
    source_of, sink = sizes[1:1 + 2 * twos:2], sizes[2:2 + 2 * twos:2]
    margin = jnp.minimum(source_of - 1, limit - sink)
    moved = jax.random.randint(jax.random.fold_in(stream_key, 1), (twos,), 0, 1 << 20) % (margin + 1)
    sizes = sizes.at[1:1 + 2 * twos:2].set(source_of - moved).at[2:2 + 2 * twos:2].set(sink + moved)
    return sizes[jax.random.permutation(jax.random.fold_in(stream_key, 2), count)]


def gaussian(own_key, dims, deviation, limit, pieces=(), held_as=jnp.bfloat16):
    drawn = deviation * jax.random.normal(own_key, dims, jnp.float32)
    if pieces:
        drawn = drawn * block_levels(own_key, dims, pieces, -0.22, 0.18)
    return jnp.clip(drawn, -limit, limit).astype(held_as)


def setup_inputs(seed: int = 0) -> dict:
    seeds = jax.random.split(jax.random.key(seed), 16)
    return {
        "tokens": gaussian(seeds[0], (MICRO, BLOCKS, ROWS, D), 1.0, 6.0, ((1, 8),)),
        "cont_lengths": jax.vmap(lambda own: uneven(own, CONT_DEV, CT_DEV, CONT_LEN, 1))(jax.random.split(seeds[1], MICRO * BLOCKS)).reshape((MICRO, BLOCKS, CONT_DEV)).astype(jnp.int32),
        "first_gain": jnp.clip(1.0 + 0.15 * jax.random.normal(seeds[2], (D,), jnp.float32), 0.25, 1.75).astype(jnp.bfloat16),
        "first_bias": gaussian(seeds[3], (D,), 0.3, 4.0, ((0, 8),)),
        "second_gain": jnp.clip(1.0 + 0.15 * jax.random.normal(seeds[4], (D,), jnp.float32), 0.25, 1.75).astype(jnp.bfloat16),
        "second_bias": gaussian(seeds[5], (D,), 0.3, 4.0, ((0, 8),)),
        "joined_weight": gaussian(seeds[6], (D, 3 * D), D ** -0.5, 0.125, ((0, 8), (1, 4))),
        "joined_bias": gaussian(seeds[7], (HEADS, 3 * HEAD_DIM), 0.3, 4.0, ((0, 4), (1, 8))),
        "dense_weight": gaussian(seeds[8], (D, D), (max(D // 64, 1)) ** -0.5, 1.0, ((0, 4), (1, 8))),
        "dense_bias": gaussian(seeds[9], (D,), 0.3, 4.0, ((0, 8),)),
        "up_weight": gaussian(seeds[10], (D, FF), D ** -0.5, 0.125, ((0, 8), (1, 4))),
        "up_bias": gaussian(seeds[11], (HEADS, FF // HEADS), 0.5, 4.0, ((0, 4), (1, 8))),
        "down_weight": gaussian(seeds[12], (FF, D), FF ** -0.5, 0.0625, ((0, 4), (1, 8))),
        "down_bias": gaussian(seeds[13], (D,), 0.3, 4.0, ((0, 8),)),
        "cotangent": gaussian(seeds[14], (MICRO, BLOCKS, ROWS, D), 1.0, 6.0, ((1, 8),)),
    }


@jax.custom_vjp
def low(v):
    return lax.optimization_barrier(v.astype(jnp.bfloat16)).astype(jnp.float32)

@jax.custom_vjp
def low_back(v):
    return v

def low_keep(v):
    return (low(v), None)

def low_pass(kept, grad):
    return (grad,)

def back_keep(v):
    return (v, None)

def back_low(kept, grad):
    return (low(grad),)
low.defvjp(low_keep, low_pass)
low_back.defvjp(back_keep, back_low)
norm_eps = 1e-05
rope_base = 10000.0
masked_score = -1e+30

def dot_high(left, right):
    return jnp.dot(left, right, precision=lax.Precision.HIGHEST, preferred_element_type=jnp.float32)

def normalize(values):
    average = lax.optimization_barrier(jnp.mean(values, axis=-1, keepdims=True))
    centered = values - average
    spread = lax.optimization_barrier(jnp.mean(centered * centered, axis=-1, keepdims=True))
    return centered * lax.rsqrt(spread + norm_eps)

def rope_tables(positions, head_size, rot_size):
    halfway = rot_size // 2
    inverse = rope_base ** (-(2.0 * jnp.arange(halfway, dtype=jnp.float32)) / rot_size)
    angles = positions.astype(jnp.float32)[:, None] * inverse[None, :]
    filler = jnp.ones((positions.shape[0], head_size - rot_size), jnp.float32)
    cosine = jnp.concatenate([jnp.cos(angles), jnp.cos(angles), filler], axis=1)[:, None, :]
    sine = jnp.concatenate([jnp.sin(angles), jnp.sin(angles), filler * 0.0], axis=1)[:, None, :]
    return (cosine, sine)

def rotate(values, cosine, sine, rot_size):
    halfway = rot_size // 2
    turned = jnp.concatenate([-values[..., halfway:rot_size], values[..., :halfway], values[..., rot_size:]], axis=-1)
    return values * cosine + turned * sine

def token_tags(lengths, block_index, prompt_rows, tail_rows, prompt_len):
    seg_ends = jnp.cumsum(lengths).astype(jnp.int32)
    slots = jnp.arange(tail_rows, dtype=jnp.int32)
    passed = (slots[:, None] >= seg_ends[None, :]).astype(jnp.int32)
    owners = lax.optimization_barrier(jnp.sum(passed, axis=1)).astype(jnp.int32)
    earlier = lax.optimization_barrier(jnp.sum(passed * lengths[None, :], axis=1)).astype(jnp.int32)
    tail_pos = (prompt_len + slots - earlier).astype(jnp.int32)
    prompt_pos = (block_index * prompt_rows + jnp.arange(prompt_rows, dtype=jnp.int32)).astype(jnp.int32)
    positions = jnp.concatenate([prompt_pos, tail_pos])
    members = jnp.concatenate([jnp.zeros((prompt_rows,), jnp.int32), (owners + 1).astype(jnp.int32)])
    return (positions, members)

def visible(query_pos, query_mem, key_pos, key_mem):
    causal = key_pos[None, :] <= query_pos[:, None]
    related = (key_mem[None, :] == 0) | (key_mem[None, :] == query_mem[:, None])
    return causal & related

def block_forward(element, shared):
    block_x, block_len, block_index = element
    prompt_keys, prompt_values, params = shared
    first_gain, first_bias, second_gain, second_bias, joined_weight, joined_bias, dense_weight, dense_bias, up_weight, up_bias, down_weight, down_bias = params
    normed = normalize(block_x)
    norm_one = low(normed * first_gain + first_bias)
    norm_two = low(normed * second_gain + second_bias)
    joined_rows = low_back(dot_high(norm_one, joined_weight) + joined_bias.reshape(-1)).reshape(ROWS, HEADS, 3, HEAD_DIM)
    positions, members = token_tags(block_len, block_index, PROMPT_DEV, CT_DEV, PROMPT)
    cosine, sine = rope_tables(positions, HEAD_DIM, ROT_DIMS)
    queries = low(rotate(joined_rows[:, :, 0], cosine, sine, ROT_DIMS))
    own_keys = low(rotate(joined_rows[PROMPT_DEV:, :, 1], cosine[PROMPT_DEV:], sine[PROMPT_DEV:], ROT_DIMS))
    own_values = low(joined_rows[PROMPT_DEV:, :, 2])
    all_keys = jnp.concatenate([prompt_keys, own_keys], axis=0)
    all_values = jnp.concatenate([prompt_values, own_values], axis=0)
    key_pos = jnp.concatenate([jnp.arange(PROMPT, dtype=jnp.int32), positions[PROMPT_DEV:]])
    key_mem = jnp.concatenate([jnp.zeros((PROMPT,), jnp.int32), members[PROMPT_DEV:]])
    allowed = visible(positions, members, key_pos, key_mem)
    scores = low_back(jnp.einsum('rhd,khd->hrk', queries, all_keys, precision=lax.Precision.HIGHEST) * HEAD_DIM ** (-0.5))
    scores = jnp.where(allowed[None], scores, masked_score)
    highest = lax.optimization_barrier(jnp.max(scores, axis=-1, keepdims=True))
    raised = jnp.exp(scores - highest)
    softened = raised / lax.optimization_barrier(jnp.sum(raised, axis=-1, keepdims=True))
    context = jnp.einsum('hrk,khd->rhd', low(softened), all_values, precision=lax.Precision.HIGHEST)
    context = low(low_back(context)).reshape(ROWS, D)
    hidden = low_back(dot_high(norm_two, up_weight) + up_bias.reshape(-1))
    activated = low(jax.nn.gelu(hidden, approximate=False))
    return block_x + dot_high(context, dense_weight) + dense_bias + dot_high(activated, down_weight) + down_bias

def group_forward(group_x, group_len, params):
    first_gain, first_bias, second_gain, second_bias, joined_weight, joined_bias, dense_weight, dense_bias, up_weight, up_bias, down_weight, down_bias = params
    prompt_x = group_x[:, :PROMPT_DEV].reshape(PROMPT, D)
    normed = normalize(prompt_x)
    norm_one = low(normed * first_gain + first_bias)
    prompt_joined = low_back(dot_high(norm_one, joined_weight) + joined_bias.reshape(-1)).reshape(PROMPT, HEADS, 3, HEAD_DIM)
    cosine, sine = rope_tables(jnp.arange(PROMPT, dtype=jnp.int32), HEAD_DIM, ROT_DIMS)
    prompt_keys = low(rotate(prompt_joined[:, :, 1], cosine, sine, ROT_DIMS))
    prompt_values = low(prompt_joined[:, :, 2])
    block_step = jax.checkpoint(block_forward)
    shared = (prompt_keys, prompt_values, params)
    indices = jnp.arange(BLOCKS, dtype=jnp.int32)
    return lax.map(lambda element: block_step(element, shared), (group_x, group_len, indices))

def reference(tokens, cont_lengths, first_gain, first_bias, second_gain, second_bias, joined_weight, joined_bias, dense_weight, dense_bias, up_weight, up_bias, down_weight, down_bias, cotangent):
    params = (first_gain.astype(jnp.float32), first_bias.astype(jnp.float32), second_gain.astype(jnp.float32), second_bias.astype(jnp.float32), joined_weight.astype(jnp.float32), joined_bias.astype(jnp.float32), dense_weight.astype(jnp.float32), dense_bias.astype(jnp.float32), up_weight.astype(jnp.float32), up_bias.astype(jnp.float32), down_weight.astype(jnp.float32), down_bias.astype(jnp.float32))
    group_step = jax.checkpoint(group_forward)

    def forward(inputs, weights):
        return lax.map(lambda element: group_step(element[0], element[1], weights), (inputs, cont_lengths))
    output, pullback = jax.vjp(forward, tokens.astype(jnp.float32), params)
    input_grad, param_grads = pullback(cotangent.astype(jnp.float32))
    return (output.astype(jnp.bfloat16), input_grad.astype(jnp.bfloat16), param_grads[0], param_grads[1], param_grads[2], param_grads[3], param_grads[4], param_grads[5], param_grads[6], param_grads[7], param_grads[8], param_grads[9], param_grads[10], param_grads[11])
```

```python
import functools

import jax
import jax.numpy as jnp
from jax import lax
from jax.experimental import pallas as pl
from jax.experimental.pallas import tpu as pltpu
from jax.sharding import PartitionSpec as P

HEAD_DIM = 256
ROT_DIMS = 64
PROMPT = 1024
LONGEST = 128

norm_eps = 1e-05
rope_base = 10000.0
masked_score = -1e30
scale = HEAD_DIM**-0.5
LANES = 128
VMEM = 60 << 20

f32, bf16 = jnp.float32, jnp.bfloat16
NN = (((1,), (0,)), ((), ()))
NT = (((1,), (1,)), ((), ()))
TN = (((0,), (0,)), ((), ()))

TAIL_P = 0.32
TAIL = (
    -0.02115197293220867,
    0.09575628590143809,
    -0.14740109756488956,
    0.06607995422323057,
    -0.0098602948578973,
    0.058840354546090344,
    0.08778712629904878,
    0.11462742044446793,
    0.12766067496581068,
    0.12766153278717104,
)
PEAK = 0.3989422804014327


def dot(a, b, dims=NN):
    return lax.dot_general(a, b, dims, preferred_element_type=f32)


def params(*_):
    return pltpu.CompilerParams(vmem_limit_bytes=VMEM)


def cost(flops, moved, exps=0):
    return pl.CostEstimate(flops=int(flops), bytes_accessed=int(moved), transcendentals=int(exps))


def rope_tables(positions):
    half = ROT_DIMS // 2
    inverse = rope_base ** (-(2.0 * jnp.arange(half, dtype=f32)) / ROT_DIMS)
    angles = positions.astype(f32)[..., None] * inverse
    ones = jnp.ones(positions.shape + (LANES - ROT_DIMS,), f32)
    c, s = jnp.cos(angles), jnp.sin(angles)
    return jnp.concatenate([c, c, ones], -1), jnp.concatenate([-s, s, ones * 0.0], -1)


def swap_halves(u, roll):
    half = ROT_DIMS // 2
    lane = lax.broadcasted_iota(jnp.int32, u.shape, u.ndim - 1)
    up, down = roll(u, LANES - half), roll(u, half)
    return jnp.where(lane < half, up, jnp.where(lane < ROT_DIMS, down, 0.0))


def rotated(u, cosine, signed, roll):
    return u * cosine + swap_halves(u, roll) * signed


def rotated_back(y, cosine, signed, roll):
    return y * cosine + swap_halves(y * signed, roll)


def kernel_roll(u, by):
    return pltpu.roll(u, by, u.ndim - 1)


def plain_roll(u, by):
    return jnp.roll(u, by, -1)


def qkv_kernel(x_ref, w_ref, bias_ref, cos_ref, sin_ref, q_ref, k_ref, v_ref):
    joined = dot(x_ref[...], w_ref[...]) + bias_ref[...]
    c, s = cos_ref[...], sin_ref[...]
    for part, ref in ((0, q_ref), (1, k_ref)):
        base = part * HEAD_DIM
        head = joined[:, base : base + HEAD_DIM]
        ref[:, :LANES] = rotated(head[:, :LANES], c, s, kernel_roll).astype(bf16)
        ref[:, LANES:] = head[:, LANES:].astype(bf16)
    v_ref[...] = joined[:, 2 * HEAD_DIM :].astype(bf16)


def qkv(norm_one, weight, bias, cosine, signed):
    micro, rows, width = norm_one.shape
    wide = 3 * HEAD_DIM
    heads = weight.shape[1] // wide
    head = pl.BlockSpec((None, None, rows, HEAD_DIM), lambda h, m: (m, h, 0, 0))
    table = pl.BlockSpec((None, rows, LANES), lambda h, m: (m, 0, 0))
    return pl.pallas_call(
        qkv_kernel,
        grid=(heads, micro),
        in_specs=[
            pl.BlockSpec((None, rows, width), lambda h, m: (m, 0, 0)),
            pl.BlockSpec((width, wide), lambda h, m: (0, h)),
            pl.BlockSpec((1, wide), lambda h, m: (0, h)),
            table,
            table,
        ],
        out_specs=[head] * 3,
        out_shape=[jax.ShapeDtypeStruct((micro, heads, rows, HEAD_DIM), bf16)] * 3,
        compiler_params=params(),
        cost_estimate=cost(2 * micro * rows * width * heads * wide, 2 * width * heads * wide + 8 * micro * rows * width),
        name="qkv",
    )(norm_one, weight, bias, cosine, signed)


def attention_kernel(
    me_ref, q_ref, k_ref, v_ref, pk_ref, pv_ref, up_ref, first_ref, cos_ref, sin_ref,
    ctx_ref, grad_ref, dpk_ref, dpv_ref, dk_acc, dv_acc,
):
    blocks, own, _ = pk_ref.shape
    rows = q_ref.shape[0]
    tail = rows - own
    shared = blocks * own
    me = me_ref[0]
    pk = pk_ref[...].reshape(shared, HEAD_DIM)
    pv = pv_ref[...].reshape(shared, HEAD_DIM)
    ck, cv = k_ref[own:, :], v_ref[own:, :]
    dk_acc[...] = jnp.zeros_like(dk_acc)
    dv_acc[...] = jnp.zeros_like(dv_acc)

    def chunk(start, count, low, high):
        here = slice(start, start + count)
        q, up = q_ref[here, :], up_ref[here, :]
        sp = dot(q, pk, NT) * scale
        parts = []
        if high > low:
            wk, wv = ck[low:high], cv[low:high]
            sw = dot(q, wk, NT) * scale
            key = lax.broadcasted_iota(jnp.int32, sw.shape, 1) + low
            slot = lax.broadcasted_iota(jnp.int32, sw.shape, 0) + (start - own)
            first = first_ref[start - own : start - own + count, :]
            sw = jnp.where((key >= first) & (key <= slot), sw, masked_score)
            parts = [(sp, pk, pv, 0), (sw, wk, wv, shared + low)]
        else:
            spot = lax.broadcasted_iota(jnp.int32, sp.shape, 1)
            key = lax.bitwise_xor(spot // own, me) * own + spot % own
            slot = lax.broadcasted_iota(jnp.int32, sp.shape, 0) + (me * own + start)
            parts = [(jnp.where(key <= slot, sp, masked_score), pk, pv, 0)]
        highest = functools.reduce(jnp.maximum, [jnp.max(s, -1, keepdims=True) for s, *_ in parts])
        raised = [jnp.exp(s - highest) for s, *_ in parts]
        total = functools.reduce(jnp.add, [jnp.sum(r, -1, keepdims=True) for r in raised])
        inverse = 1.0 / total
        probs = [r * inverse for r in raised]
        lows = [p.astype(bf16) for p in probs]
        ctx = functools.reduce(jnp.add, [dot(p, v) for p, (_, _, v, _) in zip(lows, parts)])
        ctx_ref[here, :] = ctx.astype(bf16)
        dps = [dot(up, v, NT) for _, _, v, _ in parts]
        delta = functools.reduce(
            jnp.add, [jnp.sum(p * d, -1, keepdims=True) for p, d in zip(probs, dps)]
        )
        dss = [(p * (d - delta)).astype(bf16) for p, d in zip(probs, dps)]
        dq = functools.reduce(jnp.add, [dot(d, k) for d, (_, k, _, _) in zip(dss, parts)]) * scale
        c, s = cos_ref[here, :], sin_ref[here, :]
        grad_ref[here, :LANES] = rotated_back(dq[:, :LANES], c, s, kernel_roll).astype(bf16)
        grad_ref[here, LANES:HEAD_DIM] = dq[:, LANES:].astype(bf16)
        for p, d, (_, k, _, base) in zip(lows, dss, parts):
            there = slice(base, base + k.shape[0])
            dv_acc[there, :] += dot(p, up, TN)
            dk_acc[there, :] += dot(d, q, TN)

    chunk(0, own, 0, 0)
    step = 2 * LONGEST
    for at in range(0, tail, step):
        size = min(step, tail - at)
        chunk(own + at, size, max(0, at - LONGEST), at + size)

    dpk_ref[...] = (dk_acc[:shared, :] * scale).astype(bf16).reshape(dpk_ref.shape)
    dpv_ref[...] = dv_acc[:shared, :].astype(bf16).reshape(dpv_ref.shape)
    dk = dk_acc[shared:, :] * scale
    c, s = cos_ref[own:, :], sin_ref[own:, :]
    grad_ref[:own, HEAD_DIM:] = jnp.zeros((own, 2 * HEAD_DIM), bf16)
    grad_ref[own:, HEAD_DIM : HEAD_DIM + LANES] = rotated_back(
        dk[:, :LANES], c, s, kernel_roll
    ).astype(bf16)
    grad_ref[own:, HEAD_DIM + LANES : 2 * HEAD_DIM] = dk[:, LANES:].astype(bf16)
    grad_ref[own:, 2 * HEAD_DIM :] = dv_acc[shared:, :].astype(bf16)


def attention(me, q, k, v, prompt_k, prompt_v, grad_context, first, cosine, signed):
    micro, heads, rows, _ = q.shape
    blocks, _, _, own, _ = prompt_k.shape
    shared, tail = blocks * own, rows - own
    head = pl.BlockSpec((None, None, rows, HEAD_DIM), lambda m, h, _: (m, h, 0, 0))
    prompt = pl.BlockSpec((blocks, None, None, own, HEAD_DIM), lambda m, h, _: (0, m, h, 0, 0))
    flat = pl.BlockSpec((None, rows, HEAD_DIM), lambda m, h, _: (m, 0, h))
    table = pl.BlockSpec((None, rows, LANES), lambda m, h, _: (m, 0, 0))
    flops = 6 * 2 * micro * heads * rows * (shared + 2 * LONGEST) * HEAD_DIM
    return pl.pallas_call(
        attention_kernel,
        grid_spec=pltpu.PrefetchScalarGridSpec(
            num_scalar_prefetch=1,
            grid=(micro, heads),
            in_specs=[head, head, head, prompt, prompt, flat,
                      pl.BlockSpec((None, tail, 1), lambda m, h, _: (m, 0, 0)), table, table],
            out_specs=[flat, pl.BlockSpec((None, rows, 3 * HEAD_DIM), lambda m, h, _: (m, 0, h)), prompt, prompt],
            scratch_shapes=[pltpu.VMEM((shared + tail, HEAD_DIM), f32)] * 2,
        ),
        out_shape=[
            jax.ShapeDtypeStruct((micro, rows, heads * HEAD_DIM), bf16),
            jax.ShapeDtypeStruct((micro, rows, heads * 3 * HEAD_DIM), bf16),
            jax.ShapeDtypeStruct(prompt_k.shape, bf16),
            jax.ShapeDtypeStruct(prompt_k.shape, bf16),
        ],
        compiler_params=params(),
        cost_estimate=cost(flops, 20 * micro * heads * rows * HEAD_DIM, micro * heads * rows * shared),
        name="attention",
    )(me, q, k, v, prompt_k, prompt_v, grad_context, first, cosine, signed)


def back_kernel(g_ref, w_ref, o_ref):
    blocks, _, part = w_ref.shape
    total = dot(g_ref[:, :part], w_ref[0], NT)
    for j in range(1, blocks):
        total += dot(g_ref[:, j * part : (j + 1) * part], w_ref[j], NT)
    o_ref[...] = total.astype(bf16)


def grad_context_of(g, second_weights, wide, skip):
    count, width = g.shape
    blocks, _, part = second_weights.shape
    tile = count // 5 if count % 640 == 0 else count // 4
    return pl.pallas_call(
        back_kernel,
        grid=(count // tile,),
        in_specs=[
            pl.BlockSpec((tile, width), lambda i: (i, 0)),
            pl.BlockSpec((blocks, wide, part), lambda i: (0, skip // wide, 0)),
        ],
        out_specs=pl.BlockSpec((tile, wide), lambda i: (i, 0)),
        out_shape=jax.ShapeDtypeStruct((count, wide), bf16),
        compiler_params=params(),
        cost_estimate=cost(2 * count * width * wide, 2 * count * width + 2 * width * wide),
        name="grad_context",
    )(g, second_weights)


def ff_kernel(n_ref, g_ref, up_ref, down_ref, bias_ref, act_ref, grad_ref, sum_ref):
    blocks, _, part = down_ref.shape
    h = dot(n_ref[...], up_ref[...]) + bias_ref[...]
    ga = dot(g_ref[:, :part], down_ref[0], NT)
    for j in range(1, blocks):
        ga += dot(g_ref[:, j * part : (j + 1) * part], down_ref[j], NT)
    z = jnp.abs(h)
    e = jnp.exp(-0.5 * (h * h))
    t = 1.0 / (1.0 + TAIL_P * z)
    q = jnp.full_like(t, TAIL[0])
    for co in TAIL[1:]:
        q = q * t + co
    low = e * (t * q)
    cdf = jnp.where(h >= 0.0, 1.0 - low, low)
    act_ref[...] = (h * cdf).astype(bf16)
    gh = (ga * (cdf + h * (e * PEAK))).astype(bf16)
    grad_ref[...] = gh

    @pl.when(pl.program_id(1) == 0)
    def _():
        sum_ref[...] = jnp.zeros_like(sum_ref)

    sum_ref[...] += jnp.sum(gh.astype(f32), axis=0, keepdims=True)


def feed_forward(norm_two, g, up_full, second_weights, bias):
    count, width = norm_two.shape
    hidden = up_full.shape[1]
    blocks, _, part = second_weights.shape
    cols = min(1024, hidden)
    tile = count // 5 if count % 640 == 0 else count // 4
    rows_spec = pl.BlockSpec((tile, width), lambda c, r: (r, 0))
    out = pl.BlockSpec((tile, cols), lambda c, r: (r, c))
    return pl.pallas_call(
        ff_kernel,
        grid=(hidden // cols, count // tile),
        in_specs=[
            rows_spec,
            rows_spec,
            pl.BlockSpec((width, cols), lambda c, r: (0, c)),
            pl.BlockSpec((blocks, cols, part), lambda c, r: (0, c, 0)),
            pl.BlockSpec((1, cols), lambda c, r: (0, c)),
        ],
        out_specs=[out, out, pl.BlockSpec((1, cols), lambda c, r: (0, c))],
        out_shape=[
            jax.ShapeDtypeStruct((count, hidden), bf16),
            jax.ShapeDtypeStruct((count, hidden), bf16),
            jax.ShapeDtypeStruct((1, hidden), f32),
        ],
        compiler_params=params(),
        cost_estimate=cost(4 * count * width * hidden, 4 * (count + width) * hidden + 8 * count * width, 2 * count * hidden),
        name="feed_forward",
    )(norm_two, g, up_full, second_weights, bias)


def mix_kernel(act_ref, ctx_ref, w_ref, o_ref):
    hidden = act_ref.shape[1]
    total = dot(act_ref[...], w_ref[:hidden, :])
    total += dot(ctx_ref[...], w_ref[hidden:, :])
    o_ref[...] = total.astype(bf16)


def mix(act, context, second_weights):
    count, hidden = act.shape
    wide = context.shape[1]
    blocks, both, part = second_weights.shape
    return pl.pallas_call(
        mix_kernel,
        grid=(blocks,),
        in_specs=[
            pl.BlockSpec((count, hidden), lambda j: (0, 0)),
            pl.BlockSpec((count, wide), lambda j: (0, 0)),
            pl.BlockSpec((None, both, part), lambda j: (j, 0, 0)),
        ],
        out_specs=pl.BlockSpec((count, part), lambda j: (0, j)),
        out_shape=jax.ShapeDtypeStruct((count, blocks * part), bf16),
        compiler_params=params(),
        cost_estimate=cost(2 * count * both * blocks * part, 2 * count * both + 2 * both * blocks * part),
        name="mix",
    )(act, context, second_weights)


def second_grad_kernel(act_ref, ctx_ref, g_ref, o_ref):
    hidden = act_ref.shape[1]
    o_ref[:hidden, :] = dot(act_ref[...], g_ref[...], TN).astype(bf16)
    o_ref[hidden:, :] = dot(ctx_ref[...], g_ref[...], TN).astype(bf16)


def second_grads(act, context, g, blocks):
    count, hidden = act.shape
    wide = context.shape[1]
    part = g.shape[1] // blocks
    return pl.pallas_call(
        second_grad_kernel,
        grid=(blocks,),
        in_specs=[
            pl.BlockSpec((count, hidden), lambda j: (0, 0)),
            pl.BlockSpec((count, wide), lambda j: (0, 0)),
            pl.BlockSpec((count, part), lambda j: (0, j)),
        ],
        out_specs=pl.BlockSpec((None, hidden + wide, part), lambda j: (j, 0, 0)),
        out_shape=jax.ShapeDtypeStruct((blocks, hidden + wide, part), bf16),
        compiler_params=params(),
        cost_estimate=cost(2 * count * (hidden + wide) * blocks * part, 2 * count * (hidden + wide) + 2 * (hidden + wide) * blocks * part),
        name="second_grads",
    )(act, context, g)


def norm_grad_kernel(gj_ref, gh_ref, wj_ref, wu_ref, x_ref, mean_ref, inv_ref, g1_ref, g2_ref, o_ref, stat_ref):
    one = dot(gj_ref[...], wj_ref[...], NT)
    two = dot(gh_ref[...], wu_ref[...], NT)
    normed = (x_ref[...].astype(f32) - mean_ref[...]) * inv_ref[...]
    o_ref[...] = (one * g1_ref[...] + two * g2_ref[...]).astype(bf16)

    @pl.when(pl.program_id(1) == 0)
    def _():
        stat_ref[...] = jnp.zeros_like(stat_ref)

    for i, term in enumerate((one * normed, one, two * normed, two)):
        stat_ref[i : i + 1, :] += jnp.sum(term, axis=0, keepdims=True)


def norm_grads(grad_joined, grad_hidden, joined_full, up_full, x, mean, inverse, gain_one, gain_two):
    count, width = x.shape
    cols = 512
    tile = count // 5 if count % 640 == 0 else count // 4
    wide, hidden = grad_joined.shape[1], grad_hidden.shape[1]
    out = pl.BlockSpec((tile, cols), lambda c, r: (r, c))
    column = pl.BlockSpec((tile, 1), lambda c, r: (r, 0))
    gain = pl.BlockSpec((1, cols), lambda c, r: (0, c))
    return pl.pallas_call(
        norm_grad_kernel,
        grid=(width // cols, count // tile),
        in_specs=[
            pl.BlockSpec((tile, wide), lambda c, r: (r, 0)),
            pl.BlockSpec((tile, hidden), lambda c, r: (r, 0)),
            pl.BlockSpec((cols, wide), lambda c, r: (c, 0)),
            pl.BlockSpec((cols, hidden), lambda c, r: (c, 0)),
            out, column, column, gain, gain,
        ],
        out_specs=[out, pl.BlockSpec((8, cols), lambda c, r: (0, c))],
        out_shape=[jax.ShapeDtypeStruct((count, width), bf16), jax.ShapeDtypeStruct((8, width), f32)],
        compiler_params=params(),
        cost_estimate=cost(2 * count * width * (wide + hidden), 2 * width * (wide + hidden) + 6 * count * width),
        name="norm_grads",
    )(grad_joined, grad_hidden, joined_full, up_full, x, mean, inverse, gain_one, gain_two)


def swap(value, axis, bit):
    size = lax.axis_size(axis)
    return lax.ppermute(value, axis, [(i, i ^ (1 << bit)) for i in range(size)])


def bits_of(axis):
    return lax.axis_size(axis).bit_length() - 1


def gather_relative(value, axis, order):
    count = bits_of(axis)
    held = value.reshape((1,) * count + value.shape)
    for bit in order:
        held = jnp.concatenate([held, swap(held, axis, bit)], count - 1 - bit)
    return held.reshape((1 << count,) + value.shape)


def scatter_relative(value, axis, order):
    count = bits_of(axis)
    held = value.reshape((2,) * count + value.shape[1:])
    for bit in order:
        dim = count - 1 - bit
        keep = lax.slice_in_dim(held, 0, 1, axis=dim)
        other = swap(lax.slice_in_dim(held, 1, 2, axis=dim), axis, bit)
        held = (keep.astype(f32) + other.astype(f32)).astype(bf16)
    return held.reshape(value.shape[1:])


def own_rows(value, start, count):
    return lax.dynamic_slice_in_dim(value, start, count, 0)


def sum_rows(partial, axis):
    index = lax.axis_index(axis)
    held, start = partial, jnp.int32(0)
    for bit in range(bits_of(axis)):
        mine = (index >> bit) & 1
        half = held.shape[0] // 2
        other = swap(own_rows(held, (1 - mine) * half, half).astype(bf16), axis, bit)
        held = own_rows(held, mine * half, half).astype(f32) + other.astype(f32)
        start = start + mine * half
    return held, start


def spread_rows(share, axis):
    index = lax.axis_index(axis)
    held = share
    for bit in reversed(range(bits_of(axis))):
        mine = (index >> bit) & 1
        other = swap(held, axis, bit)
        held = jnp.where(
            mine == 0, jnp.concatenate([held, other], 0), jnp.concatenate([other, held], 0)
        )
    return held


def local(
    tokens,
    cont_lengths,
    first_gain,
    first_bias,
    second_gain,
    second_bias,
    joined_weight,
    joined_bias,
    dense_weight,
    dense_bias,
    up_weight,
    up_bias,
    down_weight,
    down_bias,
    cotangent,
):
    blocks, ranks = lax.axis_size("dp"), lax.axis_size("tensor")
    me = lax.axis_index("dp").astype(jnp.int32)
    micro, _, rows, width = tokens.shape
    count = micro * rows
    own = PROMPT // blocks
    tail = rows - own
    part = width // blocks
    heads = joined_weight.shape[1] // (3 * HEAD_DIM)
    wide = heads * HEAD_DIM
    hidden = up_weight.shape[1]
    x = tokens.reshape(count, width)
    g = cotangent.reshape(count, width)

    vectors = (first_gain, first_bias, second_gain, second_bias, dense_bias, down_bias)
    small = jnp.concatenate([v.reshape(-1) for v in vectors + (joined_bias, up_bias)])
    small = lax.all_gather(small, "dp", axis=0, tiled=False).astype(f32)
    full = [small[:, i * part : (i + 1) * part].reshape(1, width) for i in range(6)]
    gain_one, bias_one, gain_two, bias_two, dense_add, down_add = full

    def by_head(start, like):
        piece = small[:, start : start + like.size].reshape((blocks,) + like.shape)
        return jnp.transpose(piece, (1, 0, 2)).reshape(1, -1)

    joined_add = by_head(6 * part, joined_bias)
    up_add = by_head(6 * part + joined_bias.size, up_bias)

    joined_full = lax.all_gather(joined_weight, "dp", axis=0, tiled=True)
    second = lax.all_gather(jnp.concatenate([down_weight, dense_weight], 0), "dp", axis=0, tiled=False)
    up_full = lax.all_gather(up_weight, "dp", axis=0, tiled=True)

    seg_ends = jnp.cumsum(cont_lengths[:, 0], axis=1)
    slots = jnp.arange(tail, dtype=jnp.int32)
    passed = (slots[None, :, None] >= seg_ends[:, None, :]).astype(jnp.int32)
    first = jnp.sum(passed * cont_lengths[:, 0][:, None, :], axis=2)
    prompt_pos = jnp.broadcast_to(me * own + jnp.arange(own, dtype=jnp.int32), (micro, own))
    positions = jnp.concatenate([prompt_pos, PROMPT + slots[None] - first], axis=1)
    cosine, signed = rope_tables(positions)

    wide_x = x.astype(f32)
    mean = jnp.mean(wide_x, axis=-1, keepdims=True)
    centered = wide_x - mean
    inverse = lax.rsqrt(jnp.mean(centered * centered, axis=-1, keepdims=True) + norm_eps)
    normed = centered * inverse
    norm_one = (normed * gain_one + bias_one).astype(bf16)
    norm_two = (normed * gain_two + bias_two).astype(bf16)
    upstream_sum = jnp.sum(g.astype(f32), axis=0)

    q, k, v = qkv(norm_one.reshape(micro, rows, width), joined_full, joined_add, cosine, signed)
    top = list(range(1, bits_of("dp")))
    prompt_k = gather_relative(k[:, :, :own], "dp", top + [0])
    prompt_v = gather_relative(v[:, :, :own], "dp", top[::-1] + [0])
    grad_context = grad_context_of(g, second, wide, hidden)
    context, grad_joined, dpk, dpv = attention(
        me.reshape(1), q, k, v, prompt_k, prompt_v, grad_context.reshape(micro, rows, wide),
        first[..., None], cosine, signed,
    )
    context = context.reshape(count, wide)
    key_grad = scatter_relative(dpk, "dp", [0] + top).astype(f32)
    value_grad = scatter_relative(dpv, "dp", [0] + top[::-1])
    c, s = cosine[:, None, :own], signed[:, None, :own]
    key_grad = jnp.concatenate(
        [rotated_back(key_grad[..., :LANES], c, s, plain_roll), key_grad[..., LANES:]], -1
    ).astype(bf16)
    fixed = jnp.stack([key_grad, value_grad], 2)
    fixed = jnp.transpose(fixed, (0, 3, 1, 2, 4))
    grad_joined = grad_joined.reshape(micro, rows, heads, 3, HEAD_DIM)
    grad_joined = lax.dynamic_update_slice(grad_joined, fixed, (0, 0, 0, 1, 0)).reshape(count, 3 * wide)

    act, grad_hidden, up_add_grad = feed_forward(norm_two, g, up_full, second, up_add)

    outputs = []
    for m in range(micro):
        here = slice(m * rows, (m + 1) * rows)
        partial = mix(act[here], context[here], second)
        share, start = sum_rows(partial, "tensor")
        mine = own_rows(x[here], start, share.shape[0]).astype(f32)
        outputs.append(spread_rows((mine + share + dense_add + down_add).astype(bf16), "tensor"))

    second_grad = second_grads(act, context, g, blocks)
    second_out = lax.psum_scatter(second_grad, "dp", scatter_dimension=0, tiled=False).astype(f32)
    up_grad = dot(norm_two, grad_hidden, TN).astype(bf16)
    up_out = lax.psum_scatter(up_grad, "dp", scatter_dimension=0, tiled=True).astype(f32)
    grad_normed, stats = norm_grads(
        grad_joined, grad_hidden, joined_full, up_full, x, mean, inverse, gain_one, gain_two
    )
    joined_grad = dot(norm_one, grad_joined, TN).astype(bf16)
    joined_out = lax.psum_scatter(joined_grad, "dp", scatter_dimension=0, tiled=True).astype(f32)
    joined_add_grad = jnp.sum(grad_joined.astype(f32), axis=0)

    grads = []
    for m in range(micro):
        here = slice(m * rows, (m + 1) * rows)
        share, start = sum_rows(grad_normed[here], "tensor")
        size = share.shape[0]
        row_mean, row_inverse = own_rows(mean[here], start, size), own_rows(inverse[here], start, size)
        row_normed = (own_rows(x[here], start, size).astype(f32) - row_mean) * row_inverse
        centred = (
            share
            - jnp.mean(share, axis=-1, keepdims=True)
            - row_normed * jnp.mean(share * row_normed, axis=-1, keepdims=True)
        )
        result = own_rows(g[here], start, size).astype(f32) + row_inverse * centred
        grads.append(spread_rows(result.astype(bf16), "tensor"))

    gains = lax.psum(stats[:4], "tensor")

    def to_blocks(value, lead):
        value = value.reshape(lead, blocks, -1)
        return jnp.transpose(value, (1, 0, 2)).reshape(blocks, -1)

    pieces = [
        to_blocks(gains, 4),
        to_blocks(upstream_sum, 1),
        to_blocks(joined_add_grad, joined_bias.shape[0]),
        to_blocks(up_add_grad, up_bias.shape[0]),
    ]
    vector = lax.psum_scatter(jnp.concatenate(pieces, 1), "dp", scatter_dimension=0, tiled=False)
    base = 5 * part
    return (
        jnp.stack(outputs)[:, None],
        jnp.stack(grads)[:, None],
        vector[:part],
        vector[part : 2 * part],
        vector[2 * part : 3 * part],
        vector[3 * part : 4 * part],
        joined_out,
        vector[base : base + joined_bias.size].reshape(joined_bias.shape),
        second_out[hidden:],
        vector[4 * part : base],
        up_out,
        vector[base + joined_bias.size :].reshape(up_bias.shape),
        second_out[:hidden],
        vector[4 * part : base],
    )


def solution(mesh):
    placed = (
        P(None, "dp", None, None),
        P(None, "dp", None),
        P("dp"),
        P("dp"),
        P("dp"),
        P("dp"),
        P("dp", "tensor"),
        P("tensor", "dp"),
        P("tensor", "dp"),
        P("dp"),
        P("dp", "tensor"),
        P("tensor", "dp"),
        P("tensor", "dp"),
        P("dp"),
        P(None, "dp", None, None),
    )
    return jax.shard_map(
        local,
        mesh=mesh,
        in_specs=placed,
        out_specs=(
            P(None, "dp", None, None),
            P(None, "dp", None, None),
            P("dp"),
            P("dp"),
            P("dp"),
            P("dp"),
            P("dp", "tensor"),
            P("tensor", "dp"),
            P("tensor", "dp"),
            P("dp"),
            P("dp", "tensor"),
            P("tensor", "dp"),
            P("tensor", "dp"),
            P("dp"),
        ),
        check_vma=False,
    )
```

```python
import functools

import jax
import jax.numpy as jnp
from jax import lax
from jax.experimental import pallas as pl
from jax.experimental.pallas import tpu as pltpu
from jax.sharding import PartitionSpec as P

HEAD_DIM = 256
ROT_DIMS = 64
PROMPT = 1024
LONGEST = 128

norm_eps = 1e-05
rope_base = 10000.0
masked_score = -1e30
scale = HEAD_DIM**-0.5
LANES = 128
VMEM = 60 << 20

f32, bf16 = jnp.float32, jnp.bfloat16
NN = (((1,), (0,)), ((), ()))
NT = (((1,), (1,)), ((), ()))
TN = (((0,), (0,)), ((), ()))

TAIL_P = 0.32
TAIL = (
    -0.02115197293220867,
    0.09575628590143809,
    -0.14740109756488956,
    0.06607995422323057,
    -0.0098602948578973,
    0.058840354546090344,
    0.08778712629904878,
    0.11462742044446793,
    0.12766067496581068,
    0.12766153278717104,
)
PEAK = 0.3989422804014327


def dot(a, b, dims=NN):
    return lax.dot_general(a, b, dims, preferred_element_type=f32)


TIMES = {
    "pack": 2.3,
    "norms": 12.4,
    "qkv": 14.0,
    "grad_context": 7.0,
    "ff_forward": 160.0,
    "attention": 26.0,
    "mix0": 13.0,
    "mix1": 13.0,
    "second_grads": 0.2,
    "fold": 3.5,
    "add_pair": 3.0,
    "finish": 20.0,
    "ff_backward": 19.5,
    "put_prompt": 27.0,
    "norm_grads0": 6.3,
    "norm_grads1": 21.0,
    "outer0": 17.0,
    "outer1": 13.0,
    "place": 4.5,
}
FLOPS = 1.15e9
SHARE = 3.0
CLOSE_FIRST = True
SECOND_AT = 2


def cost(name):
    return pl.CostEstimate(flops=int(TIMES[name] * FLOPS * SHARE), bytes_accessed=0, transcendentals=0)


ANY = pl.BlockSpec(memory_space=pl.ANY)


class Chain:
    def __init__(self):
        self.last = ()

    def run(self, kernel, args, *, grid, ins, outs, shapes, name, key=None, scalars=0, scratch=(), aliases=None):
        count, extra = len(args), tuple(e for e in self.last if all(e is not a for a in args))

        def body(*refs):
            kernel(*refs[:count], *refs[count + len(extra) :])

        results = pl.pallas_call(
            body,
            grid_spec=pltpu.PrefetchScalarGridSpec(
                num_scalar_prefetch=scalars,
                grid=grid,
                in_specs=list(ins) + [ANY] * len(extra),
                out_specs=outs,
                scratch_shapes=list(scratch),
            ),
            out_shape=shapes,
            input_output_aliases=aliases or {},
            compiler_params=pltpu.CompilerParams(vmem_limit_bytes=VMEM),
            cost_estimate=cost(key or name),
            name=name,
        )(*args, *extra)
        self.last = (results[0],)
        return results


def array(shape, dtype=bf16):
    return jax.ShapeDtypeStruct(tuple(shape), dtype)


def rope_tables(positions):
    half = ROT_DIMS // 2
    inverse = rope_base ** (-(2.0 * jnp.arange(half, dtype=f32)) / ROT_DIMS)
    angles = positions.astype(f32)[..., None] * inverse
    ones = jnp.ones(positions.shape + (LANES - ROT_DIMS,), f32)
    c, s = jnp.cos(angles), jnp.sin(angles)
    return jnp.concatenate([c, c, ones], -1), jnp.concatenate([-s, s, ones * 0.0], -1)


def swap_halves(u, roll):
    half = ROT_DIMS // 2
    lane = lax.broadcasted_iota(jnp.int32, u.shape, u.ndim - 1)
    up, down = roll(u, LANES - half), roll(u, half)
    return jnp.where(lane < half, up, jnp.where(lane < ROT_DIMS, down, 0.0))


def rotated(u, cosine, signed, roll):
    return u * cosine + swap_halves(u, roll) * signed


def rotated_back(y, cosine, signed, roll):
    return y * cosine + swap_halves(y * signed, roll)


def kernel_roll(u, by):
    return pltpu.roll(u, by, u.ndim - 1)


def plain_roll(u, by):
    return jnp.roll(u, by, -1)


def norm_kernel(x_ref, g_ref, g1_ref, b1_ref, g2_ref, b2_ref, n1_ref, n2_ref, mean_ref, inv_ref, sum_ref):
    x = x_ref[...].astype(f32)
    mean = jnp.mean(x, axis=-1, keepdims=True)
    centered = x - mean
    inverse = lax.rsqrt(jnp.mean(centered * centered, axis=-1, keepdims=True) + norm_eps)
    normed = centered * inverse
    n1_ref[...] = (normed * g1_ref[...] + b1_ref[...]).astype(bf16)
    n2_ref[...] = (normed * g2_ref[...] + b2_ref[...]).astype(bf16)
    mean_ref[...] = mean
    inv_ref[...] = inverse

    @pl.when(pl.program_id(0) == 0)
    def _():
        sum_ref[...] = jnp.zeros_like(sum_ref)

    sum_ref[...] += jnp.sum(g_ref[...].astype(f32), axis=0, keepdims=True)


def norms(chain, x, g, gain_one, bias_one, gain_two, bias_two):
    count, width = x.shape
    tile = count // 8
    row = pl.BlockSpec((tile, width), lambda i: (i, 0))
    vector = pl.BlockSpec((1, width), lambda i: (0, 0))
    column = pl.BlockSpec((tile, 1), lambda i: (i, 0))
    return chain.run(
        norm_kernel,
        (x, g, gain_one, bias_one, gain_two, bias_two),
        grid=(count // tile,),
        ins=[row, row] + [vector] * 4,
        outs=[row, row, column, column, vector],
        shapes=[array((count, width))] * 2 + [array((count, 1), f32)] * 2 + [array((1, width), f32)],
        name="norms",
    )


def outer_kernel(a_ref, b_ref, o_ref, sum_ref):
    o_ref[...] = dot(a_ref[...], b_ref[...], TN).astype(bf16)

    @pl.when(pl.program_id(0) == 0)
    def _():
        sum_ref[...] = jnp.sum(b_ref[...].astype(f32), axis=0, keepdims=True)


def outer(chain, a, b, key):
    count, width = a.shape
    cols = b.shape[1]
    tile = width // 4
    return chain.run(
        outer_kernel,
        (a, b),
        grid=(4,),
        ins=[pl.BlockSpec((count, tile), lambda i: (0, i)), pl.BlockSpec((count, cols), lambda i: (0, 0))],
        outs=[pl.BlockSpec((tile, cols), lambda i: (i, 0)), pl.BlockSpec((1, cols), lambda i: (0, 0))],
        shapes=[array((width, cols)), array((1, cols), f32)],
        name="outer",
        key=key,
    )


def place_kernel(flag_ref, *refs):
    o_ref = refs[-1]
    pieces = len(refs) // 2 if len(refs) % 2 else len(refs) // 2 - 1
    for i in range(pieces):
        for flag in (0, 1):

            @pl.when((flag_ref[0] == flag) & (pl.program_id(0) // 2 == i))
            def _():
                o_ref[...] = refs[2 * i + flag][...]


def place(chain, held, flag, pieces, start, total):
    size, width = pieces[0].own.shape
    tile = size // 2
    keep = () if held is None else (held,)
    ins, args = [], []
    for i, piece in enumerate(pieces):
        args += [piece.own, piece.third]
        ins += [
            pl.BlockSpec((tile, width), lambda j, flag, i=i: (jnp.clip(j - 2 * i, 0, 1) * (1 - flag[0]), 0)),
            pl.BlockSpec((tile, width), lambda j, flag, i=i: (jnp.clip(j - 2 * i, 0, 1) * flag[0], 0)),
        ]
    return chain.run(
        place_kernel,
        (flag, *args) + keep,
        scalars=1,
        grid=(2 * len(pieces),),
        ins=ins + [ANY] * len(keep),
        outs=[pl.BlockSpec((tile, width), lambda j, _: (start // tile + j, 0))],
        shapes=[array((total, width))],
        aliases={1 + len(args): 0} if keep else {},
        name="place",
    )[0]


def pack_kernel(joined_ref, dense_ref, o_ref):
    wide = joined_ref.shape[1]
    o_ref[:, :wide] = joined_ref[...]
    o_ref[:, wide:] = dense_ref[...].T


def pack(chain, joined, dense):
    part, wide = joined.shape
    total = wide + dense.shape[0]

    def whole(rows, columns):
        return pl.BlockSpec((rows, columns), lambda i: (0, 0))

    return chain.run(
        pack_kernel,
        (joined, dense),
        grid=(1,),
        ins=[whole(*joined.shape), whole(*dense.shape)],
        outs=[whole(part, total)],
        shapes=[array((part, total))],
        name="pack",
    )[0]


def qkv_kernel(x_ref, w_ref, bias_ref, cos_ref, sin_ref, q_ref, k_ref, v_ref, prompt_ref):
    joined = dot(x_ref[...], w_ref[...]) + bias_ref[...]
    c, s = cos_ref[...], sin_ref[...]
    for part, ref in ((0, q_ref), (1, k_ref)):
        base = part * HEAD_DIM
        head = joined[:, base : base + HEAD_DIM]
        ref[:, :LANES] = rotated(head[:, :LANES], c, s, kernel_roll).astype(bf16)
        ref[:, LANES:] = head[:, LANES:].astype(bf16)
    v_ref[...] = joined[:, 2 * HEAD_DIM :].astype(bf16)
    own = prompt_ref.shape[1]
    prompt_ref[0] = k_ref[:own, :]
    prompt_ref[1] = v_ref[:own, :]


def qkv(chain, norm_one, weight, bias, cosine, signed, own):
    micro, rows, width = norm_one.shape
    wide = 3 * HEAD_DIM
    heads = bias.shape[1] // wide
    head = pl.BlockSpec((None, None, rows, HEAD_DIM), lambda h, m: (m, h, 0, 0))
    table = pl.BlockSpec((None, rows, LANES), lambda h, m: (m, 0, 0))
    return chain.run(
        qkv_kernel,
        (norm_one, weight, bias, cosine, signed),
        grid=(heads, micro),
        ins=[
            pl.BlockSpec((None, rows, width), lambda h, m: (m, 0, 0)),
            pl.BlockSpec((width, wide), lambda h, m: (0, h)),
            pl.BlockSpec((1, wide), lambda h, m: (0, h)),
            table,
            table,
        ],
        outs=[head] * 3 + [pl.BlockSpec((2, None, None, own, HEAD_DIM), lambda h, m: (0, m, h, 0, 0))],
        shapes=[array((micro, heads, rows, HEAD_DIM))] * 3 + [array((2, micro, heads, own, HEAD_DIM))],
        name="qkv",
    )


def attention_kernel(layout, me_ref, q_ref, k_ref, v_ref, up_ref, first_ref, cos_ref, sin_ref, *refs):
    ctx_ref, grad_ref, keep_ref, send_ref, dk_acc, dv_acc = refs[-6:]
    blocks, own = len(layout), refs[0].shape[1]
    rows = q_ref.shape[0]
    tail = rows - own
    shared = blocks * own
    me = me_ref[0]
    pk = jnp.concatenate([refs[spots[0]][0] for spots in layout], 0)
    pv = jnp.concatenate([refs[spots[-1]][refs[spots[-1]].shape[0] - 1] for spots in layout], 0)
    ck, cv = k_ref[own:, :], v_ref[own:, :]
    dk_acc[...] = jnp.zeros_like(dk_acc)
    dv_acc[...] = jnp.zeros_like(dv_acc)

    def chunk(start, count, low, high):
        here = slice(start, start + count)
        q, up = q_ref[here, :], up_ref[here, :]
        sp = dot(q, pk, NT) * scale
        parts = []
        if high > low:
            wk, wv = ck[low:high], cv[low:high]
            sw = dot(q, wk, NT) * scale
            key = lax.broadcasted_iota(jnp.int32, sw.shape, 1) + low
            slot = lax.broadcasted_iota(jnp.int32, sw.shape, 0) + (start - own)
            first = first_ref[start - own : start - own + count, :]
            sw = jnp.where((key >= first) & (key <= slot), sw, masked_score)
            parts = [(sp, pk, pv, 0), (sw, wk, wv, shared + low)]
        else:
            spot = lax.broadcasted_iota(jnp.int32, sp.shape, 1)
            key = lax.bitwise_xor(spot // own, me) * own + spot % own
            slot = lax.broadcasted_iota(jnp.int32, sp.shape, 0) + (me * own + start)
            parts = [(jnp.where(key <= slot, sp, masked_score), pk, pv, 0)]
        highest = functools.reduce(jnp.maximum, [jnp.max(s, -1, keepdims=True) for s, *_ in parts])
        raised = [jnp.exp(s - highest) for s, *_ in parts]
        total = functools.reduce(jnp.add, [jnp.sum(r, -1, keepdims=True) for r in raised])
        inverse = 1.0 / total
        probs = [r * inverse for r in raised]
        lows = [p.astype(bf16) for p in probs]
        ctx = functools.reduce(jnp.add, [dot(p, v) for p, (_, _, v, _) in zip(lows, parts)])
        ctx_ref[here, :] = ctx.astype(bf16)
        dps = [dot(up, v, NT) for _, _, v, _ in parts]
        delta = functools.reduce(
            jnp.add, [jnp.sum(p * d, -1, keepdims=True) for p, d in zip(probs, dps)]
        )
        dss = [(p * (d - delta)).astype(bf16) for p, d in zip(probs, dps)]
        dq = functools.reduce(jnp.add, [dot(d, k) for d, (_, k, _, _) in zip(dss, parts)]) * scale
        c, s = cos_ref[here, :], sin_ref[here, :]
        grad_ref[here, :LANES] = rotated_back(dq[:, :LANES], c, s, kernel_roll).astype(bf16)
        grad_ref[here, LANES:HEAD_DIM] = dq[:, LANES:].astype(bf16)
        for p, d, (_, k, _, base) in zip(lows, dss, parts):
            there = slice(base, base + k.shape[0])
            dv_acc[there, :] += dot(p, up, TN)
            dk_acc[there, :] += dot(d, q, TN)

    chunk(0, own, 0, 0)
    step = 2 * LONGEST
    for at in range(0, tail, step):
        size = min(step, tail - at)
        chunk(own + at, size, max(0, at - LONGEST), at + size)

    for r in range(blocks):
        ref, there = (keep_ref, send_ref)[r % 2], slice(r * own, (r + 1) * own)
        ref[r // 2, 0] = (dk_acc[there, :] * scale).astype(bf16)
        ref[r // 2, 1] = dv_acc[there, :].astype(bf16)
    dk = dk_acc[shared:, :] * scale
    c, s = cos_ref[own:, :], sin_ref[own:, :]
    grad_ref[:own, HEAD_DIM:] = jnp.zeros((own, 2 * HEAD_DIM), bf16)
    grad_ref[own:, HEAD_DIM : HEAD_DIM + LANES] = rotated_back(
        dk[:, :LANES], c, s, kernel_roll
    ).astype(bf16)
    grad_ref[own:, HEAD_DIM + LANES : 2 * HEAD_DIM] = dk[:, LANES:].astype(bf16)
    grad_ref[own:, 2 * HEAD_DIM :] = dv_acc[shared:, :].astype(bf16)


def attention(chain, me, q, k, v, prompts, grad_context, first, cosine, signed):
    micro, heads, rows, _ = q.shape
    blocks = len(prompts)
    pieces = [piece for slot in prompts for piece in slot]
    own = pieces[0].shape[3]
    layout, at = [], 0
    for slot in prompts:
        layout.append(tuple(range(at, at + len(slot))))
        at += len(slot)
    shared, tail = blocks * own, rows - own
    head = pl.BlockSpec((None, None, rows, HEAD_DIM), lambda m, h, _: (m, h, 0, 0))
    prompt = [pl.BlockSpec((p.shape[0], None, None, own, HEAD_DIM), lambda m, h, _: (0, m, h, 0, 0)) for p in pieces]
    half = pl.BlockSpec((blocks // 2, 2, None, None, own, HEAD_DIM), lambda m, h, _: (0, 0, m, h, 0, 0))
    flat = pl.BlockSpec((rows, HEAD_DIM), lambda m, h, _: (m, h))
    table = pl.BlockSpec((None, rows, LANES), lambda m, h, _: (m, 0, 0))
    return chain.run(
        functools.partial(attention_kernel, layout),
        (me, q, k, v, grad_context, first, cosine, signed, *pieces),
        scalars=1,
        grid=(micro, heads),
        ins=[head, head, head, flat, pl.BlockSpec((None, tail, 1), lambda m, h, _: (m, 0, 0)), table, table] + prompt,
        outs=[flat, pl.BlockSpec((None, rows, 3 * HEAD_DIM), lambda m, h, _: (m, 0, h)), half, half],
        shapes=[array((micro * rows, heads * HEAD_DIM)), array((micro, rows, heads * 3 * HEAD_DIM))]
        + [array((blocks // 2, 2, micro, heads, own, HEAD_DIM))] * 2,
        scratch=[pltpu.VMEM((shared + tail, HEAD_DIM), f32)] * 2,
        name="attention",
    )


def fold_kernel(a_ref, b_ref, keep_ref, send_ref):
    for i, ref in enumerate((keep_ref, send_ref)):
        ref[0] = (a_ref[i].astype(f32) + b_ref[i].astype(f32)).astype(bf16)


def fold(chain, kept, got):
    slots, shape = kept.shape[0], kept.shape[1:]
    count = kept.size // (slots * HEAD_DIM)
    one = pl.BlockSpec((1, count, HEAD_DIM), lambda i: (i, 0, 0))
    two = pl.BlockSpec((2, count, HEAD_DIM), lambda i: (i, 0, 0))
    keep, send = chain.run(
        fold_kernel,
        (kept.reshape(slots, count, HEAD_DIM), got.reshape(slots, count, HEAD_DIM)),
        grid=(slots // 2,),
        ins=[two, two],
        outs=[one, one],
        shapes=[array((slots // 2, count, HEAD_DIM))] * 2,
        name="fold",
    )
    return keep.reshape((slots // 2,) + shape), send.reshape((slots // 2,) + shape)


def slot_of(j, me, part, low, size):
    return pl.ds(pl.multiple_of(lax.bitwise_xor(jnp.int32(j), me) * part + low, LANES), size)


def context_kernel(g_ref, w_ref, o_ref):
    o_ref[...] = dot(g_ref[...], w_ref[...]).astype(bf16)


def grad_context_of(chain, g, packed, wide):
    count, width = g.shape
    tile = count // 4
    at = packed.shape[1] // wide - 1
    return chain.run(
        context_kernel,
        (g, packed),
        grid=(count // tile,),
        ins=[pl.BlockSpec((tile, width), lambda i: (i, 0)), pl.BlockSpec((width, wide), lambda i: (0, at))],
        outs=[pl.BlockSpec((tile, wide), lambda i: (i, 0))],
        shapes=[array((count, wide))],
        name="grad_context",
    )[0]


def forward_kernel(spots, part, me_ref, n_ref, bias_ref, *refs):
    ups, (act_ref, slope_ref, up_ref) = refs[: len(spots)], refs[len(spots) :]
    me = me_ref[0]

    @pl.when(pl.program_id(1) == 0)
    def _():
        for (r, low), ref in zip(spots, ups):
            up_ref[slot_of(r, me, part, low, ref.shape[0]), :] = ref[...]

    h = dot(n_ref[...], up_ref[...]) + bias_ref[...]
    z = jnp.abs(h)
    e = jnp.exp(-0.5 * (h * h))
    t = 1.0 / (1.0 + TAIL_P * z)
    q = jnp.full_like(t, TAIL[0])
    for co in TAIL[1:]:
        q = q * t + co
    low = e * (t * q)
    cdf = jnp.where(h >= 0.0, 1.0 - low, low)
    act_ref[...] = (h * cdf).astype(bf16)
    slope_ref[...] = (cdf + h * (e * PEAK)).astype(bf16)


def spots_of(slots):
    spots, pieces = [], []
    for r, slot in enumerate(slots):
        low = 0
        for piece in slot:
            spots.append((r, low))
            pieces.append(piece)
            low += piece.shape[0]
    return spots, pieces


def ff_forward(chain, me, norm_two, ups, bias, rows):
    count, width = norm_two.shape
    spots, pieces = spots_of(ups)
    part, hidden = ups[0][0].shape
    cols = min(512, hidden)
    out = pl.BlockSpec((rows, cols), lambda c, r, _: (r, c))
    return chain.run(
        functools.partial(forward_kernel, spots, part),
        (me, norm_two, bias, *pieces),
        scalars=1,
        grid=(hidden // cols, count // rows),
        ins=[
            pl.BlockSpec((rows, width), lambda c, r, _: (r, 0)),
            pl.BlockSpec((1, cols), lambda c, r, _: (0, c)),
        ]
        + [pl.BlockSpec((p.shape[0], cols), lambda c, r, _: (0, c)) for p in pieces],
        outs=[out, out],
        shapes=[array((count, hidden))] * 2,
        scratch=[pltpu.VMEM((width, cols), bf16)],
        name="ff_forward",
    )


def backward_kernel(g_ref, down_ref, slope_ref, grad_ref, rows_ref):
    blocks, _, part = down_ref.shape

    @pl.when(pl.program_id(1) == 0)
    def _():
        for j in range(blocks):
            rows_ref[:, j * part : (j + 1) * part] = down_ref[j]

    ga = dot(g_ref[...], rows_ref[...], NT)
    grad_ref[...] = (ga * slope_ref[...].astype(f32)).astype(bf16)


def ff_backward(chain, g, down, slope, rows):
    count, width = g.shape
    blocks, hidden, part = down.shape
    cols = min(1024, hidden)
    out = pl.BlockSpec((rows, cols), lambda c, r: (r, c))
    return chain.run(
        backward_kernel,
        (g, down, slope),
        grid=(hidden // cols, count // rows),
        ins=[
            pl.BlockSpec((rows, width), lambda c, r: (r, 0)),
            pl.BlockSpec((blocks, cols, part), lambda c, r: (0, c, 0)),
            out,
        ],
        outs=[out],
        shapes=[array((count, hidden))],
        scratch=[pltpu.VMEM((cols, width), bf16)],
        name="ff_backward",
    )[0]


def mix_kernel(act_ref, ctx_ref, down_ref, dense_ref, *o_refs):
    total = dot(act_ref[...], down_ref[...])
    total += dot(ctx_ref[...], dense_ref[...], NT)
    size = total.shape[0] // len(o_refs)
    for i, ref in enumerate(o_refs):
        ref[...] = total[i * size : (i + 1) * size].astype(bf16)


def mix(chain, act, context, down, packed, rows, index, pieces):
    hidden = act.shape[1]
    wide = context.shape[1]
    blocks, _, part = down.shape
    size = rows // pieces
    at = packed.shape[1] // wide - 1
    return chain.run(
        mix_kernel,
        (act, context, down, packed),
        grid=(blocks,),
        ins=[
            pl.BlockSpec((rows, hidden), lambda j: (index, 0)),
            pl.BlockSpec((rows, wide), lambda j: (index, 0)),
            pl.BlockSpec((None, hidden, part), lambda j: (j, 0, 0)),
            pl.BlockSpec((part, wide), lambda j: (j, at)),
        ],
        outs=[pl.BlockSpec((size, part), lambda j: (0, j))] * pieces,
        shapes=[array((size, blocks * part))] * pieces,
        name="mix",
        key="mix%d" % min(index, 1),
    )


def second_grad_kernel(act_ref, ctx_ref, g_ref, o_ref):
    hidden = act_ref.shape[1]
    o_ref[:hidden, :] = dot(act_ref[...], g_ref[...], TN).astype(bf16)
    o_ref[hidden:, :] = dot(ctx_ref[...], g_ref[...], TN).astype(bf16)


def second_grads(chain, act, context, g, blocks):
    count, hidden = act.shape
    wide = context.shape[1]
    part = g.shape[1] // blocks
    return chain.run(
        second_grad_kernel,
        (act, context, g),
        grid=(blocks,),
        ins=[
            pl.BlockSpec((count, hidden), lambda j: (0, 0)),
            pl.BlockSpec((count, wide), lambda j: (0, 0)),
            pl.BlockSpec((count, part), lambda j: (0, j)),
        ],
        outs=[pl.BlockSpec((None, hidden + wide, part), lambda j: (j, 0, 0))],
        shapes=[array((blocks, hidden + wide, part))],
        name="second_grads",
    )[0]


def norm_grad_kernel(spots, me_ref, gj_ref, gh_ref, wj_ref, x_ref, mean_ref, inv_ref, g1_ref, g2_ref, *refs):
    ups, (*o_refs, stat_ref, two_ref) = refs[: len(spots)], refs[len(spots) :]
    slot = lax.bitwise_xor(pl.program_id(0), me_ref[0])
    for at in range(max(r for r, _ in spots) + 1):

        @pl.when(slot == at)
        def _():
            for (r, low), ref in zip(spots, ups):
                if r == at:
                    two_ref[:, low : low + ref.shape[0]] = dot(gh_ref[...], ref[...], NT)

    one, two = dot(gj_ref[...], wj_ref[...], NT), two_ref[...]
    normed = (x_ref[...].astype(f32) - mean_ref[...]) * inv_ref[...]
    total = one * g1_ref[...] + two * g2_ref[...]
    size = total.shape[0] // len(o_refs)
    for i, ref in enumerate(o_refs):
        ref[...] = total[i * size : (i + 1) * size].astype(bf16)
    for i, term in enumerate((one * normed, one, two * normed, two)):
        stat_ref[i : i + 1, :] = jnp.sum(term, axis=0, keepdims=True)


def norm_grads(chain, me, grad_joined, grad_hidden, packed, ups, x, mean, inverse, gain_one, gain_two, rows, index, pieces):
    width = x.shape[1]
    wide, hidden = grad_joined.shape[1], grad_hidden.shape[1]
    spots, parts = spots_of(ups)
    blocks, part = len(ups), ups[0][0].shape[0]
    size = rows // pieces
    column = pl.BlockSpec((rows, 1), lambda c, _: (index, 0))
    gain = pl.BlockSpec((1, part), lambda c, _: (0, c))
    return chain.run(
        functools.partial(norm_grad_kernel, spots),
        (me, grad_joined, grad_hidden, packed, x, mean, inverse, gain_one, gain_two, *parts),
        scalars=1,
        grid=(blocks,),
        ins=[
            pl.BlockSpec((rows, wide), lambda c, _: (index, 0)),
            pl.BlockSpec((rows, hidden), lambda c, _: (index, 0)),
            pl.BlockSpec((part, wide), lambda c, _: (c, 0)),
            pl.BlockSpec((rows, part), lambda c, _: (index, c)),
            column, column, gain, gain,
        ]
        + [pl.BlockSpec(p.shape, lambda c, _: (0, 0), pipeline_mode=pl.Buffered(1)) for p in parts],
        outs=[pl.BlockSpec((size, part), lambda c, _: (0, c))] * pieces + [pl.BlockSpec((8, part), lambda c, _: (0, c))],
        shapes=[array((size, width))] * pieces + [array((8, width), f32)],
        scratch=[pltpu.VMEM((rows, part), f32)],
        name="norm_grads",
        key="norm_grads%d" % min(index, 1),
    )


def prompt_kernel(keep_ref, got_ref, cos_ref, sin_ref, _, o_ref):
    total = keep_ref[...].astype(f32) + got_ref[...].astype(f32)

    @pl.when(pl.program_id(2) == 0)
    def _():
        first = rotated_back(total[:, :LANES], cos_ref[...], sin_ref[...], kernel_roll)
        o_ref[:, :LANES] = first.astype(bf16)
        o_ref[:, LANES:] = total[:, LANES:].astype(bf16)

    @pl.when(pl.program_id(2) == 1)
    def _():
        o_ref[...] = total.astype(bf16)


def put_prompt(chain, grad_joined, kept, got, cosine, signed):
    _, _, micro, heads, own, _ = kept.shape
    part = pl.BlockSpec((None, None, None, None, own, HEAD_DIM), lambda m, h, i: (0, i, m, h, 0, 0))
    table = pl.BlockSpec((None, own, LANES), lambda m, h, i: (m, 0, 0))
    return chain.run(
        prompt_kernel,
        (kept, got, cosine, signed, grad_joined),
        grid=(micro, heads, 2),
        ins=[part, part, table, table, ANY],
        outs=[pl.BlockSpec((None, own, HEAD_DIM), lambda m, h, i: (m, 0, 3 * h + 1 + i))],
        shapes=[array(grad_joined.shape)],
        aliases={4: 0},
        name="put_prompt",
    )[0]


def pair_kernel(a_ref, b_ref, o_ref):
    o_ref[...] = (a_ref[...].astype(f32) + b_ref[...].astype(f32)).astype(bf16)


def add_pair(chain, a, b):
    size, width = a.shape
    tile = size // 2
    row = pl.BlockSpec((tile, width), lambda i: (i, 0))
    return chain.run(
        pair_kernel,
        (a, b),
        grid=(size // tile,),
        ins=[row, row],
        outs=[row],
        shapes=[array((size, width))],
        name="add_pair",
    )[0]


def output_kernel(a_ref, b_ref, x_ref, dense_ref, down_ref, o_ref):
    total = a_ref[...].astype(f32) + b_ref[...].astype(f32)
    o_ref[...] = (x_ref[...].astype(f32) + total + dense_ref[...] + down_ref[...]).astype(bf16)


def input_kernel(a_ref, b_ref, x_ref, g_ref, mean_ref, inv_ref, o_ref):
    total = a_ref[...].astype(f32) + b_ref[...].astype(f32)
    inverse = inv_ref[...]
    normed = (x_ref[...].astype(f32) - mean_ref[...]) * inverse
    centred = (
        total
        - jnp.mean(total, axis=-1, keepdims=True)
        - normed * jnp.mean(total * normed, axis=-1, keepdims=True)
    )
    o_ref[...] = (g_ref[...].astype(f32) + inverse * centred).astype(bf16)


def finish(chain, a, b, start, rows, columns=(), vectors=()):
    size, width = a.shape
    tile = size // 2
    at = start // tile
    here = pl.BlockSpec((tile, width), lambda i: (i, 0))
    there = pl.BlockSpec((tile, width), lambda i: (at + i, 0))
    column = pl.BlockSpec((tile, 1), lambda i: (at + i, 0))
    vector = pl.BlockSpec((1, width), lambda i: (0, 0))
    return chain.run(
        input_kernel if columns else output_kernel,
        (a, b, *rows, *columns, *vectors),
        grid=(size // tile,),
        ins=[here, here] + [there] * len(rows) + [column] * len(columns) + [vector] * len(vectors),
        outs=[here],
        shapes=[array((size, width))],
        name="finish",
    )[0]


def swap(value, axis, bit):
    size = lax.axis_size(axis)
    return lax.ppermute(value, axis, [(i, i ^ (1 << bit)) for i in range(size)])


def bits_of(axis):
    return lax.axis_size(axis).bit_length() - 1


def send_xor(value, axis, offset):
    size = lax.axis_size(axis)
    return lax.ppermute(value, axis, [(i, i ^ offset) for i in range(size)])


def join(*values):
    return lax.optimization_barrier(values)


class Gather:
    def __init__(self, value, axis):
        self.axis, self.size = axis, lax.axis_size(axis)
        self.direct = self.size != 8
        offsets = range(2, self.size, 2) if self.direct else (2, 4)
        self.slots = [None] * self.size
        self.slots[0] = [value]
        self.slots[1] = [send_xor(value, axis, 1)]
        for r in offsets:
            self.slots[r] = [send_xor(value, axis, r)]

    def first(self, *others):
        here = [r for r in range(self.size) if r and self.slots[r]]
        values = join(*[self.slots[r][0] for r in here], *others)
        for r, value in zip(here, values):
            self.slots[r] = [value]
        self.fresh = []
        if not self.direct:
            near, far = self.slots[2][0], self.slots[4][0]
            half = near.shape[0] // 2
            self.fresh = [send_xor(near[:half], self.axis, 4), send_xor(far[half:], self.axis, 2)]
        self.twins = [r for r in here if r > 1]
        self.fresh += [send_xor(self.slots[r][0], self.axis, 1) for r in self.twins]
        return values[len(here) :]

    def second(self, *others):
        values = join(*self.fresh, *others)
        if not self.direct:
            self.slots[6] = list(values[:2])
            self.slots[7] = [send_xor(piece, self.axis, 1) for piece in self.slots[6]]
        for r, value in zip(self.twins, values[len(self.fresh) - len(self.twins) :]):
            self.slots[r + 1] = [value]
        return values[len(self.fresh) :]


def gather_ordered(value, axis):
    index = lax.axis_index(axis)
    held = value[None]
    for bit in range(bits_of(axis)):
        other = swap(held, axis, bit)
        low = ((index >> bit) & 1) == 0
        held = jnp.concatenate([jnp.where(low, held, other), jnp.where(low, other, held)], 0)
    return held


def scatter_ordered(value, axis):
    index = lax.axis_index(axis)
    held = value
    for bit in reversed(range(bits_of(axis))):
        low = ((index >> bit) & 1) == 0
        half = held.shape[0] // 2
        first, last = held[:half], held[half:]
        held = jnp.where(low, first, last) + swap(jnp.where(low, last, first), axis, bit)
    return held[0]


def add_up(value, axis):
    for bit in range(bits_of(axis)):
        value = value + swap(value, axis, bit)
    return value


def own_rows(value, start, count):
    return lax.dynamic_slice_in_dim(value, start, count, 0)


def sum_rows(partial, axis):
    index = lax.axis_index(axis)
    held, start = partial, jnp.int32(0)
    for bit in range(bits_of(axis)):
        mine = (index >> bit) & 1
        half = held.shape[0] // 2
        other = swap(own_rows(held, (1 - mine) * half, half).astype(bf16), axis, bit)
        held = own_rows(held, mine * half, half).astype(f32) + other.astype(f32)
        start = start + mine * half
    return held, start


def spread_rows(share, axis):
    index = lax.axis_index(axis)
    held = share
    for bit in reversed(range(bits_of(axis))):
        mine = (index >> bit) & 1
        other = swap(held, axis, bit)
        held = jnp.where(
            mine == 0, jnp.concatenate([held, other], 0), jnp.concatenate([other, held], 0)
        )
    return held


TO_MIDDLE = [(0, 1), (3, 2)]
ACROSS = [(1, 2), (2, 1)]
TO_ENDS = [(1, 0), (2, 3)]


class Piece:
    def __init__(self, chain, partial, axis, close, earlier=None):
        self.chain, self.axis, self.closing = chain, axis, close
        if earlier is not None:
            partial, earlier.pair = join(partial, earlier.pair)
        self.partial = partial
        self.first = lax.ppermute(partial, axis, TO_MIDDLE)

    def cross(self):
        self.pair = add_pair(self.chain, self.partial, self.first)
        self.second = lax.ppermute(self.pair, self.axis, ACROSS)

    def close(self, earlier=None):
        if earlier is not None:
            earlier.third, self.pair = join(earlier.third, self.pair)
        self.own = self.closing(self.pair, self.second)
        self.third = lax.ppermute(self.own, self.axis, TO_ENDS)


def local(
    tokens,
    cont_lengths,
    first_gain,
    first_bias,
    second_gain,
    second_bias,
    joined_weight,
    joined_bias,
    dense_weight,
    dense_bias,
    up_weight,
    up_bias,
    down_weight,
    down_bias,
    cotangent,
):
    blocks, ranks = lax.axis_size("dp"), lax.axis_size("tensor")
    me = lax.axis_index("dp").astype(jnp.int32)
    micro, _, rows, width = tokens.shape
    count = micro * rows
    own = PROMPT // blocks
    tail = rows - own
    part = width // blocks
    heads = joined_weight.shape[1] // (3 * HEAD_DIM)
    wide = heads * HEAD_DIM
    hidden = up_weight.shape[1]
    x = tokens.reshape(count, width)
    g = cotangent.reshape(count, width)
    here = me.reshape(1)

    chain = Chain()
    packed, first_gain = join(pack(chain, joined_weight, dense_weight), first_gain)
    packed = lax.all_gather(packed, "dp", axis=0, tiled=True)
    down = lax.all_gather(down_weight, "dp", axis=0, tiled=False)

    vectors = (first_gain, first_bias, second_gain, second_bias, dense_bias, down_bias)
    small = jnp.concatenate([v.reshape(-1) for v in vectors + (joined_bias, up_bias)])
    small = gather_ordered(small, "dp")
    up_here, small = join(up_weight, small)
    ups = Gather(up_here, "dp")

    small = small.astype(f32)
    full = [small[:, i * part : (i + 1) * part].reshape(1, width) for i in range(6)]
    gain_one, bias_one, gain_two, bias_two, dense_add, down_add = full

    def by_head(start, like):
        piece = small[:, start : start + like.size].reshape((blocks,) + like.shape)
        return jnp.transpose(piece, (1, 0, 2)).reshape(1, -1)

    joined_add = by_head(6 * part, joined_bias)
    up_add = by_head(6 * part + joined_bias.size, up_bias)

    seg_ends = jnp.cumsum(cont_lengths[:, 0], axis=1)
    slots = jnp.arange(tail, dtype=jnp.int32)
    passed = (slots[None, :, None] >= seg_ends[:, None, :]).astype(jnp.int32)
    first = jnp.sum(passed * cont_lengths[:, 0][:, None, :], axis=2)
    prompt_pos = jnp.broadcast_to(me * own + jnp.arange(own, dtype=jnp.int32), (micro, own))
    positions = jnp.concatenate([prompt_pos, PROMPT + slots[None] - first], axis=1)
    cosine, signed = rope_tables(positions)

    norm_one, norm_two, mean, inverse, upstream_sum = norms(chain, x, g, gain_one, bias_one, gain_two, bias_two)
    norm_one, cosine, signed, packed = ups.first(norm_one, cosine, signed, packed)

    q, k, v, prompt = qkv(chain, norm_one.reshape(micro, rows, width), packed, joined_add, cosine, signed, own)
    (prompt,) = ups.second(prompt)
    prompts = Gather(prompt, "dp")
    act, slope = ff_forward(chain, here, norm_two, ups.slots, up_add, rows)
    (slope,) = prompts.first(slope)
    grad_context = grad_context_of(chain, g, packed, wide)
    (grad_context,) = prompts.second(grad_context)
    prompts, ups = prompts.slots, ups.slots

    line = ranks == 4
    pieces = 2
    size = rows // pieces
    outs, turned = [], []
    context, grad_joined, kept, sent = attention(
        chain, here, q, k, v, prompts, grad_context, first[..., None], cosine, signed
    )
    got = send_xor(sent, "dp", 1)

    def close_output(start):
        return lambda a, b: finish(chain, a, b, start, (x,), vectors=(dense_add, down_add))

    def close_input(start):
        return lambda a, b: finish(chain, a, b, start, (x, g), columns=(mean, inverse))

    def split(parts, m, close, into, before):
        for i, partial in enumerate(parts):
            if line:
                crossed = [p for p in (before + into)[:-1] if hasattr(p, "pair")]
                earlier = crossed[-1] if crossed else None
                partial = Piece(chain, partial, "tensor", close(m * rows + i * size), earlier)
            into.append(partial)

    def sync(k):
        if line:
            every = outs + turned
            if k < len(every) and not CLOSE_FIRST:
                every[k].cross()
            if 0 < k:
                every[k - 1].close(every[k - 2] if k > 1 else None)
            if k < len(every) and CLOSE_FIRST:
                every[k].cross()

    parts = mix(chain, act, context, down, packed, rows, 0, pieces)
    split(parts, 0, close_output, outs, [])
    later = [mix(chain, act, context, down, packed, rows, m, pieces) for m in range(1, micro)]
    def second_part():
        second_grad = second_grads(chain, act, context, g, blocks)
        return lax.psum_scatter(second_grad, "dp", scatter_dimension=0, tiled=False)

    if SECOND_AT == 0:
        second_out = second_part()
    sync(0)
    if SECOND_AT == 1:
        second_out = second_part()
    for m, parts in enumerate(later, 1):
        split(parts, m, close_output, outs, [])
    kept, sent = fold(chain, kept, got)
    got = send_xor(sent, "dp", 2)
    if SECOND_AT == 3:
        second_out = second_part()
    grad_hidden = ff_backward(chain, g, down, slope, rows)
    sync(1)
    if SECOND_AT == 2:
        second_out = second_part()
    for bit in range(2, bits_of("dp")):
        kept, sent = fold(chain, kept, got)
        got = send_xor(sent, "dp", 1 << bit)
    if line:
        rank = lax.axis_index("tensor")
        end = ((rank == 0) | (rank == 3)).astype(jnp.int32).reshape(1)
        output = None

    def put_output(i):
        return place(chain, output, end, outs[i : i + 2], i * size, count)

    sync(2)
    grad_joined = put_prompt(chain, grad_joined, kept, got, cosine, signed).reshape(count, 3 * wide)
    stats = []
    for m in range(micro):
        *parts, stat = norm_grads(
            chain, here, grad_joined, grad_hidden, packed, ups, x, mean, inverse, gain_one, gain_two, rows, m, pieces
        )
        stats.append(stat[:4])
        if m == 0:
            split(parts, m, close_input, turned, outs)
            sync(3)
            if line:
                output = put_output(0)
    gains = functools.reduce(jnp.add, stats)
    split(parts, micro - 1, close_input, turned, outs)
    sync(4)
    up_grad, up_add_grad = outer(chain, norm_two, grad_hidden, "outer0")
    up_out = lax.psum_scatter(up_grad, "dp", scatter_dimension=0, tiled=True)
    if line:
        turned[0].pair, second_out = join(turned[0].pair, second_out)
    sync(5)
    if line:
        output = put_output(2)
    joined_grad, joined_add_grad = outer(chain, norm_one, grad_joined, "outer1")
    joined_out = lax.psum_scatter(joined_grad, "dp", scatter_dimension=0, tiled=True)

    if line:
        sync(6)
        turned[2].pair, up_out = join(turned[2].pair, up_out)
        sync(7)
        turned[3].pair, joined_add_grad = join(turned[3].pair, joined_add_grad)

    def to_blocks(value, lead):
        value = value.reshape(lead, blocks, -1)
        return jnp.transpose(value, (1, 0, 2)).reshape(blocks, -1)

    vector = [
        to_blocks(gains, 4),
        to_blocks(upstream_sum, 1),
        to_blocks(joined_add_grad, joined_bias.shape[0]),
        to_blocks(up_add_grad, up_bias.shape[0]),
    ]
    vector = scatter_ordered(jnp.concatenate(vector, 1), "dp")
    base = 5 * part
    gains = vector[: 4 * part]

    if line:
        other = swap(gains, "tensor", 0)
        input_grad = place(chain, None, end, turned[:2], 0, count)
        turned[3].pair, other = join(turned[3].pair, other)
        gains = gains + other
        sync(8)
        gains = gains + swap(gains, "tensor", 1)
        input_grad = place(chain, input_grad, end, turned[2:], 2 * size, count)
        output = output.reshape(micro, rows, width)
        input_grad = input_grad.reshape(micro, rows, width)
    else:
        gains = add_up(gains, "tensor")
        outputs, inputs = [], []
        for m in range(micro):
            share, start = sum_rows(jnp.concatenate(outs[m * pieces : (m + 1) * pieces]), "tensor")
            span = share.shape[0]
            mine = own_rows(x, m * rows + start, span).astype(f32)
            outputs.append(spread_rows((mine + share + dense_add + down_add).astype(bf16), "tensor"))
            share, start = sum_rows(jnp.concatenate(turned[m * pieces : (m + 1) * pieces]), "tensor")
            start = m * rows + start
            row_inverse = own_rows(inverse, start, span)
            row_normed = (own_rows(x, start, span).astype(f32) - own_rows(mean, start, span)) * row_inverse
            centred = (
                share
                - jnp.mean(share, axis=-1, keepdims=True)
                - row_normed * jnp.mean(share * row_normed, axis=-1, keepdims=True)
            )
            result = own_rows(g, start, span).astype(f32) + row_inverse * centred
            inputs.append(spread_rows(result.astype(bf16), "tensor"))
        output, input_grad = jnp.stack(outputs), jnp.stack(inputs)

    return (
        output[:, None],
        input_grad[:, None],
        gains[:part],
        gains[part : 2 * part],
        gains[2 * part : 3 * part],
        gains[3 * part :],
        joined_out.astype(f32),
        vector[base : base + joined_bias.size].reshape(joined_bias.shape),
        second_out[hidden:].astype(f32),
        vector[4 * part : base],
        up_out.astype(f32),
        vector[base + joined_bias.size :].reshape(up_bias.shape),
        second_out[:hidden].astype(f32),
        vector[4 * part : base],
    )


def solution(mesh):
    placed = (
        P(None, "dp", None, None),
        P(None, "dp", None),
        P("dp"),
        P("dp"),
        P("dp"),
        P("dp"),
        P("dp", "tensor"),
        P("tensor", "dp"),
        P("tensor", "dp"),
        P("dp"),
        P("dp", "tensor"),
        P("tensor", "dp"),
        P("tensor", "dp"),
        P("dp"),
        P(None, "dp", None, None),
    )
    return jax.shard_map(
        local,
        mesh=mesh,
        in_specs=placed,
        out_specs=(
            P(None, "dp", None, None),
            P(None, "dp", None, None),
            P("dp"),
            P("dp"),
            P("dp"),
            P("dp"),
            P("dp", "tensor"),
            P("tensor", "dp"),
            P("tensor", "dp"),
            P("dp"),
            P("dp", "tensor"),
            P("tensor", "dp"),
            P("tensor", "dp"),
            P("dp"),
        ),
        check_vma=False,
    )
```

```python
import functools

import jax
import jax.numpy as jnp
from jax import lax
from jax.experimental import pallas as pl
from jax.experimental.pallas import tpu as pltpu
from jax.sharding import PartitionSpec as P

HEAD_DIM = 256
ROT_DIMS = 64
PROMPT = 1024
LONGEST = 128

norm_eps = 1e-05
rope_base = 10000.0
masked_score = -1e30
scale = HEAD_DIM**-0.5
LANES = 128
VMEM = 60 << 20

f32, bf16 = jnp.float32, jnp.bfloat16
NN = (((1,), (0,)), ((), ()))
NT = (((1,), (1,)), ((), ()))
TN = (((0,), (0,)), ((), ()))

TAIL_P = 0.32
TAIL = (
    -0.02115197293220867,
    0.09575628590143809,
    -0.14740109756488956,
    0.06607995422323057,
    -0.0098602948578973,
    0.058840354546090344,
    0.08778712629904878,
    0.11462742044446793,
    0.12766067496581068,
    0.12766153278717104,
)
PEAK = 0.3989422804014327


def dot(a, b, dims=NN):
    return lax.dot_general(a, b, dims, preferred_element_type=f32)


TIMES = {
    "pack": 2.3,
    "norms": 12.4,
    "qkv": 14.0,
    "grad_context": 7.0,
    "ff_forward": 28.0,
    "attention": 25.0,
    "mix0": 13.0,
    "mix1": 13.0,
    "second_grads": 20.0,
    "fold": 3.5,
    "add_pair": 3.0,
    "finish": 4.0,
    "ff_backward": 18.5,
    "put_prompt": 5.4,
    "norm_grads0": 21.0,
    "norm_grads1": 21.0,
    "outer0": 17.0,
    "outer1": 13.0,
    "place": 4.5,
}
FLOPS = 1.15e9
SHARE = 2.0
BACK = 5
PLAN = (('mix', 0), ('go', 0, 0), ('go', 0, 1), ('mix', 1), ('fold',), ('ffb',), ('cross', 0), ('go', 1, 0, 0), ('up',), ('cross', 1), ('go', 1, 1, 1), ('send', 'up', 1), ('fold',), ('close', 0), ('second',), ('cross', 2), ('send', 'second', 2), ('close', 1), ('prompt',), ('norm', 0), ('go', 2, 0, 2), ('cross', 3), ('go', 2, 1, 3), ('close', 2), ('place', 0, 2), ('norm', 1), ('go', 3, 0, 3), ('cross', 4), ('go', 3, 1, 4), ('close', 3), ('joined',), ('cross', 5), ('send', 'joined_grad', 5), ('close', 4), ('place', 2, 4), ('cross', 6), ('close', 5), ('cross', 7), ('close', 6), ('place', 4, 6), ('tie', 'up', 7), ('tie', 'second', 7), ('close', 7), ('place', 6, 8))
MERGED = ()


def cost(name):
    return pl.CostEstimate(flops=int(TIMES[name] * FLOPS * SHARE), bytes_accessed=0, transcendentals=0)


ANY = pl.BlockSpec(memory_space=pl.ANY)


class Chain:
    def __init__(self):
        self.last = ()

    def run(self, kernel, args, *, grid, ins, outs, shapes, name, key=None, scalars=0, scratch=(), aliases=None):
        count, extra = len(args), tuple(e for e in self.last if all(e is not a for a in args))

        def body(*refs):
            kernel(*refs[:count], *refs[count + len(extra) :])

        results = pl.pallas_call(
            body,
            grid_spec=pltpu.PrefetchScalarGridSpec(
                num_scalar_prefetch=scalars,
                grid=grid,
                in_specs=list(ins) + [ANY] * len(extra),
                out_specs=outs,
                scratch_shapes=list(scratch),
            ),
            out_shape=shapes,
            input_output_aliases=aliases or {},
            compiler_params=pltpu.CompilerParams(vmem_limit_bytes=VMEM),
            cost_estimate=cost(key or name),
            name=name,
        )(*args, *extra)
        self.last = (results[0],)
        return results


def array(shape, dtype=bf16):
    return jax.ShapeDtypeStruct(tuple(shape), dtype)


def rope_tables(positions):
    half = ROT_DIMS // 2
    inverse = rope_base ** (-(2.0 * jnp.arange(half, dtype=f32)) / ROT_DIMS)
    angles = positions.astype(f32)[..., None] * inverse
    ones = jnp.ones(positions.shape + (LANES - ROT_DIMS,), f32)
    c, s = jnp.cos(angles), jnp.sin(angles)
    return jnp.concatenate([c, c, ones], -1), jnp.concatenate([-s, s, ones * 0.0], -1)


def swap_halves(u, roll):
    half = ROT_DIMS // 2
    lane = lax.broadcasted_iota(jnp.int32, u.shape, u.ndim - 1)
    up, down = roll(u, LANES - half), roll(u, half)
    return jnp.where(lane < half, up, jnp.where(lane < ROT_DIMS, down, 0.0))


def rotated(u, cosine, signed, roll):
    return u * cosine + swap_halves(u, roll) * signed


def rotated_back(y, cosine, signed, roll):
    return y * cosine + swap_halves(y * signed, roll)


def kernel_roll(u, by):
    return pltpu.roll(u, by, u.ndim - 1)


def plain_roll(u, by):
    return jnp.roll(u, by, -1)


def norm_kernel(x_ref, g_ref, g1_ref, b1_ref, g2_ref, b2_ref, n1_ref, n2_ref, mean_ref, inv_ref, sum_ref):
    x = x_ref[...].astype(f32)
    mean = jnp.mean(x, axis=-1, keepdims=True)
    centered = x - mean
    inverse = lax.rsqrt(jnp.mean(centered * centered, axis=-1, keepdims=True) + norm_eps)
    normed = centered * inverse
    n1_ref[...] = (normed * g1_ref[...] + b1_ref[...]).astype(bf16)
    n2_ref[...] = (normed * g2_ref[...] + b2_ref[...]).astype(bf16)
    mean_ref[...] = mean
    inv_ref[...] = inverse

    @pl.when(pl.program_id(0) == 0)
    def _():
        sum_ref[...] = jnp.zeros_like(sum_ref)

    sum_ref[...] += jnp.sum(g_ref[...].astype(f32), axis=0, keepdims=True)


def norms(chain, x, g, gain_one, bias_one, gain_two, bias_two):
    count, width = x.shape
    tile = count // 8
    row = pl.BlockSpec((tile, width), lambda i: (i, 0))
    vector = pl.BlockSpec((1, width), lambda i: (0, 0))
    column = pl.BlockSpec((tile, 1), lambda i: (i, 0))
    return chain.run(
        norm_kernel,
        (x, g, gain_one, bias_one, gain_two, bias_two),
        grid=(count // tile,),
        ins=[row, row] + [vector] * 4,
        outs=[row, row, column, column, vector],
        shapes=[array((count, width))] * 2 + [array((count, 1), f32)] * 2 + [array((1, width), f32)],
        name="norms",
    )


def outer_kernel(a_ref, b_ref, o_ref, sum_ref):
    o_ref[...] = dot(a_ref[...], b_ref[...], TN).astype(bf16)

    @pl.when(pl.program_id(0) == 0)
    def _():
        sum_ref[...] = jnp.sum(b_ref[...].astype(f32), axis=0, keepdims=True)


def outer(chain, a, b, key):
    count, width = a.shape
    cols = b.shape[1]
    tile = width // 4
    return chain.run(
        outer_kernel,
        (a, b),
        grid=(4,),
        ins=[pl.BlockSpec((count, tile), lambda i: (0, i)), pl.BlockSpec((count, cols), lambda i: (0, 0))],
        outs=[pl.BlockSpec((tile, cols), lambda i: (i, 0)), pl.BlockSpec((1, cols), lambda i: (0, 0))],
        shapes=[array((width, cols)), array((1, cols), f32)],
        name="outer",
        key=key,
    )


def outer_more_kernel(a_ref, b_ref, more_ref, o_ref):
    cols = b_ref.shape[1]
    o_ref[:, :cols] = dot(a_ref[...], b_ref[...], TN).astype(bf16)
    o_ref[:, cols:] = jnp.zeros((o_ref.shape[0], LANES), bf16)
    o_ref[:, cols : cols + more_ref.shape[0]] = more_ref[...].T.astype(bf16)


def outer_more(chain, a, b, more, key):
    count, width = a.shape
    cols = b.shape[1]
    tile = width // 4
    return chain.run(
        outer_more_kernel,
        (a, b, more),
        grid=(4,),
        ins=[
            pl.BlockSpec((count, tile), lambda i: (0, i)),
            pl.BlockSpec((count, cols), lambda i: (0, 0)),
            pl.BlockSpec((more.shape[0], tile), lambda i: (0, i)),
        ],
        outs=[pl.BlockSpec((tile, cols + LANES), lambda i: (i, 0))],
        shapes=[array((width, cols + LANES))],
        name="outer",
        key=key,
    )[0]


def place_kernel(flag_ref, *refs):
    o_ref = refs[-1]
    pieces = len(refs) // 2 if len(refs) % 2 else len(refs) // 2 - 1
    for i in range(pieces):
        for flag in (0, 1):

            @pl.when((flag_ref[0] == flag) & (pl.program_id(0) // 2 == i))
            def _():
                o_ref[...] = refs[2 * i + flag][...]


def place(chain, held, flag, pieces, start, total):
    size, width = pieces[0].own.shape
    tile = size // 2
    keep = () if held is None else (held,)
    ins, args = [], []
    for i, piece in enumerate(pieces):
        args += [piece.own, piece.third]
        ins += [
            pl.BlockSpec((tile, width), lambda j, flag, i=i: (jnp.clip(j - 2 * i, 0, 1) * (1 - flag[0]), 0)),
            pl.BlockSpec((tile, width), lambda j, flag, i=i: (jnp.clip(j - 2 * i, 0, 1) * flag[0], 0)),
        ]
    return chain.run(
        place_kernel,
        (flag, *args) + keep,
        scalars=1,
        grid=(2 * len(pieces),),
        ins=ins + [ANY] * len(keep),
        outs=[pl.BlockSpec((tile, width), lambda j, _: (start // tile + j, 0))],
        shapes=[array((total, width))],
        aliases={1 + len(args): 0} if keep else {},
        name="place",
    )[0]


def pack_kernel(joined_ref, dense_ref, o_ref):
    wide = joined_ref.shape[1]
    o_ref[:, :wide] = joined_ref[...]
    o_ref[:, wide:] = dense_ref[...].T


def pack(chain, joined, dense):
    part, wide = joined.shape
    total = wide + dense.shape[0]

    def whole(rows, columns):
        return pl.BlockSpec((rows, columns), lambda i: (0, 0))

    return chain.run(
        pack_kernel,
        (joined, dense),
        grid=(1,),
        ins=[whole(*joined.shape), whole(*dense.shape)],
        outs=[whole(part, total)],
        shapes=[array((part, total))],
        name="pack",
    )[0]


def qkv_kernel(x_ref, w_ref, bias_ref, cos_ref, sin_ref, q_ref, k_ref, v_ref, prompt_ref):
    joined = dot(x_ref[...], w_ref[...]) + bias_ref[...]
    c, s = cos_ref[...], sin_ref[...]
    for part, ref in ((0, q_ref), (1, k_ref)):
        base = part * HEAD_DIM
        head = joined[:, base : base + HEAD_DIM]
        ref[:, :LANES] = rotated(head[:, :LANES], c, s, kernel_roll).astype(bf16)
        ref[:, LANES:] = head[:, LANES:].astype(bf16)
    v_ref[...] = joined[:, 2 * HEAD_DIM :].astype(bf16)
    own = prompt_ref.shape[1]
    prompt_ref[0] = k_ref[:own, :]
    prompt_ref[1] = v_ref[:own, :]


def qkv(chain, norm_one, weight, bias, cosine, signed, own):
    micro, rows, width = norm_one.shape
    wide = 3 * HEAD_DIM
    heads = bias.shape[1] // wide
    head = pl.BlockSpec((None, None, rows, HEAD_DIM), lambda h, m: (m, h, 0, 0))
    table = pl.BlockSpec((None, rows, LANES), lambda h, m: (m, 0, 0))
    return chain.run(
        qkv_kernel,
        (norm_one, weight, bias, cosine, signed),
        grid=(heads, micro),
        ins=[
            pl.BlockSpec((None, rows, width), lambda h, m: (m, 0, 0)),
            pl.BlockSpec((width, wide), lambda h, m: (0, h)),
            pl.BlockSpec((1, wide), lambda h, m: (0, h)),
            table,
            table,
        ],
        outs=[head] * 3 + [pl.BlockSpec((2, None, None, own, HEAD_DIM), lambda h, m: (0, m, h, 0, 0))],
        shapes=[array((micro, heads, rows, HEAD_DIM))] * 3 + [array((2, micro, heads, own, HEAD_DIM))],
        name="qkv",
    )


def attention_kernel(layout, me_ref, q_ref, k_ref, v_ref, up_ref, first_ref, cos_ref, sin_ref, *refs):
    ctx_ref, grad_ref, keep_ref, send_ref, dk_acc, dv_acc = refs[-6:]
    blocks, own = len(layout), refs[0].shape[1]
    rows = q_ref.shape[0]
    tail = rows - own
    shared = blocks * own
    me = me_ref[0]
    pk = jnp.concatenate([refs[spots[0]][0] for spots in layout], 0)
    pv = jnp.concatenate([refs[spots[-1]][refs[spots[-1]].shape[0] - 1] for spots in layout], 0)
    ck, cv = k_ref[own:, :], v_ref[own:, :]
    dk_acc[...] = jnp.zeros_like(dk_acc)
    dv_acc[...] = jnp.zeros_like(dv_acc)

    def chunk(start, count, low, high):
        here = slice(start, start + count)
        q, up = q_ref[here, :], up_ref[here, :]
        sp = dot(q, pk, NT) * scale
        parts = []
        if high > low:
            wk, wv = ck[low:high], cv[low:high]
            sw = dot(q, wk, NT) * scale
            key = lax.broadcasted_iota(jnp.int32, sw.shape, 1) + low
            slot = lax.broadcasted_iota(jnp.int32, sw.shape, 0) + (start - own)
            first = first_ref[start - own : start - own + count, :]
            sw = jnp.where((key >= first) & (key <= slot), sw, masked_score)
            parts = [(sp, pk, pv, 0), (sw, wk, wv, shared + low)]
        else:
            spot = lax.broadcasted_iota(jnp.int32, sp.shape, 1)
            key = lax.bitwise_xor(spot // own, me) * own + spot % own
            slot = lax.broadcasted_iota(jnp.int32, sp.shape, 0) + (me * own + start)
            parts = [(jnp.where(key <= slot, sp, masked_score), pk, pv, 0)]
        highest = functools.reduce(jnp.maximum, [jnp.max(s, -1, keepdims=True) for s, *_ in parts])
        raised = [jnp.exp(s - highest) for s, *_ in parts]
        total = functools.reduce(jnp.add, [jnp.sum(r, -1, keepdims=True) for r in raised])
        inverse = 1.0 / total
        probs = [r * inverse for r in raised]
        lows = [p.astype(bf16) for p in probs]
        ctx = functools.reduce(jnp.add, [dot(p, v) for p, (_, _, v, _) in zip(lows, parts)])
        ctx_ref[here, :] = ctx.astype(bf16)
        dps = [dot(up, v, NT) for _, _, v, _ in parts]
        delta = functools.reduce(
            jnp.add, [jnp.sum(p * d, -1, keepdims=True) for p, d in zip(probs, dps)]
        )
        dss = [(p * (d - delta)).astype(bf16) for p, d in zip(probs, dps)]
        dq = functools.reduce(jnp.add, [dot(d, k) for d, (_, k, _, _) in zip(dss, parts)]) * scale
        c, s = cos_ref[here, :], sin_ref[here, :]
        grad_ref[here, :LANES] = rotated_back(dq[:, :LANES], c, s, kernel_roll).astype(bf16)
        grad_ref[here, LANES:HEAD_DIM] = dq[:, LANES:].astype(bf16)
        for p, d, (_, k, _, base) in zip(lows, dss, parts):
            there = slice(base, base + k.shape[0])
            dv_acc[there, :] += dot(p, up, TN)
            dk_acc[there, :] += dot(d, q, TN)

    chunk(0, own, 0, 0)
    step = 2 * LONGEST
    for at in range(0, tail, step):
        size = min(step, tail - at)
        chunk(own + at, size, max(0, at - LONGEST), at + size)

    for r in range(blocks):
        ref, there = (keep_ref, send_ref)[r % 2], slice(r * own, (r + 1) * own)
        ref[r // 2, 0] = (dk_acc[there, :] * scale).astype(bf16)
        ref[r // 2, 1] = dv_acc[there, :].astype(bf16)
    dk = dk_acc[shared:, :] * scale
    c, s = cos_ref[own:, :], sin_ref[own:, :]
    grad_ref[:own, HEAD_DIM:] = jnp.zeros((own, 2 * HEAD_DIM), bf16)
    grad_ref[own:, HEAD_DIM : HEAD_DIM + LANES] = rotated_back(
        dk[:, :LANES], c, s, kernel_roll
    ).astype(bf16)
    grad_ref[own:, HEAD_DIM + LANES : 2 * HEAD_DIM] = dk[:, LANES:].astype(bf16)
    grad_ref[own:, 2 * HEAD_DIM :] = dv_acc[shared:, :].astype(bf16)


def attention(chain, me, q, k, v, prompts, grad_context, first, cosine, signed):
    micro, heads, rows, _ = q.shape
    blocks = len(prompts)
    pieces = [piece for slot in prompts for piece in slot]
    own = pieces[0].shape[3]
    layout, at = [], 0
    for slot in prompts:
        layout.append(tuple(range(at, at + len(slot))))
        at += len(slot)
    shared, tail = blocks * own, rows - own
    head = pl.BlockSpec((None, None, rows, HEAD_DIM), lambda m, h, _: (m, h, 0, 0))
    prompt = [pl.BlockSpec((p.shape[0], None, None, own, HEAD_DIM), lambda m, h, _: (0, m, h, 0, 0)) for p in pieces]
    half = pl.BlockSpec((blocks // 2, 2, None, None, own, HEAD_DIM), lambda m, h, _: (0, 0, m, h, 0, 0))
    flat = pl.BlockSpec((rows, HEAD_DIM), lambda m, h, _: (m, h))
    table = pl.BlockSpec((None, rows, LANES), lambda m, h, _: (m, 0, 0))
    return chain.run(
        functools.partial(attention_kernel, layout),
        (me, q, k, v, grad_context, first, cosine, signed, *pieces),
        scalars=1,
        grid=(micro, heads),
        ins=[head, head, head, flat, pl.BlockSpec((None, tail, 1), lambda m, h, _: (m, 0, 0)), table, table] + prompt,
        outs=[flat, pl.BlockSpec((None, rows, 3 * HEAD_DIM), lambda m, h, _: (m, 0, h)), half, half],
        shapes=[array((micro * rows, heads * HEAD_DIM)), array((micro, rows, heads * 3 * HEAD_DIM))]
        + [array((blocks // 2, 2, micro, heads, own, HEAD_DIM))] * 2,
        scratch=[pltpu.VMEM((shared + tail, HEAD_DIM), f32)] * 2,
        name="attention",
    )


def fold_kernel(a_ref, b_ref, keep_ref, send_ref):
    for i, ref in enumerate((keep_ref, send_ref)):
        ref[0] = (a_ref[i].astype(f32) + b_ref[i].astype(f32)).astype(bf16)


def fold(chain, kept, got):
    slots, shape = kept.shape[0], kept.shape[1:]
    count = kept.size // (slots * HEAD_DIM)
    one = pl.BlockSpec((1, count, HEAD_DIM), lambda i: (i, 0, 0))
    two = pl.BlockSpec((2, count, HEAD_DIM), lambda i: (i, 0, 0))
    keep, send = chain.run(
        fold_kernel,
        (kept.reshape(slots, count, HEAD_DIM), got.reshape(slots, count, HEAD_DIM)),
        grid=(slots // 2,),
        ins=[two, two],
        outs=[one, one],
        shapes=[array((slots // 2, count, HEAD_DIM))] * 2,
        name="fold",
    )
    return keep.reshape((slots // 2,) + shape), send.reshape((slots // 2,) + shape)


def slot_of(j, me, part, low, size):
    return pl.ds(pl.multiple_of(lax.bitwise_xor(jnp.int32(j), me) * part + low, LANES), size)


def context_kernel(g_ref, w_ref, o_ref):
    o_ref[...] = dot(g_ref[...], w_ref[...]).astype(bf16)


def grad_context_of(chain, g, packed, wide):
    count, width = g.shape
    tile = count // 4
    at = packed.shape[1] // wide - 1
    return chain.run(
        context_kernel,
        (g, packed),
        grid=(count // tile,),
        ins=[pl.BlockSpec((tile, width), lambda i: (i, 0)), pl.BlockSpec((width, wide), lambda i: (0, at))],
        outs=[pl.BlockSpec((tile, wide), lambda i: (i, 0))],
        shapes=[array((count, wide))],
        name="grad_context",
    )[0]


def forward_kernel(spots, part, me_ref, n_ref, bias_ref, *refs):
    ups, (act_ref, slope_ref, up_ref) = refs[: len(spots)], refs[len(spots) :]
    me = me_ref[0]

    @pl.when(pl.program_id(1) == 0)
    def _():
        for (r, low), ref in zip(spots, ups):
            up_ref[slot_of(r, me, part, low, ref.shape[0]), :] = ref[...]

    h = dot(n_ref[...], up_ref[...]) + bias_ref[...]
    z = jnp.abs(h)
    e = jnp.exp(-0.5 * (h * h))
    t = 1.0 / (1.0 + TAIL_P * z)
    q = jnp.full_like(t, TAIL[0])
    for co in TAIL[1:]:
        q = q * t + co
    low = e * (t * q)
    cdf = jnp.where(h >= 0.0, 1.0 - low, low)
    act_ref[...] = (h * cdf).astype(bf16)
    slope_ref[...] = (cdf + h * (e * PEAK)).astype(bf16)


def spots_of(slots):
    spots, pieces = [], []
    for r, slot in enumerate(slots):
        low = 0
        for piece in slot:
            spots.append((r, low))
            pieces.append(piece)
            low += piece.shape[0]
    return spots, pieces


def ff_forward(chain, me, norm_two, ups, bias, rows):
    count, width = norm_two.shape
    spots, pieces = spots_of(ups)
    part, hidden = ups[0][0].shape
    cols = min(512, hidden)
    out = pl.BlockSpec((rows, cols), lambda c, r, _: (r, c))
    return chain.run(
        functools.partial(forward_kernel, spots, part),
        (me, norm_two, bias, *pieces),
        scalars=1,
        grid=(hidden // cols, count // rows),
        ins=[
            pl.BlockSpec((rows, width), lambda c, r, _: (r, 0)),
            pl.BlockSpec((1, cols), lambda c, r, _: (0, c)),
        ]
        + [pl.BlockSpec((p.shape[0], cols), lambda c, r, _: (0, c)) for p in pieces],
        outs=[out, out],
        shapes=[array((count, hidden))] * 2,
        scratch=[pltpu.VMEM((width, cols), bf16)],
        name="ff_forward",
    )


def backward_kernel(g_ref, down_ref, slope_ref, grad_ref, rows_ref):
    blocks, _, part = down_ref.shape

    @pl.when(pl.program_id(1) == 0)
    def _():
        for j in range(blocks):
            rows_ref[:, j * part : (j + 1) * part] = down_ref[j]

    ga = dot(g_ref[...], rows_ref[...], NT)
    grad_ref[...] = (ga * slope_ref[...].astype(f32)).astype(bf16)


def ff_backward(chain, g, down, slope, rows):
    count, width = g.shape
    blocks, hidden, part = down.shape
    cols = min(1024, hidden)
    out = pl.BlockSpec((rows, cols), lambda c, r: (r, c))
    return chain.run(
        backward_kernel,
        (g, down, slope),
        grid=(hidden // cols, count // rows),
        ins=[
            pl.BlockSpec((rows, width), lambda c, r: (r, 0)),
            pl.BlockSpec((blocks, cols, part), lambda c, r: (0, c, 0)),
            out,
        ],
        outs=[out],
        shapes=[array((count, hidden))],
        scratch=[pltpu.VMEM((cols, width), bf16)],
        name="ff_backward",
    )[0]


def mix_kernel(act_ref, ctx_ref, down_ref, dense_ref, *o_refs):
    total = dot(act_ref[...], down_ref[...])
    total += dot(ctx_ref[...], dense_ref[...], NT)
    size = total.shape[0] // len(o_refs)
    for i, ref in enumerate(o_refs):
        ref[...] = total[i * size : (i + 1) * size].astype(bf16)


def mix(chain, act, context, down, packed, rows, index, pieces):
    hidden = act.shape[1]
    wide = context.shape[1]
    blocks, _, part = down.shape
    size = rows // pieces
    at = packed.shape[1] // wide - 1
    return chain.run(
        mix_kernel,
        (act, context, down, packed),
        grid=(blocks,),
        ins=[
            pl.BlockSpec((rows, hidden), lambda j: (index, 0)),
            pl.BlockSpec((rows, wide), lambda j: (index, 0)),
            pl.BlockSpec((None, hidden, part), lambda j: (j, 0, 0)),
            pl.BlockSpec((part, wide), lambda j: (j, at)),
        ],
        outs=[pl.BlockSpec((size, part), lambda j: (0, j))] * pieces,
        shapes=[array((size, blocks * part))] * pieces,
        name="mix",
        key="mix%d" % min(index, 1),
    )


def second_grad_kernel(act_ref, ctx_ref, g_ref, o_ref):
    hidden = act_ref.shape[1]
    o_ref[:hidden, :] = dot(act_ref[...], g_ref[...], TN).astype(bf16)
    o_ref[hidden:, :] = dot(ctx_ref[...], g_ref[...], TN).astype(bf16)


def second_grads(chain, act, context, g, blocks):
    count, hidden = act.shape
    wide = context.shape[1]
    part = g.shape[1] // blocks
    return chain.run(
        second_grad_kernel,
        (act, context, g),
        grid=(blocks,),
        ins=[
            pl.BlockSpec((count, hidden), lambda j: (0, 0)),
            pl.BlockSpec((count, wide), lambda j: (0, 0)),
            pl.BlockSpec((count, part), lambda j: (0, j)),
        ],
        outs=[pl.BlockSpec((None, hidden + wide, part), lambda j: (j, 0, 0))],
        shapes=[array((blocks, hidden + wide, part))],
        name="second_grads",
    )[0]


def norm_grad_kernel(spots, me_ref, gj_ref, gh_ref, wj_ref, x_ref, mean_ref, inv_ref, g1_ref, g2_ref, *refs):
    ups, (*o_refs, stat_ref, sum_ref, two_ref) = refs[: len(spots)], refs[len(spots) :]
    slot = lax.bitwise_xor(pl.program_id(0), me_ref[0])
    for at in range(max(r for r, _ in spots) + 1):

        @pl.when(slot == at)
        def _():
            for (r, low), ref in zip(spots, ups):
                if r == at:
                    two_ref[:, low : low + ref.shape[0]] = dot(gh_ref[...], ref[...], NT)

    @pl.when(pl.program_id(0) == 0)
    def _():
        sum_ref[...] = jnp.sum(gj_ref[...].astype(f32), axis=0, keepdims=True)

    one, two = dot(gj_ref[...], wj_ref[...], NT), two_ref[...]
    normed = (x_ref[...].astype(f32) - mean_ref[...]) * inv_ref[...]
    total = one * g1_ref[...] + two * g2_ref[...]
    size = total.shape[0] // len(o_refs)
    for i, ref in enumerate(o_refs):
        ref[...] = total[i * size : (i + 1) * size].astype(bf16)
    for i, term in enumerate((one * normed, one, two * normed, two)):
        stat_ref[i : i + 1, :] = jnp.sum(term, axis=0, keepdims=True)


def norm_grads(chain, me, grad_joined, grad_hidden, packed, ups, x, mean, inverse, gain_one, gain_two, rows, index, pieces):
    width = x.shape[1]
    wide, hidden = grad_joined.shape[1], grad_hidden.shape[1]
    spots, parts = spots_of(ups)
    blocks, part = len(ups), ups[0][0].shape[0]
    size = rows // pieces
    column = pl.BlockSpec((rows, 1), lambda c, _: (index, 0))
    gain = pl.BlockSpec((1, part), lambda c, _: (0, c))
    return chain.run(
        functools.partial(norm_grad_kernel, spots),
        (me, grad_joined, grad_hidden, packed, x, mean, inverse, gain_one, gain_two, *parts),
        scalars=1,
        grid=(blocks,),
        ins=[
            pl.BlockSpec((rows, wide), lambda c, _: (index, 0)),
            pl.BlockSpec((rows, hidden), lambda c, _: (index, 0)),
            pl.BlockSpec((part, wide), lambda c, _: (c, 0)),
            pl.BlockSpec((rows, part), lambda c, _: (index, c)),
            column, column, gain, gain,
        ]
        + [pl.BlockSpec(p.shape, lambda c, _: (0, 0), pipeline_mode=pl.Buffered(1)) for p in parts],
        outs=[pl.BlockSpec((size, part), lambda c, _: (0, c))] * pieces
        + [pl.BlockSpec((8, part), lambda c, _: (0, c)), pl.BlockSpec((1, wide), lambda c, _: (0, 0))],
        shapes=[array((size, width))] * pieces + [array((8, width), f32), array((1, wide), f32)],
        scratch=[pltpu.VMEM((rows, part), f32)],
        name="norm_grads",
        key="norm_grads%d" % min(index, 1),
    )


def prompt_kernel(keep_ref, got_ref, cos_ref, sin_ref, _, o_ref):
    total = keep_ref[...].astype(f32) + got_ref[...].astype(f32)

    @pl.when(pl.program_id(2) == 0)
    def _():
        first = rotated_back(total[:, :LANES], cos_ref[...], sin_ref[...], kernel_roll)
        o_ref[:, :LANES] = first.astype(bf16)
        o_ref[:, LANES:] = total[:, LANES:].astype(bf16)

    @pl.when(pl.program_id(2) == 1)
    def _():
        o_ref[...] = total.astype(bf16)


def put_prompt(chain, grad_joined, kept, got, cosine, signed):
    _, _, micro, heads, own, _ = kept.shape
    part = pl.BlockSpec((None, None, None, None, own, HEAD_DIM), lambda m, h, i: (0, i, m, h, 0, 0))
    table = pl.BlockSpec((None, own, LANES), lambda m, h, i: (m, 0, 0))
    return chain.run(
        prompt_kernel,
        (kept, got, cosine, signed, grad_joined),
        grid=(micro, heads, 2),
        ins=[part, part, table, table, ANY],
        outs=[pl.BlockSpec((None, own, HEAD_DIM), lambda m, h, i: (m, 0, 3 * h + 1 + i))],
        shapes=[array(grad_joined.shape)],
        aliases={4: 0},
        name="put_prompt",
    )[0]


def pair_kernel(a_ref, b_ref, o_ref):
    o_ref[...] = (a_ref[...].astype(f32) + b_ref[...].astype(f32)).astype(bf16)


def add_pair(chain, a, b, low, size):
    width = a.shape[1]
    tile = size // 2
    row = pl.BlockSpec((tile, width), lambda i: (low // tile + i, 0))
    return chain.run(
        pair_kernel,
        (a, b),
        grid=(size // tile,),
        ins=[row, row],
        outs=[pl.BlockSpec((tile, width), lambda i: (i, 0))],
        shapes=[array((size, width))],
        name="add_pair",
    )[0]


def output_kernel(a_ref, b_ref, x_ref, dense_ref, down_ref, o_ref):
    total = a_ref[...].astype(f32) + b_ref[...].astype(f32)
    o_ref[...] = (x_ref[...].astype(f32) + total + dense_ref[...] + down_ref[...]).astype(bf16)


def input_kernel(a_ref, b_ref, x_ref, g_ref, mean_ref, inv_ref, o_ref):
    total = a_ref[...].astype(f32) + b_ref[...].astype(f32)
    inverse = inv_ref[...]
    normed = (x_ref[...].astype(f32) - mean_ref[...]) * inverse
    centred = (
        total
        - jnp.mean(total, axis=-1, keepdims=True)
        - normed * jnp.mean(total * normed, axis=-1, keepdims=True)
    )
    o_ref[...] = (g_ref[...].astype(f32) + inverse * centred).astype(bf16)


def finish(chain, a, b, start, rows, columns=(), vectors=()):
    size, width = a.shape
    tile = size // 2
    at = start // tile
    here = pl.BlockSpec((tile, width), lambda i: (i, 0))
    there = pl.BlockSpec((tile, width), lambda i: (at + i, 0))
    column = pl.BlockSpec((tile, 1), lambda i: (at + i, 0))
    vector = pl.BlockSpec((1, width), lambda i: (0, 0))
    return chain.run(
        input_kernel if columns else output_kernel,
        (a, b, *rows, *columns, *vectors),
        grid=(size // tile,),
        ins=[here, here] + [there] * len(rows) + [column] * len(columns) + [vector] * len(vectors),
        outs=[here],
        shapes=[array((size, width))],
        name="finish",
    )[0]


def swap(value, axis, bit):
    size = lax.axis_size(axis)
    return lax.ppermute(value, axis, [(i, i ^ (1 << bit)) for i in range(size)])


def bits_of(axis):
    return lax.axis_size(axis).bit_length() - 1


def send_xor(value, axis, offset):
    size = lax.axis_size(axis)
    return lax.ppermute(value, axis, [(i, i ^ offset) for i in range(size)])


def join(*values):
    return lax.optimization_barrier(values)


class Gather:
    def __init__(self, value, axis):
        self.axis, self.size = axis, lax.axis_size(axis)
        self.direct = self.size != 8
        offsets = range(2, self.size, 2) if self.direct else (2, 4)
        self.slots = [None] * self.size
        self.slots[0] = [value]
        self.slots[1] = [send_xor(value, axis, 1)]
        for r in offsets:
            self.slots[r] = [send_xor(value, axis, r)]

    def first(self, *others):
        here = [r for r in range(self.size) if r and self.slots[r]]
        values = join(*[self.slots[r][0] for r in here], *others)
        for r, value in zip(here, values):
            self.slots[r] = [value]
        self.fresh = []
        if not self.direct:
            near, far = self.slots[2][0], self.slots[4][0]
            half = near.shape[0] // 2
            self.fresh = [send_xor(near[:half], self.axis, 4), send_xor(far[half:], self.axis, 2)]
        self.twins = [r for r in here if r > 1]
        self.fresh += [send_xor(self.slots[r][0], self.axis, 1) for r in self.twins]
        return values[len(here) :]

    def second(self, *others):
        values = join(*self.fresh, *others)
        if not self.direct:
            self.slots[6] = list(values[:2])
            self.slots[7] = [send_xor(piece, self.axis, 1) for piece in self.slots[6]]
        for r, value in zip(self.twins, values[len(self.fresh) - len(self.twins) :]):
            self.slots[r + 1] = [value]
        return values[len(self.fresh) :]


def gather_ordered(value, axis):
    index = lax.axis_index(axis)
    held = value[None]
    for bit in range(bits_of(axis)):
        other = swap(held, axis, bit)
        low = ((index >> bit) & 1) == 0
        held = jnp.concatenate([jnp.where(low, held, other), jnp.where(low, other, held)], 0)
    return held


def add_up(value, axis):
    for bit in range(bits_of(axis)):
        value = value + swap(value, axis, bit)
    return value


def own_rows(value, start, count):
    return lax.dynamic_slice_in_dim(value, start, count, 0)


def sum_rows(partial, axis):
    index = lax.axis_index(axis)
    held, start = partial, jnp.int32(0)
    for bit in range(bits_of(axis)):
        mine = (index >> bit) & 1
        half = held.shape[0] // 2
        other = swap(own_rows(held, (1 - mine) * half, half).astype(bf16), axis, bit)
        held = own_rows(held, mine * half, half).astype(f32) + other.astype(f32)
        start = start + mine * half
    return held, start


def spread_rows(share, axis):
    index = lax.axis_index(axis)
    held = share
    for bit in reversed(range(bits_of(axis))):
        mine = (index >> bit) & 1
        other = swap(held, axis, bit)
        held = jnp.where(
            mine == 0, jnp.concatenate([held, other], 0), jnp.concatenate([other, held], 0)
        )
    return held


TO_MIDDLE = [(0, 1), (3, 2)]
ACROSS = [(1, 2), (2, 1)]
TO_ENDS = [(1, 0), (2, 3)]


class Piece:
    def __init__(self, chain, partial, first, low, size, axis, closing):
        self.chain, self.axis, self.closing = chain, axis, closing
        self.partial, self.first, self.low, self.size = partial, first, low, size

    def cross(self):
        self.pair = add_pair(self.chain, self.partial, self.first, self.low, self.size)
        self.second = lax.ppermute(self.pair, self.axis, ACROSS)

    def close(self):
        self.own = self.closing(self.pair, self.second)
        self.third = lax.ppermute(self.own, self.axis, TO_ENDS)


def local(
    tokens,
    cont_lengths,
    first_gain,
    first_bias,
    second_gain,
    second_bias,
    joined_weight,
    joined_bias,
    dense_weight,
    dense_bias,
    up_weight,
    up_bias,
    down_weight,
    down_bias,
    cotangent,
):
    blocks, ranks = lax.axis_size("dp"), lax.axis_size("tensor")
    me = lax.axis_index("dp").astype(jnp.int32)
    micro, _, rows, width = tokens.shape
    count = micro * rows
    own = PROMPT // blocks
    tail = rows - own
    part = width // blocks
    heads = joined_weight.shape[1] // (3 * HEAD_DIM)
    wide = heads * HEAD_DIM
    hidden = up_weight.shape[1]
    x = tokens.reshape(count, width)
    g = cotangent.reshape(count, width)
    here = me.reshape(1)

    chain = Chain()
    packed, first_gain = join(pack(chain, joined_weight, dense_weight), first_gain)
    packed = lax.all_gather(packed, "dp", axis=0, tiled=True)
    down = lax.all_gather(down_weight, "dp", axis=0, tiled=False)

    vectors = (first_gain, first_bias, second_gain, second_bias, dense_bias, down_bias)
    small = jnp.concatenate([v.reshape(-1) for v in vectors + (joined_bias, up_bias)])
    small = gather_ordered(small, "dp")
    up_here, small = join(up_weight, small)
    ups = Gather(up_here, "dp")

    small = small.astype(f32)
    full = [small[:, i * part : (i + 1) * part].reshape(1, width) for i in range(6)]
    gain_one, bias_one, gain_two, bias_two, dense_add, down_add = full

    def by_head(start, like):
        piece = small[:, start : start + like.size].reshape((blocks,) + like.shape)
        return jnp.transpose(piece, (1, 0, 2)).reshape(1, -1)

    joined_add = by_head(6 * part, joined_bias)
    up_add = by_head(6 * part + joined_bias.size, up_bias)

    seg_ends = jnp.cumsum(cont_lengths[:, 0], axis=1)
    slots = jnp.arange(tail, dtype=jnp.int32)
    passed = (slots[None, :, None] >= seg_ends[:, None, :]).astype(jnp.int32)
    first = jnp.sum(passed * cont_lengths[:, 0][:, None, :], axis=2)
    prompt_pos = jnp.broadcast_to(me * own + jnp.arange(own, dtype=jnp.int32), (micro, own))
    positions = jnp.concatenate([prompt_pos, PROMPT + slots[None] - first], axis=1)
    cosine, signed = rope_tables(positions)

    norm_one, norm_two, mean, inverse, upstream_sum = norms(chain, x, g, gain_one, bias_one, gain_two, bias_two)
    norm_one, cosine, signed, packed = ups.first(norm_one, cosine, signed, packed)

    q, k, v, prompt = qkv(chain, norm_one.reshape(micro, rows, width), packed, joined_add, cosine, signed, own)
    (prompt,) = ups.second(prompt)
    prompts = Gather(prompt, "dp")
    act, slope = ff_forward(chain, here, norm_two, ups.slots, up_add, rows)
    (slope,) = prompts.first(slope)
    grad_context = grad_context_of(chain, g, packed, wide)
    (grad_context,) = prompts.second(grad_context)
    prompts, ups = prompts.slots, ups.slots

    line = ranks == 4
    pieces = 2
    size = rows // pieces
    context, grad_joined, kept, sent = attention(
        chain, here, q, k, v, prompts, grad_context, first[..., None], cosine, signed
    )
    got = send_xor(sent, "dp", 1)

    def close_output(start):
        return lambda a, b: finish(chain, a, b, start, (x,), vectors=(dense_add, down_add))

    def close_input(start):
        return lambda a, b: finish(chain, a, b, start, (x, g), columns=(mean, inverse))

    rank = lax.axis_index("tensor")
    end = ((rank == 0) | (rank == 3)).astype(jnp.int32).reshape(1)
    have = {"kept": kept, "got": got, "bit": 1, "joined": grad_joined, "stats": [], "joined_sums": [], "results": [None, None]}
    partials, sums = [None] * (2 * micro), []

    def along_rows(value, like):
        lead, span = like.shape
        value = jnp.transpose(value.reshape(lead, blocks, span), (1, 0, 2)).reshape(blocks, lead * span)
        return jnp.pad(value, ((0, 0), (0, part - lead * span))).reshape(1, width)

    def sums_of_all():
        stats = functools.reduce(jnp.add, have["stats"])
        joined_sums = functools.reduce(jnp.add, have["joined_sums"])
        rows_of = [stats, upstream_sum, along_rows(have["up_sums"], up_bias), along_rows(joined_sums, joined_bias)]
        return jnp.concatenate(rows_of + [jnp.zeros((1, width), f32)], 0)

    def scattered(value):
        return lax.psum_scatter(value, "dp", scatter_dimension=0, tiled=value.ndim == 2)

    def step(what, *which):
        if what == "mix":
            partials[which[0]] = mix(chain, act, context, down, packed, rows, which[0], 1 if which[0] in MERGED else pieces)
        elif what == "go":
            stage, i, *behind = which
            partial, start = partials[stage][i], (stage % micro) * rows + i * size
            if line:
                if behind:
                    piece = sums[behind[0]]
                    partial, piece.pair = join(partial, piece.pair)
                got = lax.ppermute(partial, "tensor", TO_MIDDLE)
                for low in range(0, partial.shape[0], size):
                    closing = (close_output, close_input)[stage // micro](start + low)
                    sums.append(Piece(chain, partial, got, low, size, "tensor", closing))
        elif what == "fold":
            for _ in range(1 if line or have["bit"] == 1 else bits_of("dp") - 2):
                kept, sent = fold(chain, have["kept"], have["got"])
                have["kept"], have["got"] = kept, send_xor(sent, "dp", 1 << have["bit"])
                have["bit"] += 1
        elif what == "ffb":
            have["hidden"] = ff_backward(chain, g, down, slope, rows)
        elif what == "up":
            have["up"], have["up_sums"] = outer(chain, norm_two, have["hidden"], "outer0")
        elif what == "second":
            have["second"] = second_grads(chain, act, context, g, blocks)
        elif what == "joined":
            have["joined_grad"] = outer_more(chain, norm_one, have["joined"], sums_of_all(), "outer1")
        elif what == "send":
            if line and len(which) > 1:
                piece = sums[which[1]]
                piece.pair, have[which[0]] = join(piece.pair, have[which[0]])
            have[which[0]] = scattered(have[which[0]])
        elif what == "prompt":
            put = put_prompt(chain, have["joined"], have["kept"], have["got"], cosine, signed)
            have["joined"] = put.reshape(count, 3 * wide)
        elif what == "norm":
            m = which[0]
            *parts, stat, joined_sums = norm_grads(
                chain, here, have["joined"], have["hidden"], packed, ups, x, mean, inverse, gain_one, gain_two,
                rows, m, 1 if micro + m in MERGED else pieces,
            )
            partials[micro + m] = parts
            have["stats"].append(stat[:4])
            have["joined_sums"].append(joined_sums)
        elif not line:
            pass
        elif what == "cross":
            sums[which[0]].cross()
        elif what == "close":
            k = which[0]
            if 1 <= k < BACK:
                sums[k].pair, sums[k - 1].third = join(sums[k].pair, sums[k - 1].third)
            sums[k].close()
        elif what == "place":
            low, high = which
            kind = low // (2 * pieces)
            have["results"][kind] = place(chain, have["results"][kind], end, sums[low:high], low * size % count, count)
        elif what == "tie":
            piece = sums[which[1]]
            piece.pair, have[which[0]] = join(piece.pair, have[which[0]])

    for one in PLAN:
        step(*one)
    up_out, second_out, joined_out = have["up"], have["second"], have["joined_grad"]
    if line:
        have["results"][1], joined_out = join(have["results"][1], joined_out)
        output, input_grad = [r.reshape(micro, rows, width) for r in have["results"]]
    joined_out = joined_out.astype(f32)
    vector = joined_out[:, 3 * wide : 3 * wide + 8].T
    joined_out = joined_out[:, : 3 * wide]
    gains = add_up(vector[:4], "tensor")
    if not line:
        outputs, inputs = [], []
        for m in range(micro):
            share, start = sum_rows(jnp.concatenate(partials[m]), "tensor")
            span = share.shape[0]
            mine = own_rows(x, m * rows + start, span).astype(f32)
            outputs.append(spread_rows((mine + share + dense_add + down_add).astype(bf16), "tensor"))
            share, start = sum_rows(jnp.concatenate(partials[micro + m]), "tensor")
            start = m * rows + start
            row_inverse = own_rows(inverse, start, span)
            row_normed = (own_rows(x, start, span).astype(f32) - own_rows(mean, start, span)) * row_inverse
            centred = (
                share
                - jnp.mean(share, axis=-1, keepdims=True)
                - row_normed * jnp.mean(share * row_normed, axis=-1, keepdims=True)
            )
            result = own_rows(g, start, span).astype(f32) + row_inverse * centred
            inputs.append(spread_rows(result.astype(bf16), "tensor"))
        output, input_grad = jnp.stack(outputs), jnp.stack(inputs)

    return (
        output[:, None],
        input_grad[:, None],
        gains[0],
        gains[1],
        gains[2],
        gains[3],
        joined_out,
        vector[6, : joined_bias.size].reshape(joined_bias.shape),
        second_out[hidden:].astype(f32),
        vector[4],
        up_out.astype(f32),
        vector[5, : up_bias.size].reshape(up_bias.shape),
        second_out[:hidden].astype(f32),
        vector[4],
    )


def solution(mesh):
    placed = (
        P(None, "dp", None, None),
        P(None, "dp", None),
        P("dp"),
        P("dp"),
        P("dp"),
        P("dp"),
        P("dp", "tensor"),
        P("tensor", "dp"),
        P("tensor", "dp"),
        P("dp"),
        P("dp", "tensor"),
        P("tensor", "dp"),
        P("tensor", "dp"),
        P("dp"),
        P(None, "dp", None, None),
    )
    return jax.shard_map(
        local,
        mesh=mesh,
        in_specs=placed,
        out_specs=(
            P(None, "dp", None, None),
            P(None, "dp", None, None),
            P("dp"),
            P("dp"),
            P("dp"),
            P("dp"),
            P("dp", "tensor"),
            P("tensor", "dp"),
            P("tensor", "dp"),
            P("dp"),
            P("dp", "tensor"),
            P("tensor", "dp"),
            P("tensor", "dp"),
            P("dp"),
        ),
        check_vma=False,
    )
```

```python
import functools

import jax
import jax.numpy as jnp
from jax import lax
from jax.experimental import pallas as pl
from jax.experimental.pallas import tpu as pltpu
from jax.sharding import PartitionSpec as P

HEAD_DIM = 256
ROT_DIMS = 64
PROMPT = 1024
LONGEST = 128

norm_eps = 1e-05
rope_base = 10000.0
masked_score = -1e30
scale = HEAD_DIM**-0.5
LANES = 128
VMEM = 60 << 20

f32, bf16 = jnp.float32, jnp.bfloat16
NN = (((1,), (0,)), ((), ()))
NT = (((1,), (1,)), ((), ()))
TN = (((0,), (0,)), ((), ()))

TAIL_P = 0.32
TAIL = (
    -0.02115197293220867,
    0.09575628590143809,
    -0.14740109756488956,
    0.06607995422323057,
    -0.0098602948578973,
    0.058840354546090344,
    0.08778712629904878,
    0.11462742044446793,
    0.12766067496581068,
    0.12766153278717104,
)
PEAK = 0.3989422804014327


def dot(a, b, dims=NN):
    return lax.dot_general(a, b, dims, preferred_element_type=f32)


TIMES = {
    "pack": 2.3,
    "norms": 12.4,
    "qkv": 14.0,
    "grad_context": 7.0,
    "ff_forward": 28.0,
    "attention": 25.0,
    "mix0": 13.0,
    "mix1": 13.0,
    "second_grads": 20.0,
    "fold": 3.5,
    "add_pair": 3.0,
    "finish": 40.0,
    "ff_backward": 18.5,
    "put_prompt": 5.4,
    "norm_grads0": 16.0,
    "norm_grads1": 16.0,
    "stack": 8.0,
    "outer0": 17.0,
    "outer1": 13.0,
    "place": 4.5,
}
FLOPS = 1.15e9
SHARE = 2.0
BACK = 5
END_TIE = 7
PLAN = (('mix', 0), ('go', 0, 0), ('go', 0, 1), ('mix', 1), ('fold',), ('ffb',), ('cross', 0), ('go', 1, 0, 0), ('up',), ('cross', 1), ('go', 1, 1, 1), ('send', 'up', 1), ('stack',), ('fold',), ('close', 0), ('second',), ('cross', 2), ('send', 'second', 2), ('close', 1), ('prompt',), ('norm', 0), ('go', 2, 0, 2), ('cross', 3), ('go', 2, 1, 3), ('close', 2), ('place', 0, 2), ('norm', 1), ('go', 3, 0, 3), ('cross', 4), ('go', 3, 1, 4), ('close', 3), ('joined',), ('cross', 5), ('send', 'joined_grad', 5), ('close', 4), ('place', 2, 4), ('cross', 6), ('close', 5), ('cross', 7), ('close', 6), ('place', 4, 6), ('tie', 'up', 7), ('tie', 'second', 7), ('close', 7), ('place', 6, 7), ('place', 7, 8))
MERGED = ()


def cost(name):
    return pl.CostEstimate(flops=int(TIMES[name] * FLOPS * SHARE), bytes_accessed=0, transcendentals=0)


ANY = pl.BlockSpec(memory_space=pl.ANY)


class Chain:
    def __init__(self):
        self.last = ()

    def run(self, kernel, args, *, grid, ins, outs, shapes, name, key=None, scalars=0, scratch=(), aliases=None):
        count, extra = len(args), tuple(e for e in self.last if all(e is not a for a in args))

        def body(*refs):
            kernel(*refs[:count], *refs[count + len(extra) :])

        results = pl.pallas_call(
            body,
            grid_spec=pltpu.PrefetchScalarGridSpec(
                num_scalar_prefetch=scalars,
                grid=grid,
                in_specs=list(ins) + [ANY] * len(extra),
                out_specs=outs,
                scratch_shapes=list(scratch),
            ),
            out_shape=shapes,
            input_output_aliases=aliases or {},
            compiler_params=pltpu.CompilerParams(vmem_limit_bytes=VMEM),
            cost_estimate=cost(key or name),
            name=name,
        )(*args, *extra)
        self.last = (results[0],)
        return results


def array(shape, dtype=bf16):
    return jax.ShapeDtypeStruct(tuple(shape), dtype)


def rope_tables(positions):
    half = ROT_DIMS // 2
    inverse = rope_base ** (-(2.0 * jnp.arange(half, dtype=f32)) / ROT_DIMS)
    angles = positions.astype(f32)[..., None] * inverse
    ones = jnp.ones(positions.shape + (LANES - ROT_DIMS,), f32)
    c, s = jnp.cos(angles), jnp.sin(angles)
    return jnp.concatenate([c, c, ones], -1), jnp.concatenate([-s, s, ones * 0.0], -1)


def swap_halves(u, roll):
    half = ROT_DIMS // 2
    lane = lax.broadcasted_iota(jnp.int32, u.shape, u.ndim - 1)
    up, down = roll(u, LANES - half), roll(u, half)
    return jnp.where(lane < half, up, jnp.where(lane < ROT_DIMS, down, 0.0))


def rotated(u, cosine, signed, roll):
    return u * cosine + swap_halves(u, roll) * signed


def rotated_back(y, cosine, signed, roll):
    return y * cosine + swap_halves(y * signed, roll)


def kernel_roll(u, by):
    return pltpu.roll(u, by, u.ndim - 1)


def plain_roll(u, by):
    return jnp.roll(u, by, -1)


def norm_kernel(x_ref, g_ref, g1_ref, b1_ref, g2_ref, b2_ref, n1_ref, n2_ref, mean_ref, inv_ref, sum_ref):
    x = x_ref[...].astype(f32)
    mean = jnp.mean(x, axis=-1, keepdims=True)
    centered = x - mean
    inverse = lax.rsqrt(jnp.mean(centered * centered, axis=-1, keepdims=True) + norm_eps)
    normed = centered * inverse
    n1_ref[...] = (normed * g1_ref[...] + b1_ref[...]).astype(bf16)
    n2_ref[...] = (normed * g2_ref[...] + b2_ref[...]).astype(bf16)
    mean_ref[...] = mean
    inv_ref[...] = inverse

    @pl.when(pl.program_id(0) == 0)
    def _():
        sum_ref[...] = jnp.zeros_like(sum_ref)

    sum_ref[...] += jnp.sum(g_ref[...].astype(f32), axis=0, keepdims=True)


def norms(chain, x, g, gain_one, bias_one, gain_two, bias_two):
    count, width = x.shape
    tile = count // 8
    row = pl.BlockSpec((tile, width), lambda i: (i, 0))
    vector = pl.BlockSpec((1, width), lambda i: (0, 0))
    column = pl.BlockSpec((tile, 1), lambda i: (i, 0))
    return chain.run(
        norm_kernel,
        (x, g, gain_one, bias_one, gain_two, bias_two),
        grid=(count // tile,),
        ins=[row, row] + [vector] * 4,
        outs=[row, row, column, column, vector],
        shapes=[array((count, width))] * 2 + [array((count, 1), f32)] * 2 + [array((1, width), f32)],
        name="norms",
    )


def outer_kernel(a_ref, b_ref, o_ref, sum_ref):
    o_ref[...] = dot(a_ref[...], b_ref[...], TN).astype(bf16)

    @pl.when(pl.program_id(0) == 0)
    def _():
        sum_ref[...] = jnp.sum(b_ref[...].astype(f32), axis=0, keepdims=True)


def outer(chain, a, b, key):
    count, width = a.shape
    cols = b.shape[1]
    tile = width // 4
    return chain.run(
        outer_kernel,
        (a, b),
        grid=(4,),
        ins=[pl.BlockSpec((count, tile), lambda i: (0, i)), pl.BlockSpec((count, cols), lambda i: (0, 0))],
        outs=[pl.BlockSpec((tile, cols), lambda i: (i, 0)), pl.BlockSpec((1, cols), lambda i: (0, 0))],
        shapes=[array((width, cols)), array((1, cols), f32)],
        name="outer",
        key=key,
    )


def outer_more_kernel(a_ref, b_ref, more_ref, o_ref):
    cols = b_ref.shape[1]
    o_ref[:, :cols] = dot(a_ref[...], b_ref[...], TN).astype(bf16)
    o_ref[:, cols:] = jnp.zeros((o_ref.shape[0], LANES), bf16)
    o_ref[:, cols : cols + more_ref.shape[0]] = more_ref[...].T.astype(bf16)


def outer_more(chain, a, b, more, key):
    count, width = a.shape
    cols = b.shape[1]
    tile = width // 4
    return chain.run(
        outer_more_kernel,
        (a, b, more),
        grid=(4,),
        ins=[
            pl.BlockSpec((count, tile), lambda i: (0, i)),
            pl.BlockSpec((count, cols), lambda i: (0, 0)),
            pl.BlockSpec((more.shape[0], tile), lambda i: (0, i)),
        ],
        outs=[pl.BlockSpec((tile, cols + LANES), lambda i: (i, 0))],
        shapes=[array((width, cols + LANES))],
        name="outer",
        key=key,
    )[0]


def place_kernel(flag_ref, *refs):
    o_ref = refs[-1]
    pieces = len(refs) // 2 if len(refs) % 2 else len(refs) // 2 - 1
    for i in range(pieces):
        for flag in (0, 1):

            @pl.when((flag_ref[0] == flag) & (pl.program_id(0) // 2 == i))
            def _():
                o_ref[...] = refs[2 * i + flag][...]


def place(chain, held, flag, pieces, start, total):
    size, width = pieces[0].own.shape
    tile = size // 2
    keep = () if held is None else (held,)
    ins, args = [], []
    for i, piece in enumerate(pieces):
        args += [piece.own, piece.third]
        ins += [
            pl.BlockSpec((tile, width), lambda j, flag, i=i: (jnp.clip(j - 2 * i, 0, 1) * (1 - flag[0]), 0)),
            pl.BlockSpec((tile, width), lambda j, flag, i=i: (jnp.clip(j - 2 * i, 0, 1) * flag[0], 0)),
        ]
    return chain.run(
        place_kernel,
        (flag, *args) + keep,
        scalars=1,
        grid=(2 * len(pieces),),
        ins=ins + [ANY] * len(keep),
        outs=[pl.BlockSpec((tile, width), lambda j, _: (start // tile + j, 0))],
        shapes=[array((total, width))],
        aliases={1 + len(args): 0} if keep else {},
        name="place",
    )[0]


def pack_kernel(joined_ref, dense_ref, o_ref):
    wide = joined_ref.shape[1]
    o_ref[:, :wide] = joined_ref[...]
    o_ref[:, wide:] = dense_ref[...].T


def pack(chain, joined, dense):
    part, wide = joined.shape
    total = wide + dense.shape[0]

    def whole(rows, columns):
        return pl.BlockSpec((rows, columns), lambda i: (0, 0))

    return chain.run(
        pack_kernel,
        (joined, dense),
        grid=(1,),
        ins=[whole(*joined.shape), whole(*dense.shape)],
        outs=[whole(part, total)],
        shapes=[array((part, total))],
        name="pack",
    )[0]


def qkv_kernel(x_ref, w_ref, bias_ref, cos_ref, sin_ref, q_ref, k_ref, v_ref, prompt_ref):
    joined = dot(x_ref[...], w_ref[...]) + bias_ref[...]
    c, s = cos_ref[...], sin_ref[...]
    for part, ref in ((0, q_ref), (1, k_ref)):
        base = part * HEAD_DIM
        head = joined[:, base : base + HEAD_DIM]
        ref[:, :LANES] = rotated(head[:, :LANES], c, s, kernel_roll).astype(bf16)
        ref[:, LANES:] = head[:, LANES:].astype(bf16)
    v_ref[...] = joined[:, 2 * HEAD_DIM :].astype(bf16)
    own = prompt_ref.shape[1]
    prompt_ref[0] = k_ref[:own, :]
    prompt_ref[1] = v_ref[:own, :]


def qkv(chain, norm_one, weight, bias, cosine, signed, own):
    micro, rows, width = norm_one.shape
    wide = 3 * HEAD_DIM
    heads = bias.shape[1] // wide
    head = pl.BlockSpec((None, None, rows, HEAD_DIM), lambda h, m: (m, h, 0, 0))
    table = pl.BlockSpec((None, rows, LANES), lambda h, m: (m, 0, 0))
    return chain.run(
        qkv_kernel,
        (norm_one, weight, bias, cosine, signed),
        grid=(heads, micro),
        ins=[
            pl.BlockSpec((None, rows, width), lambda h, m: (m, 0, 0)),
            pl.BlockSpec((width, wide), lambda h, m: (0, h)),
            pl.BlockSpec((1, wide), lambda h, m: (0, h)),
            table,
            table,
        ],
        outs=[head] * 3 + [pl.BlockSpec((2, None, None, own, HEAD_DIM), lambda h, m: (0, m, h, 0, 0))],
        shapes=[array((micro, heads, rows, HEAD_DIM))] * 3 + [array((2, micro, heads, own, HEAD_DIM))],
        name="qkv",
    )


def attention_kernel(layout, me_ref, q_ref, k_ref, v_ref, up_ref, first_ref, cos_ref, sin_ref, *refs):
    ctx_ref, grad_ref, keep_ref, send_ref, dk_acc, dv_acc = refs[-6:]
    blocks, own = len(layout), refs[0].shape[1]
    rows = q_ref.shape[0]
    tail = rows - own
    shared = blocks * own
    me = me_ref[0]
    pk = jnp.concatenate([refs[spots[0]][0] for spots in layout], 0)
    pv = jnp.concatenate([refs[spots[-1]][refs[spots[-1]].shape[0] - 1] for spots in layout], 0)
    ck, cv = k_ref[own:, :], v_ref[own:, :]
    dk_acc[...] = jnp.zeros_like(dk_acc)
    dv_acc[...] = jnp.zeros_like(dv_acc)

    def chunk(start, count, low, high):
        here = slice(start, start + count)
        q, up = q_ref[here, :], up_ref[here, :]
        sp = dot(q, pk, NT) * scale
        parts = []
        if high > low:
            wk, wv = ck[low:high], cv[low:high]
            sw = dot(q, wk, NT) * scale
            key = lax.broadcasted_iota(jnp.int32, sw.shape, 1) + low
            slot = lax.broadcasted_iota(jnp.int32, sw.shape, 0) + (start - own)
            first = first_ref[start - own : start - own + count, :]
            sw = jnp.where((key >= first) & (key <= slot), sw, masked_score)
            parts = [(sp, pk, pv, 0), (sw, wk, wv, shared + low)]
        else:
            spot = lax.broadcasted_iota(jnp.int32, sp.shape, 1)
            key = lax.bitwise_xor(spot // own, me) * own + spot % own
            slot = lax.broadcasted_iota(jnp.int32, sp.shape, 0) + (me * own + start)
            parts = [(jnp.where(key <= slot, sp, masked_score), pk, pv, 0)]
        highest = functools.reduce(jnp.maximum, [jnp.max(s, -1, keepdims=True) for s, *_ in parts])
        raised = [jnp.exp(s - highest) for s, *_ in parts]
        total = functools.reduce(jnp.add, [jnp.sum(r, -1, keepdims=True) for r in raised])
        inverse = 1.0 / total
        probs = [r * inverse for r in raised]
        lows = [p.astype(bf16) for p in probs]
        ctx = functools.reduce(jnp.add, [dot(p, v) for p, (_, _, v, _) in zip(lows, parts)])
        ctx_ref[here, :] = ctx.astype(bf16)
        dps = [dot(up, v, NT) for _, _, v, _ in parts]
        delta = functools.reduce(
            jnp.add, [jnp.sum(p * d, -1, keepdims=True) for p, d in zip(probs, dps)]
        )
        dss = [(p * (d - delta)).astype(bf16) for p, d in zip(probs, dps)]
        dq = functools.reduce(jnp.add, [dot(d, k) for d, (_, k, _, _) in zip(dss, parts)]) * scale
        c, s = cos_ref[here, :], sin_ref[here, :]
        grad_ref[here, :LANES] = rotated_back(dq[:, :LANES], c, s, kernel_roll).astype(bf16)
        grad_ref[here, LANES:HEAD_DIM] = dq[:, LANES:].astype(bf16)
        for p, d, (_, k, _, base) in zip(lows, dss, parts):
            there = slice(base, base + k.shape[0])
            dv_acc[there, :] += dot(p, up, TN)
            dk_acc[there, :] += dot(d, q, TN)

    chunk(0, own, 0, 0)
    step = 2 * LONGEST
    for at in range(0, tail, step):
        size = min(step, tail - at)
        chunk(own + at, size, max(0, at - LONGEST), at + size)

    for r in range(blocks):
        ref, there = (keep_ref, send_ref)[r % 2], slice(r * own, (r + 1) * own)
        ref[r // 2, 0] = (dk_acc[there, :] * scale).astype(bf16)
        ref[r // 2, 1] = dv_acc[there, :].astype(bf16)
    dk = dk_acc[shared:, :] * scale
    c, s = cos_ref[own:, :], sin_ref[own:, :]
    grad_ref[:own, HEAD_DIM:] = jnp.zeros((own, 2 * HEAD_DIM), bf16)
    grad_ref[own:, HEAD_DIM : HEAD_DIM + LANES] = rotated_back(
        dk[:, :LANES], c, s, kernel_roll
    ).astype(bf16)
    grad_ref[own:, HEAD_DIM + LANES : 2 * HEAD_DIM] = dk[:, LANES:].astype(bf16)
    grad_ref[own:, 2 * HEAD_DIM :] = dv_acc[shared:, :].astype(bf16)


def attention(chain, me, q, k, v, prompts, grad_context, first, cosine, signed):
    micro, heads, rows, _ = q.shape
    blocks = len(prompts)
    pieces = [piece for slot in prompts for piece in slot]
    own = pieces[0].shape[3]
    layout, at = [], 0
    for slot in prompts:
        layout.append(tuple(range(at, at + len(slot))))
        at += len(slot)
    shared, tail = blocks * own, rows - own
    head = pl.BlockSpec((None, None, rows, HEAD_DIM), lambda m, h, _: (m, h, 0, 0))
    prompt = [pl.BlockSpec((p.shape[0], None, None, own, HEAD_DIM), lambda m, h, _: (0, m, h, 0, 0)) for p in pieces]
    half = pl.BlockSpec((blocks // 2, 2, None, None, own, HEAD_DIM), lambda m, h, _: (0, 0, m, h, 0, 0))
    flat = pl.BlockSpec((rows, HEAD_DIM), lambda m, h, _: (m, h))
    table = pl.BlockSpec((None, rows, LANES), lambda m, h, _: (m, 0, 0))
    return chain.run(
        functools.partial(attention_kernel, layout),
        (me, q, k, v, grad_context, first, cosine, signed, *pieces),
        scalars=1,
        grid=(micro, heads),
        ins=[head, head, head, flat, pl.BlockSpec((None, tail, 1), lambda m, h, _: (m, 0, 0)), table, table] + prompt,
        outs=[flat, pl.BlockSpec((None, rows, 3 * HEAD_DIM), lambda m, h, _: (m, 0, h)), half, half],
        shapes=[array((micro * rows, heads * HEAD_DIM)), array((micro, rows, heads * 3 * HEAD_DIM))]
        + [array((blocks // 2, 2, micro, heads, own, HEAD_DIM))] * 2,
        scratch=[pltpu.VMEM((shared + tail, HEAD_DIM), f32)] * 2,
        name="attention",
    )


def fold_kernel(a_ref, b_ref, keep_ref, send_ref):
    for i, ref in enumerate((keep_ref, send_ref)):
        ref[0] = (a_ref[i].astype(f32) + b_ref[i].astype(f32)).astype(bf16)


def fold(chain, kept, got):
    slots, shape = kept.shape[0], kept.shape[1:]
    count = kept.size // (slots * HEAD_DIM)
    one = pl.BlockSpec((1, count, HEAD_DIM), lambda i: (i, 0, 0))
    two = pl.BlockSpec((2, count, HEAD_DIM), lambda i: (i, 0, 0))
    keep, send = chain.run(
        fold_kernel,
        (kept.reshape(slots, count, HEAD_DIM), got.reshape(slots, count, HEAD_DIM)),
        grid=(slots // 2,),
        ins=[two, two],
        outs=[one, one],
        shapes=[array((slots // 2, count, HEAD_DIM))] * 2,
        name="fold",
    )
    return keep.reshape((slots // 2,) + shape), send.reshape((slots // 2,) + shape)


def slot_of(j, me, part, low, size):
    return pl.ds(pl.multiple_of(lax.bitwise_xor(jnp.int32(j), me) * part + low, LANES), size)


def context_kernel(g_ref, w_ref, o_ref):
    o_ref[...] = dot(g_ref[...], w_ref[...]).astype(bf16)


def grad_context_of(chain, g, packed, wide):
    count, width = g.shape
    tile = count // 4
    at = packed.shape[1] // wide - 1
    return chain.run(
        context_kernel,
        (g, packed),
        grid=(count // tile,),
        ins=[pl.BlockSpec((tile, width), lambda i: (i, 0)), pl.BlockSpec((width, wide), lambda i: (0, at))],
        outs=[pl.BlockSpec((tile, wide), lambda i: (i, 0))],
        shapes=[array((count, wide))],
        name="grad_context",
    )[0]


def forward_kernel(spots, part, me_ref, n_ref, bias_ref, *refs):
    ups, (act_ref, slope_ref, up_ref) = refs[: len(spots)], refs[len(spots) :]
    me = me_ref[0]

    @pl.when(pl.program_id(1) == 0)
    def _():
        for (r, low), ref in zip(spots, ups):
            up_ref[slot_of(r, me, part, low, ref.shape[0]), :] = ref[...]

    h = dot(n_ref[...], up_ref[...]) + bias_ref[...]
    z = jnp.abs(h)
    e = jnp.exp(-0.5 * (h * h))
    t = 1.0 / (1.0 + TAIL_P * z)
    q = jnp.full_like(t, TAIL[0])
    for co in TAIL[1:]:
        q = q * t + co
    low = e * (t * q)
    cdf = jnp.where(h >= 0.0, 1.0 - low, low)
    act_ref[...] = (h * cdf).astype(bf16)
    slope_ref[...] = (cdf + h * (e * PEAK)).astype(bf16)


def spots_of(slots):
    spots, pieces = [], []
    for r, slot in enumerate(slots):
        low = 0
        for piece in slot:
            spots.append((r, low))
            pieces.append(piece)
            low += piece.shape[0]
    return spots, pieces


def ff_forward(chain, me, norm_two, ups, bias, rows):
    count, width = norm_two.shape
    spots, pieces = spots_of(ups)
    part, hidden = ups[0][0].shape
    cols = min(512, hidden)
    out = pl.BlockSpec((rows, cols), lambda c, r, _: (r, c))
    return chain.run(
        functools.partial(forward_kernel, spots, part),
        (me, norm_two, bias, *pieces),
        scalars=1,
        grid=(hidden // cols, count // rows),
        ins=[
            pl.BlockSpec((rows, width), lambda c, r, _: (r, 0)),
            pl.BlockSpec((1, cols), lambda c, r, _: (0, c)),
        ]
        + [pl.BlockSpec((p.shape[0], cols), lambda c, r, _: (0, c)) for p in pieces],
        outs=[out, out],
        shapes=[array((count, hidden))] * 2,
        scratch=[pltpu.VMEM((width, cols), bf16)],
        name="ff_forward",
    )


def stack_kernel(spots, *refs):
    o_ref = refs[-1]
    for (r, low), ref in zip(spots, refs):
        o_ref[r, low : low + ref.shape[0], :] = ref[...]


def stack(chain, slots):
    spots, pieces = spots_of(slots)
    part, hidden = slots[0][0].shape
    cols = min(512, hidden)
    return chain.run(
        functools.partial(stack_kernel, spots),
        tuple(pieces),
        grid=(hidden // cols,),
        ins=[pl.BlockSpec((p.shape[0], cols), lambda c: (0, c)) for p in pieces],
        outs=[pl.BlockSpec((len(slots), part, cols), lambda c: (0, 0, c))],
        shapes=[array((len(slots), part, hidden))],
        name="stack",
    )[0]


def backward_kernel(g_ref, down_ref, slope_ref, grad_ref, rows_ref):
    blocks, _, part = down_ref.shape

    @pl.when(pl.program_id(1) == 0)
    def _():
        for j in range(blocks):
            rows_ref[:, j * part : (j + 1) * part] = down_ref[j]

    ga = dot(g_ref[...], rows_ref[...], NT)
    grad_ref[...] = (ga * slope_ref[...].astype(f32)).astype(bf16)


def ff_backward(chain, g, down, slope, rows):
    count, width = g.shape
    blocks, hidden, part = down.shape
    cols = min(1024, hidden)
    out = pl.BlockSpec((rows, cols), lambda c, r: (r, c))
    return chain.run(
        backward_kernel,
        (g, down, slope),
        grid=(hidden // cols, count // rows),
        ins=[
            pl.BlockSpec((rows, width), lambda c, r: (r, 0)),
            pl.BlockSpec((blocks, cols, part), lambda c, r: (0, c, 0)),
            out,
        ],
        outs=[out],
        shapes=[array((count, hidden))],
        scratch=[pltpu.VMEM((cols, width), bf16)],
        name="ff_backward",
    )[0]


def mix_kernel(act_ref, ctx_ref, down_ref, dense_ref, *o_refs):
    total = dot(act_ref[...], down_ref[...])
    total += dot(ctx_ref[...], dense_ref[...], NT)
    size = total.shape[0] // len(o_refs)
    for i, ref in enumerate(o_refs):
        ref[...] = total[i * size : (i + 1) * size].astype(bf16)


def mix(chain, act, context, down, packed, rows, index, pieces):
    hidden = act.shape[1]
    wide = context.shape[1]
    blocks, _, part = down.shape
    size = rows // pieces
    at = packed.shape[1] // wide - 1
    return chain.run(
        mix_kernel,
        (act, context, down, packed),
        grid=(blocks,),
        ins=[
            pl.BlockSpec((rows, hidden), lambda j: (index, 0)),
            pl.BlockSpec((rows, wide), lambda j: (index, 0)),
            pl.BlockSpec((None, hidden, part), lambda j: (j, 0, 0)),
            pl.BlockSpec((part, wide), lambda j: (j, at)),
        ],
        outs=[pl.BlockSpec((size, part), lambda j: (0, j))] * pieces,
        shapes=[array((size, blocks * part))] * pieces,
        name="mix",
        key="mix%d" % min(index, 1),
    )


def second_grad_kernel(act_ref, ctx_ref, g_ref, o_ref):
    hidden = act_ref.shape[1]
    o_ref[:hidden, :] = dot(act_ref[...], g_ref[...], TN).astype(bf16)
    o_ref[hidden:, :] = dot(ctx_ref[...], g_ref[...], TN).astype(bf16)


def second_grads(chain, act, context, g, blocks):
    count, hidden = act.shape
    wide = context.shape[1]
    part = g.shape[1] // blocks
    return chain.run(
        second_grad_kernel,
        (act, context, g),
        grid=(blocks,),
        ins=[
            pl.BlockSpec((count, hidden), lambda j: (0, 0)),
            pl.BlockSpec((count, wide), lambda j: (0, 0)),
            pl.BlockSpec((count, part), lambda j: (0, j)),
        ],
        outs=[pl.BlockSpec((None, hidden + wide, part), lambda j: (j, 0, 0))],
        shapes=[array((blocks, hidden + wide, part))],
        name="second_grads",
    )[0]


def norm_grad_kernel(me_ref, gj_ref, gh_ref, wj_ref, wu_ref, x_ref, mean_ref, inv_ref, g1_ref, g2_ref, *outs):
    *o_refs, stat_ref, sum_ref = outs

    @pl.when(pl.program_id(0) == 0)
    def _():
        sum_ref[...] = jnp.sum(gj_ref[...].astype(f32), axis=0, keepdims=True)

    one = dot(gj_ref[...], wj_ref[...], NT)
    two = dot(gh_ref[...], wu_ref[...], NT)
    normed = (x_ref[...].astype(f32) - mean_ref[...]) * inv_ref[...]
    total = one * g1_ref[...] + two * g2_ref[...]
    size = total.shape[0] // len(o_refs)
    for i, ref in enumerate(o_refs):
        ref[...] = total[i * size : (i + 1) * size].astype(bf16)
    for i, term in enumerate((one * normed, one, two * normed, two)):
        stat_ref[i : i + 1, :] = jnp.sum(term, axis=0, keepdims=True)


def norm_grads(chain, me, grad_joined, grad_hidden, packed, up, x, mean, inverse, gain_one, gain_two, rows, index, pieces):
    width = x.shape[1]
    wide, hidden = grad_joined.shape[1], grad_hidden.shape[1]
    blocks, part, _ = up.shape
    size = rows // pieces
    column = pl.BlockSpec((rows, 1), lambda c, _: (index, 0))
    gain = pl.BlockSpec((1, part), lambda c, _: (0, c))
    return chain.run(
        norm_grad_kernel,
        (me, grad_joined, grad_hidden, packed, up, x, mean, inverse, gain_one, gain_two),
        scalars=1,
        grid=(blocks,),
        ins=[
            pl.BlockSpec((rows, wide), lambda c, _: (index, 0)),
            pl.BlockSpec((rows, hidden), lambda c, _: (index, 0)),
            pl.BlockSpec((part, wide), lambda c, _: (c, 0)),
            pl.BlockSpec((None, part, hidden), lambda c, me: (lax.bitwise_xor(c, me[0]), 0, 0)),
            pl.BlockSpec((rows, part), lambda c, _: (index, c)),
            column, column, gain, gain,
        ],
        outs=[pl.BlockSpec((size, part), lambda c, _: (0, c))] * pieces
        + [pl.BlockSpec((8, part), lambda c, _: (0, c)), pl.BlockSpec((1, wide), lambda c, _: (0, 0))],
        shapes=[array((size, width))] * pieces + [array((8, width), f32), array((1, wide), f32)],
        name="norm_grads",
        key="norm_grads%d" % min(index, 1),
    )


def prompt_kernel(keep_ref, got_ref, cos_ref, sin_ref, _, o_ref):
    total = keep_ref[...].astype(f32) + got_ref[...].astype(f32)

    @pl.when(pl.program_id(2) == 0)
    def _():
        first = rotated_back(total[:, :LANES], cos_ref[...], sin_ref[...], kernel_roll)
        o_ref[:, :LANES] = first.astype(bf16)
        o_ref[:, LANES:] = total[:, LANES:].astype(bf16)

    @pl.when(pl.program_id(2) == 1)
    def _():
        o_ref[...] = total.astype(bf16)


def put_prompt(chain, grad_joined, kept, got, cosine, signed):
    _, _, micro, heads, own, _ = kept.shape
    part = pl.BlockSpec((None, None, None, None, own, HEAD_DIM), lambda m, h, i: (0, i, m, h, 0, 0))
    table = pl.BlockSpec((None, own, LANES), lambda m, h, i: (m, 0, 0))
    return chain.run(
        prompt_kernel,
        (kept, got, cosine, signed, grad_joined),
        grid=(micro, heads, 2),
        ins=[part, part, table, table, ANY],
        outs=[pl.BlockSpec((None, own, HEAD_DIM), lambda m, h, i: (m, 0, 3 * h + 1 + i))],
        shapes=[array(grad_joined.shape)],
        aliases={4: 0},
        name="put_prompt",
    )[0]


def pair_kernel(a_ref, b_ref, o_ref):
    o_ref[...] = (a_ref[...].astype(f32) + b_ref[...].astype(f32)).astype(bf16)


def add_pair(chain, a, b, low, size):
    width = a.shape[1]
    tile = size // 2
    row = pl.BlockSpec((tile, width), lambda i: (low // tile + i, 0))
    return chain.run(
        pair_kernel,
        (a, b),
        grid=(size // tile,),
        ins=[row, row],
        outs=[pl.BlockSpec((tile, width), lambda i: (i, 0))],
        shapes=[array((size, width))],
        name="add_pair",
    )[0]


def output_kernel(a_ref, b_ref, x_ref, dense_ref, down_ref, o_ref):
    total = a_ref[...].astype(f32) + b_ref[...].astype(f32)
    o_ref[...] = (x_ref[...].astype(f32) + total + dense_ref[...] + down_ref[...]).astype(bf16)


def input_kernel(a_ref, b_ref, x_ref, g_ref, mean_ref, inv_ref, o_ref):
    total = a_ref[...].astype(f32) + b_ref[...].astype(f32)
    inverse = inv_ref[...]
    normed = (x_ref[...].astype(f32) - mean_ref[...]) * inverse
    centred = (
        total
        - jnp.mean(total, axis=-1, keepdims=True)
        - normed * jnp.mean(total * normed, axis=-1, keepdims=True)
    )
    o_ref[...] = (g_ref[...].astype(f32) + inverse * centred).astype(bf16)


def finish(chain, a, b, start, rows, columns=(), vectors=()):
    size, width = a.shape
    tile = size // 2
    at = start // tile
    here = pl.BlockSpec((tile, width), lambda i: (i, 0))
    there = pl.BlockSpec((tile, width), lambda i: (at + i, 0))
    column = pl.BlockSpec((tile, 1), lambda i: (at + i, 0))
    vector = pl.BlockSpec((1, width), lambda i: (0, 0))
    return chain.run(
        input_kernel if columns else output_kernel,
        (a, b, *rows, *columns, *vectors),
        grid=(size // tile,),
        ins=[here, here] + [there] * len(rows) + [column] * len(columns) + [vector] * len(vectors),
        outs=[here],
        shapes=[array((size, width))],
        name="finish",
    )[0]


def swap(value, axis, bit):
    size = lax.axis_size(axis)
    return lax.ppermute(value, axis, [(i, i ^ (1 << bit)) for i in range(size)])


def bits_of(axis):
    return lax.axis_size(axis).bit_length() - 1


def send_xor(value, axis, offset):
    size = lax.axis_size(axis)
    return lax.ppermute(value, axis, [(i, i ^ offset) for i in range(size)])


def join(*values):
    return lax.optimization_barrier(values)


class Gather:
    def __init__(self, value, axis):
        self.axis, self.size = axis, lax.axis_size(axis)
        self.direct = self.size != 8
        offsets = range(2, self.size, 2) if self.direct else (2, 4)
        self.slots = [None] * self.size
        self.slots[0] = [value]
        self.slots[1] = [send_xor(value, axis, 1)]
        for r in offsets:
            self.slots[r] = [send_xor(value, axis, r)]

    def first(self, *others):
        here = [r for r in range(self.size) if r and self.slots[r]]
        values = join(*[self.slots[r][0] for r in here], *others)
        for r, value in zip(here, values):
            self.slots[r] = [value]
        self.fresh = []
        if not self.direct:
            near, far = self.slots[2][0], self.slots[4][0]
            half = near.shape[0] // 2
            self.fresh = [send_xor(near[:half], self.axis, 4), send_xor(far[half:], self.axis, 2)]
        self.twins = [r for r in here if r > 1]
        self.fresh += [send_xor(self.slots[r][0], self.axis, 1) for r in self.twins]
        return values[len(here) :]

    def second(self, *others):
        values = join(*self.fresh, *others)
        if not self.direct:
            self.slots[6] = list(values[:2])
            self.slots[7] = [send_xor(piece, self.axis, 1) for piece in self.slots[6]]
        for r, value in zip(self.twins, values[len(self.fresh) - len(self.twins) :]):
            self.slots[r + 1] = [value]
        return values[len(self.fresh) :]


def gather_ordered(value, axis):
    index = lax.axis_index(axis)
    held = value[None]
    for bit in range(bits_of(axis)):
        other = swap(held, axis, bit)
        low = ((index >> bit) & 1) == 0
        held = jnp.concatenate([jnp.where(low, held, other), jnp.where(low, other, held)], 0)
    return held


def add_up(value, axis):
    for bit in range(bits_of(axis)):
        value = value + swap(value, axis, bit)
    return value


def own_rows(value, start, count):
    return lax.dynamic_slice_in_dim(value, start, count, 0)


def sum_rows(partial, axis):
    index = lax.axis_index(axis)
    held, start = partial, jnp.int32(0)
    for bit in range(bits_of(axis)):
        mine = (index >> bit) & 1
        half = held.shape[0] // 2
        other = swap(own_rows(held, (1 - mine) * half, half).astype(bf16), axis, bit)
        held = own_rows(held, mine * half, half).astype(f32) + other.astype(f32)
        start = start + mine * half
    return held, start


def spread_rows(share, axis):
    index = lax.axis_index(axis)
    held = share
    for bit in reversed(range(bits_of(axis))):
        mine = (index >> bit) & 1
        other = swap(held, axis, bit)
        held = jnp.where(
            mine == 0, jnp.concatenate([held, other], 0), jnp.concatenate([other, held], 0)
        )
    return held


TO_MIDDLE = [(0, 1), (3, 2)]
ACROSS = [(1, 2), (2, 1)]
TO_ENDS = [(1, 0), (2, 3)]


class Piece:
    def __init__(self, chain, partial, first, low, size, axis, closing):
        self.chain, self.axis, self.closing = chain, axis, closing
        self.partial, self.first, self.low, self.size = partial, first, low, size

    def cross(self):
        self.pair = add_pair(self.chain, self.partial, self.first, self.low, self.size)
        self.second = lax.ppermute(self.pair, self.axis, ACROSS)

    def close(self):
        self.own = self.closing(self.pair, self.second)
        self.third = lax.ppermute(self.own, self.axis, TO_ENDS)


def local(
    tokens,
    cont_lengths,
    first_gain,
    first_bias,
    second_gain,
    second_bias,
    joined_weight,
    joined_bias,
    dense_weight,
    dense_bias,
    up_weight,
    up_bias,
    down_weight,
    down_bias,
    cotangent,
):
    blocks, ranks = lax.axis_size("dp"), lax.axis_size("tensor")
    me = lax.axis_index("dp").astype(jnp.int32)
    micro, _, rows, width = tokens.shape
    count = micro * rows
    own = PROMPT // blocks
    tail = rows - own
    part = width // blocks
    heads = joined_weight.shape[1] // (3 * HEAD_DIM)
    wide = heads * HEAD_DIM
    hidden = up_weight.shape[1]
    x = tokens.reshape(count, width)
    g = cotangent.reshape(count, width)
    here = me.reshape(1)

    chain = Chain()
    packed, first_gain = join(pack(chain, joined_weight, dense_weight), first_gain)
    packed = lax.all_gather(packed, "dp", axis=0, tiled=True)
    down = lax.all_gather(down_weight, "dp", axis=0, tiled=False)

    vectors = (first_gain, first_bias, second_gain, second_bias, dense_bias, down_bias)
    small = jnp.concatenate([v.reshape(-1) for v in vectors + (joined_bias, up_bias)])
    small = gather_ordered(small, "dp")
    up_here, small = join(up_weight, small)
    ups = Gather(up_here, "dp")

    small = small.astype(f32)
    full = [small[:, i * part : (i + 1) * part].reshape(1, width) for i in range(6)]
    gain_one, bias_one, gain_two, bias_two, dense_add, down_add = full

    def by_head(start, like):
        piece = small[:, start : start + like.size].reshape((blocks,) + like.shape)
        return jnp.transpose(piece, (1, 0, 2)).reshape(1, -1)

    joined_add = by_head(6 * part, joined_bias)
    up_add = by_head(6 * part + joined_bias.size, up_bias)

    seg_ends = jnp.cumsum(cont_lengths[:, 0], axis=1)
    slots = jnp.arange(tail, dtype=jnp.int32)
    passed = (slots[None, :, None] >= seg_ends[:, None, :]).astype(jnp.int32)
    first = jnp.sum(passed * cont_lengths[:, 0][:, None, :], axis=2)
    prompt_pos = jnp.broadcast_to(me * own + jnp.arange(own, dtype=jnp.int32), (micro, own))
    positions = jnp.concatenate([prompt_pos, PROMPT + slots[None] - first], axis=1)
    cosine, signed = rope_tables(positions)

    norm_one, norm_two, mean, inverse, upstream_sum = norms(chain, x, g, gain_one, bias_one, gain_two, bias_two)
    norm_one, cosine, signed, packed = ups.first(norm_one, cosine, signed, packed)

    q, k, v, prompt = qkv(chain, norm_one.reshape(micro, rows, width), packed, joined_add, cosine, signed, own)
    (prompt,) = ups.second(prompt)
    prompts = Gather(prompt, "dp")
    act, slope = ff_forward(chain, here, norm_two, ups.slots, up_add, rows)
    (slope,) = prompts.first(slope)
    grad_context = grad_context_of(chain, g, packed, wide)
    (grad_context,) = prompts.second(grad_context)
    prompts, ups = prompts.slots, ups.slots

    line = ranks == 4
    pieces = 2
    size = rows // pieces
    context, grad_joined, kept, sent = attention(
        chain, here, q, k, v, prompts, grad_context, first[..., None], cosine, signed
    )
    got = send_xor(sent, "dp", 1)

    def close_output(start):
        return lambda a, b: finish(chain, a, b, start, (x,), vectors=(dense_add, down_add))

    def close_input(start):
        return lambda a, b: finish(chain, a, b, start, (x, g), columns=(mean, inverse))

    rank = lax.axis_index("tensor")
    end = ((rank == 0) | (rank == 3)).astype(jnp.int32).reshape(1)
    have = {"kept": kept, "got": got, "bit": 1, "joined": grad_joined, "stats": [], "joined_sums": [], "results": [None, None]}
    partials, sums = [None] * (2 * micro), []

    def along_rows(value, like):
        lead, span = like.shape
        value = jnp.transpose(value.reshape(lead, blocks, span), (1, 0, 2)).reshape(blocks, lead * span)
        return jnp.pad(value, ((0, 0), (0, part - lead * span))).reshape(1, width)

    def sums_of_all():
        stats = functools.reduce(jnp.add, have["stats"])
        joined_sums = functools.reduce(jnp.add, have["joined_sums"])
        rows_of = [stats, upstream_sum, along_rows(have["up_sums"], up_bias), along_rows(joined_sums, joined_bias)]
        return jnp.concatenate(rows_of + [jnp.zeros((1, width), f32)], 0)

    def scattered(value):
        return lax.psum_scatter(value, "dp", scatter_dimension=0, tiled=value.ndim == 2)

    def step(what, *which):
        if what == "mix":
            partials[which[0]] = mix(chain, act, context, down, packed, rows, which[0], 1 if which[0] in MERGED else pieces)
        elif what == "go":
            stage, i, *behind = which
            partial, start = partials[stage][i], (stage % micro) * rows + i * size
            if line:
                if behind:
                    piece = sums[behind[0]]
                    partial, piece.pair = join(partial, piece.pair)
                got = lax.ppermute(partial, "tensor", TO_MIDDLE)
                for low in range(0, partial.shape[0], size):
                    closing = (close_output, close_input)[stage // micro](start + low)
                    sums.append(Piece(chain, partial, got, low, size, "tensor", closing))
        elif what == "fold":
            for _ in range(1 if line or have["bit"] == 1 else bits_of("dp") - 2):
                kept, sent = fold(chain, have["kept"], have["got"])
                have["kept"], have["got"] = kept, send_xor(sent, "dp", 1 << have["bit"])
                have["bit"] += 1
        elif what == "ffb":
            have["hidden"] = ff_backward(chain, g, down, slope, rows)
        elif what == "up":
            have["up"], have["up_sums"] = outer(chain, norm_two, have["hidden"], "outer0")
        elif what == "stack":
            have["ups"] = stack(chain, ups)
        elif what == "second":
            have["second"] = second_grads(chain, act, context, g, blocks)
        elif what == "joined":
            have["joined_grad"] = outer_more(chain, norm_one, have["joined"], sums_of_all(), "outer1")
        elif what == "send":
            if line and len(which) > 1:
                piece = sums[which[1]]
                piece.pair, have[which[0]] = join(piece.pair, have[which[0]])
            have[which[0]] = scattered(have[which[0]])
        elif what == "prompt":
            put = put_prompt(chain, have["joined"], have["kept"], have["got"], cosine, signed)
            have["joined"] = put.reshape(count, 3 * wide)
        elif what == "norm":
            m = which[0]
            *parts, stat, joined_sums = norm_grads(
                chain, here, have["joined"], have["hidden"], packed, have["ups"], x, mean, inverse, gain_one, gain_two,
                rows, m, 1 if micro + m in MERGED else pieces,
            )
            partials[micro + m] = parts
            have["stats"].append(stat[:4])
            have["joined_sums"].append(joined_sums)
        elif not line:
            pass
        elif what == "cross":
            sums[which[0]].cross()
        elif what == "close":
            k = which[0]
            if 1 <= k < BACK:
                sums[k].pair, sums[k - 1].third = join(sums[k].pair, sums[k - 1].third)
            sums[k].close()
            if k == END_TIE:
                sums[k].own, have["joined_grad"] = join(sums[k].own, have["joined_grad"])
        elif what == "place":
            low, high = which
            kind = low // (2 * pieces)
            have["results"][kind] = place(chain, have["results"][kind], end, sums[low:high], low * size % count, count)
        elif what == "tie":
            piece = sums[which[1]]
            piece.pair, have[which[0]] = join(piece.pair, have[which[0]])

    for one in PLAN:
        step(*one)
    up_out, second_out, joined_out = have["up"], have["second"], have["joined_grad"]
    joined_out = joined_out.astype(f32)
    vector = joined_out[:, 3 * wide : 3 * wide + 8].T
    joined_out = joined_out[:, : 3 * wide]
    gains = vector[:4]
    if line:
        have["results"][1], gains = join(have["results"][1], gains)
        output, input_grad = [r.reshape(micro, rows, width) for r in have["results"]]
    gains = add_up(gains, "tensor")
    if not line:
        outputs, inputs = [], []
        for m in range(micro):
            share, start = sum_rows(jnp.concatenate(partials[m]), "tensor")
            span = share.shape[0]
            mine = own_rows(x, m * rows + start, span).astype(f32)
            outputs.append(spread_rows((mine + share + dense_add + down_add).astype(bf16), "tensor"))
            share, start = sum_rows(jnp.concatenate(partials[micro + m]), "tensor")
            start = m * rows + start
            row_inverse = own_rows(inverse, start, span)
            row_normed = (own_rows(x, start, span).astype(f32) - own_rows(mean, start, span)) * row_inverse
            centred = (
                share
                - jnp.mean(share, axis=-1, keepdims=True)
                - row_normed * jnp.mean(share * row_normed, axis=-1, keepdims=True)
            )
            result = own_rows(g, start, span).astype(f32) + row_inverse * centred
            inputs.append(spread_rows(result.astype(bf16), "tensor"))
        output, input_grad = jnp.stack(outputs), jnp.stack(inputs)

    return (
        output[:, None],
        input_grad[:, None],
        gains[0],
        gains[1],
        gains[2],
        gains[3],
        joined_out,
        vector[6, : joined_bias.size].reshape(joined_bias.shape),
        second_out[hidden:].astype(f32),
        vector[4],
        up_out.astype(f32),
        vector[5, : up_bias.size].reshape(up_bias.shape),
        second_out[:hidden].astype(f32),
        vector[4],
    )


def solution(mesh):
    placed = (
        P(None, "dp", None, None),
        P(None, "dp", None),
        P("dp"),
        P("dp"),
        P("dp"),
        P("dp"),
        P("dp", "tensor"),
        P("tensor", "dp"),
        P("tensor", "dp"),
        P("dp"),
        P("dp", "tensor"),
        P("tensor", "dp"),
        P("tensor", "dp"),
        P("dp"),
        P(None, "dp", None, None),
    )
    return jax.shard_map(
        local,
        mesh=mesh,
        in_specs=placed,
        out_specs=(
            P(None, "dp", None, None),
            P(None, "dp", None, None),
            P("dp"),
            P("dp"),
            P("dp"),
            P("dp"),
            P("dp", "tensor"),
            P("tensor", "dp"),
            P("tensor", "dp"),
            P("dp"),
            P("dp", "tensor"),
            P("tensor", "dp"),
            P("tensor", "dp"),
            P("dp"),
        ),
        check_vma=False,
    )
```

```python
import functools

import jax
import jax.numpy as jnp
from jax import lax
from jax.experimental import pallas as pl
from jax.experimental.pallas import tpu as pltpu
from jax.sharding import PartitionSpec as P

HEAD_DIM = 256
ROT_DIMS = 64
PROMPT = 1024
LONGEST = 128

norm_eps = 1e-05
rope_base = 10000.0
masked_score = -1e30
scale = HEAD_DIM**-0.5
LANES = 128
VMEM = 60 << 20

f32, bf16 = jnp.float32, jnp.bfloat16
NN = (((1,), (0,)), ((), ()))
NT = (((1,), (1,)), ((), ()))
TN = (((0,), (0,)), ((), ()))

TAIL_P = 0.32
TAIL = (
    -0.02115197293220867,
    0.09575628590143809,
    -0.14740109756488956,
    0.06607995422323057,
    -0.0098602948578973,
    0.058840354546090344,
    0.08778712629904878,
    0.11462742044446793,
    0.12766067496581068,
    0.12766153278717104,
)
PEAK = 0.3989422804014327


def dot(a, b, dims=NN):
    return lax.dot_general(a, b, dims, preferred_element_type=f32)


TIMES = {
    "pack": 2.3,
    "norms": 12.4,
    "qkv": 14.0,
    "grad_context": 7.0,
    "ff_forward": 28.0,
    "attention": 25.0,
    "mix0": 13.0,
    "mix1": 13.0,
    "second_grads": 20.0,
    "fold": 3.5,
    "add_pair": 3.0,
    "finish": 40.0,
    "ff_backward": 18.5,
    "put_prompt": 5.4,
    "norm_grads0": 16.0,
    "norm_grads1": 16.0,
    "stack": 8.0,
    "outer0": 17.0,
    "outer1": 13.0,
    "place": 4.5,
}
FLOPS = 1.15e9
SHARE = 2.0
BACK = 5
END_TIE = 7
PLAN = (('mix', 0), ('go', 0, 0), ('go', 0, 1), ('mix', 1), ('fold',), ('ffb',), ('cross', 0), ('go', 1, 0, 0), ('up',), ('cross', 1), ('go', 1, 1, 1), ('send', 'up', 1), ('stack',), ('fold',), ('close', 0), ('second',), ('cross', 2), ('send', 'second', 2), ('close', 1), ('prompt',), ('norm', 0), ('go', 2, 0, 2), ('cross', 3), ('go', 2, 1, 3), ('close', 2), ('place', 0, 2), ('norm', 1), ('go', 3, 0, 3), ('cross', 4), ('go', 3, 1, 4), ('close', 3), ('joined',), ('cross', 5), ('send', 'joined_grad', 5), ('close', 4), ('place', 2, 4), ('cross', 6), ('close', 5), ('cross', 7), ('close', 6), ('place', 4, 6), ('tie', 'up', 7), ('tie', 'second', 7), ('close', 7), ('place', 6, 7), ('place', 7, 8))
MERGED = ()


def cost(name):
    return pl.CostEstimate(flops=int(TIMES[name] * FLOPS * SHARE), bytes_accessed=0, transcendentals=0)


ANY = pl.BlockSpec(memory_space=pl.ANY)


class Chain:
    def __init__(self):
        self.last = ()

    def run(self, kernel, args, *, grid, ins, outs, shapes, name, key=None, scalars=0, scratch=(), aliases=None):
        count, extra = len(args), tuple(e for e in self.last if all(e is not a for a in args))

        def body(*refs):
            kernel(*refs[:count], *refs[count + len(extra) :])

        results = pl.pallas_call(
            body,
            grid_spec=pltpu.PrefetchScalarGridSpec(
                num_scalar_prefetch=scalars,
                grid=grid,
                in_specs=list(ins) + [ANY] * len(extra),
                out_specs=outs,
                scratch_shapes=list(scratch),
            ),
            out_shape=shapes,
            input_output_aliases=aliases or {},
            compiler_params=pltpu.CompilerParams(vmem_limit_bytes=VMEM),
            cost_estimate=cost(key or name),
            name=name,
        )(*args, *extra)
        self.last = (results[0],)
        return results


def array(shape, dtype=bf16):
    return jax.ShapeDtypeStruct(tuple(shape), dtype)


def rope_tables(positions):
    half = ROT_DIMS // 2
    inverse = rope_base ** (-(2.0 * jnp.arange(half, dtype=f32)) / ROT_DIMS)
    angles = positions.astype(f32)[..., None] * inverse
    ones = jnp.ones(positions.shape + (LANES - ROT_DIMS,), f32)
    c, s = jnp.cos(angles), jnp.sin(angles)
    return jnp.concatenate([c, c, ones], -1), jnp.concatenate([-s, s, ones * 0.0], -1)


def swap_halves(u, roll):
    half = ROT_DIMS // 2
    lane = lax.broadcasted_iota(jnp.int32, u.shape, u.ndim - 1)
    up, down = roll(u, LANES - half), roll(u, half)
    return jnp.where(lane < half, up, jnp.where(lane < ROT_DIMS, down, 0.0))


def rotated(u, cosine, signed, roll):
    return u * cosine + swap_halves(u, roll) * signed


def rotated_back(y, cosine, signed, roll):
    return y * cosine + swap_halves(y * signed, roll)


def kernel_roll(u, by):
    return pltpu.roll(u, by, u.ndim - 1)


def plain_roll(u, by):
    return jnp.roll(u, by, -1)


def norm_kernel(x_ref, g_ref, g1_ref, b1_ref, g2_ref, b2_ref, n1_ref, n2_ref, mean_ref, inv_ref, sum_ref):
    x = x_ref[...].astype(f32)
    mean = jnp.mean(x, axis=-1, keepdims=True)
    centered = x - mean
    inverse = lax.rsqrt(jnp.mean(centered * centered, axis=-1, keepdims=True) + norm_eps)
    normed = centered * inverse
    n1_ref[...] = (normed * g1_ref[...] + b1_ref[...]).astype(bf16)
    n2_ref[...] = (normed * g2_ref[...] + b2_ref[...]).astype(bf16)
    mean_ref[...] = mean
    inv_ref[...] = inverse

    @pl.when(pl.program_id(0) == 0)
    def _():
        sum_ref[...] = jnp.zeros_like(sum_ref)

    sum_ref[...] += jnp.sum(g_ref[...].astype(f32), axis=0, keepdims=True)


def norms(chain, x, g, gain_one, bias_one, gain_two, bias_two):
    count, width = x.shape
    tile = count // 8
    row = pl.BlockSpec((tile, width), lambda i: (i, 0))
    vector = pl.BlockSpec((1, width), lambda i: (0, 0))
    column = pl.BlockSpec((tile, 1), lambda i: (i, 0))
    return chain.run(
        norm_kernel,
        (x, g, gain_one, bias_one, gain_two, bias_two),
        grid=(count // tile,),
        ins=[row, row] + [vector] * 4,
        outs=[row, row, column, column, vector],
        shapes=[array((count, width))] * 2 + [array((count, 1), f32)] * 2 + [array((1, width), f32)],
        name="norms",
    )


def outer_kernel(a_ref, b_ref, o_ref, sum_ref):
    o_ref[...] = dot(a_ref[...], b_ref[...], TN).astype(bf16)

    @pl.when(pl.program_id(0) == 0)
    def _():
        sum_ref[...] = jnp.sum(b_ref[...].astype(f32), axis=0, keepdims=True)


def outer(chain, a, b, key):
    count, width = a.shape
    cols = b.shape[1]
    tile = width // 4
    return chain.run(
        outer_kernel,
        (a, b),
        grid=(4,),
        ins=[pl.BlockSpec((count, tile), lambda i: (0, i)), pl.BlockSpec((count, cols), lambda i: (0, 0))],
        outs=[pl.BlockSpec((tile, cols), lambda i: (i, 0)), pl.BlockSpec((1, cols), lambda i: (0, 0))],
        shapes=[array((width, cols)), array((1, cols), f32)],
        name="outer",
        key=key,
    )


def outer_more_kernel(a_ref, b_ref, more_ref, o_ref):
    cols = b_ref.shape[1]
    o_ref[:, :cols] = dot(a_ref[...], b_ref[...], TN).astype(bf16)
    o_ref[:, cols:] = jnp.zeros((o_ref.shape[0], LANES), bf16)
    o_ref[:, cols : cols + more_ref.shape[0]] = more_ref[...].T.astype(bf16)


def outer_more(chain, a, b, more, key):
    count, width = a.shape
    cols = b.shape[1]
    tile = width // 4
    return chain.run(
        outer_more_kernel,
        (a, b, more),
        grid=(4,),
        ins=[
            pl.BlockSpec((count, tile), lambda i: (0, i)),
            pl.BlockSpec((count, cols), lambda i: (0, 0)),
            pl.BlockSpec((more.shape[0], tile), lambda i: (0, i)),
        ],
        outs=[pl.BlockSpec((tile, cols + LANES), lambda i: (i, 0))],
        shapes=[array((width, cols + LANES))],
        name="outer",
        key=key,
    )[0]


def place_kernel(flag_ref, *refs):
    o_ref = refs[-1]
    pieces = len(refs) // 2 if len(refs) % 2 else len(refs) // 2 - 1
    for i in range(pieces):
        for flag in (0, 1):

            @pl.when((flag_ref[0] == flag) & (pl.program_id(0) // 2 == i))
            def _():
                o_ref[...] = refs[2 * i + flag][...]


def place(chain, held, flag, pieces, start, total):
    size, width = pieces[0].own.shape
    tile = size // 2
    keep = () if held is None else (held,)
    ins, args = [], []
    for i, piece in enumerate(pieces):
        args += [piece.own, piece.third]
        ins += [
            pl.BlockSpec((tile, width), lambda j, flag, i=i: (jnp.clip(j - 2 * i, 0, 1) * (1 - flag[0]), 0)),
            pl.BlockSpec((tile, width), lambda j, flag, i=i: (jnp.clip(j - 2 * i, 0, 1) * flag[0], 0)),
        ]
    return chain.run(
        place_kernel,
        (flag, *args) + keep,
        scalars=1,
        grid=(2 * len(pieces),),
        ins=ins + [ANY] * len(keep),
        outs=[pl.BlockSpec((tile, width), lambda j, _: (start // tile + j, 0))],
        shapes=[array((total, width))],
        aliases={1 + len(args): 0} if keep else {},
        name="place",
    )[0]


def pack_kernel(joined_ref, dense_ref, o_ref):
    wide = joined_ref.shape[1]
    o_ref[:, :wide] = joined_ref[...]
    o_ref[:, wide:] = dense_ref[...].T


def pack(chain, joined, dense):
    part, wide = joined.shape
    total = wide + dense.shape[0]

    def whole(rows, columns):
        return pl.BlockSpec((rows, columns), lambda i: (0, 0))

    return chain.run(
        pack_kernel,
        (joined, dense),
        grid=(1,),
        ins=[whole(*joined.shape), whole(*dense.shape)],
        outs=[whole(part, total)],
        shapes=[array((part, total))],
        name="pack",
    )[0]


def qkv_kernel(x_ref, w_ref, bias_ref, cos_ref, sin_ref, q_ref, k_ref, v_ref, prompt_ref):
    joined = dot(x_ref[...], w_ref[...]) + bias_ref[...]
    c, s = cos_ref[...], sin_ref[...]
    for part, ref in ((0, q_ref), (1, k_ref)):
        base = part * HEAD_DIM
        head = joined[:, base : base + HEAD_DIM]
        ref[:, :LANES] = rotated(head[:, :LANES], c, s, kernel_roll).astype(bf16)
        ref[:, LANES:] = head[:, LANES:].astype(bf16)
    v_ref[...] = joined[:, 2 * HEAD_DIM :].astype(bf16)
    own = prompt_ref.shape[1]
    prompt_ref[0] = k_ref[:own, :]
    prompt_ref[1] = v_ref[:own, :]


def qkv(chain, norm_one, weight, bias, cosine, signed, own):
    micro, rows, width = norm_one.shape
    wide = 3 * HEAD_DIM
    heads = bias.shape[1] // wide
    head = pl.BlockSpec((None, None, rows, HEAD_DIM), lambda h, m: (m, h, 0, 0))
    table = pl.BlockSpec((None, rows, LANES), lambda h, m: (m, 0, 0))
    return chain.run(
        qkv_kernel,
        (norm_one, weight, bias, cosine, signed),
        grid=(heads, micro),
        ins=[
            pl.BlockSpec((None, rows, width), lambda h, m: (m, 0, 0)),
            pl.BlockSpec((width, wide), lambda h, m: (0, h)),
            pl.BlockSpec((1, wide), lambda h, m: (0, h)),
            table,
            table,
        ],
        outs=[head] * 3 + [pl.BlockSpec((2, None, None, own, HEAD_DIM), lambda h, m: (0, m, h, 0, 0))],
        shapes=[array((micro, heads, rows, HEAD_DIM))] * 3 + [array((2, micro, heads, own, HEAD_DIM))],
        name="qkv",
    )


def attention_kernel(layout, me_ref, q_ref, k_ref, v_ref, up_ref, first_ref, cos_ref, sin_ref, *refs):
    ctx_ref, grad_ref, keep_ref, send_ref, dk_acc, dv_acc = refs[-6:]
    blocks, own = len(layout), refs[0].shape[1]
    rows = q_ref.shape[0]
    tail = rows - own
    shared = blocks * own
    me = me_ref[0]
    pk = jnp.concatenate([refs[spots[0]][0] for spots in layout], 0)
    pv = jnp.concatenate([refs[spots[-1]][refs[spots[-1]].shape[0] - 1] for spots in layout], 0)
    ck, cv = k_ref[own:, :], v_ref[own:, :]
    dk_acc[...] = jnp.zeros_like(dk_acc)
    dv_acc[...] = jnp.zeros_like(dv_acc)

    def chunk(start, count, low, high):
        here = slice(start, start + count)
        q, up = q_ref[here, :], up_ref[here, :]
        sp = dot(q, pk, NT) * scale
        parts = []
        if high > low:
            wk, wv = ck[low:high], cv[low:high]
            sw = dot(q, wk, NT) * scale
            key = lax.broadcasted_iota(jnp.int32, sw.shape, 1) + low
            slot = lax.broadcasted_iota(jnp.int32, sw.shape, 0) + (start - own)
            first = first_ref[start - own : start - own + count, :]
            sw = jnp.where((key >= first) & (key <= slot), sw, masked_score)
            parts = [(sp, pk, pv, 0), (sw, wk, wv, shared + low)]
        else:
            spot = lax.broadcasted_iota(jnp.int32, sp.shape, 1)
            key = lax.bitwise_xor(spot // own, me) * own + spot % own
            slot = lax.broadcasted_iota(jnp.int32, sp.shape, 0) + (me * own + start)
            parts = [(jnp.where(key <= slot, sp, masked_score), pk, pv, 0)]
        highest = functools.reduce(jnp.maximum, [jnp.max(s, -1, keepdims=True) for s, *_ in parts])
        raised = [jnp.exp(s - highest) for s, *_ in parts]
        total = functools.reduce(jnp.add, [jnp.sum(r, -1, keepdims=True) for r in raised])
        inverse = 1.0 / total
        probs = [r * inverse for r in raised]
        lows = [p.astype(bf16) for p in probs]
        ctx = functools.reduce(jnp.add, [dot(p, v) for p, (_, _, v, _) in zip(lows, parts)])
        ctx_ref[here, :] = ctx.astype(bf16)
        dps = [dot(up, v, NT) for _, _, v, _ in parts]
        delta = functools.reduce(
            jnp.add, [jnp.sum(p * d, -1, keepdims=True) for p, d in zip(probs, dps)]
        )
        dss = [(p * (d - delta)).astype(bf16) for p, d in zip(probs, dps)]
        dq = functools.reduce(jnp.add, [dot(d, k) for d, (_, k, _, _) in zip(dss, parts)]) * scale
        c, s = cos_ref[here, :], sin_ref[here, :]
        grad_ref[here, :LANES] = rotated_back(dq[:, :LANES], c, s, kernel_roll).astype(bf16)
        grad_ref[here, LANES:HEAD_DIM] = dq[:, LANES:].astype(bf16)
        for p, d, (_, k, _, base) in zip(lows, dss, parts):
            there = slice(base, base + k.shape[0])
            dv_acc[there, :] += dot(p, up, TN)
            dk_acc[there, :] += dot(d, q, TN)

    chunk(0, own, 0, 0)
    step = 4 * LONGEST
    for at in range(0, tail, step):
        size = min(step, tail - at)
        chunk(own + at, size, max(0, at - LONGEST), at + size)

    for r in range(blocks):
        ref, there = (keep_ref, send_ref)[r % 2], slice(r * own, (r + 1) * own)
        ref[r // 2, 0] = (dk_acc[there, :] * scale).astype(bf16)
        ref[r // 2, 1] = dv_acc[there, :].astype(bf16)
    dk = dk_acc[shared:, :] * scale
    c, s = cos_ref[own:, :], sin_ref[own:, :]
    grad_ref[:own, HEAD_DIM:] = jnp.zeros((own, 2 * HEAD_DIM), bf16)
    grad_ref[own:, HEAD_DIM : HEAD_DIM + LANES] = rotated_back(
        dk[:, :LANES], c, s, kernel_roll
    ).astype(bf16)
    grad_ref[own:, HEAD_DIM + LANES : 2 * HEAD_DIM] = dk[:, LANES:].astype(bf16)
    grad_ref[own:, 2 * HEAD_DIM :] = dv_acc[shared:, :].astype(bf16)


def attention(chain, me, q, k, v, prompts, grad_context, first, cosine, signed):
    micro, heads, rows, _ = q.shape
    blocks = len(prompts)
    pieces = [piece for slot in prompts for piece in slot]
    own = pieces[0].shape[3]
    layout, at = [], 0
    for slot in prompts:
        layout.append(tuple(range(at, at + len(slot))))
        at += len(slot)
    shared, tail = blocks * own, rows - own
    head = pl.BlockSpec((None, None, rows, HEAD_DIM), lambda m, h, _: (m, h, 0, 0))
    prompt = [pl.BlockSpec((p.shape[0], None, None, own, HEAD_DIM), lambda m, h, _: (0, m, h, 0, 0)) for p in pieces]
    half = pl.BlockSpec((blocks // 2, 2, None, None, own, HEAD_DIM), lambda m, h, _: (0, 0, m, h, 0, 0))
    flat = pl.BlockSpec((rows, HEAD_DIM), lambda m, h, _: (m, h))
    table = pl.BlockSpec((None, rows, LANES), lambda m, h, _: (m, 0, 0))
    return chain.run(
        functools.partial(attention_kernel, layout),
        (me, q, k, v, grad_context, first, cosine, signed, *pieces),
        scalars=1,
        grid=(micro, heads),
        ins=[head, head, head, flat, pl.BlockSpec((None, tail, 1), lambda m, h, _: (m, 0, 0)), table, table] + prompt,
        outs=[flat, pl.BlockSpec((None, rows, 3 * HEAD_DIM), lambda m, h, _: (m, 0, h)), half, half],
        shapes=[array((micro * rows, heads * HEAD_DIM)), array((micro, rows, heads * 3 * HEAD_DIM))]
        + [array((blocks // 2, 2, micro, heads, own, HEAD_DIM))] * 2,
        scratch=[pltpu.VMEM((shared + tail, HEAD_DIM), f32)] * 2,
        name="attention",
    )


def fold_kernel(a_ref, b_ref, keep_ref, send_ref):
    for i, ref in enumerate((keep_ref, send_ref)):
        ref[0] = (a_ref[i].astype(f32) + b_ref[i].astype(f32)).astype(bf16)


def fold(chain, kept, got):
    slots, shape = kept.shape[0], kept.shape[1:]
    count = kept.size // (slots * HEAD_DIM)
    one = pl.BlockSpec((1, count, HEAD_DIM), lambda i: (i, 0, 0))
    two = pl.BlockSpec((2, count, HEAD_DIM), lambda i: (i, 0, 0))
    keep, send = chain.run(
        fold_kernel,
        (kept.reshape(slots, count, HEAD_DIM), got.reshape(slots, count, HEAD_DIM)),
        grid=(slots // 2,),
        ins=[two, two],
        outs=[one, one],
        shapes=[array((slots // 2, count, HEAD_DIM))] * 2,
        name="fold",
    )
    return keep.reshape((slots // 2,) + shape), send.reshape((slots // 2,) + shape)


def slot_of(j, me, part, low, size):
    return pl.ds(pl.multiple_of(lax.bitwise_xor(jnp.int32(j), me) * part + low, LANES), size)


def context_kernel(g_ref, w_ref, o_ref):
    o_ref[...] = dot(g_ref[...], w_ref[...]).astype(bf16)


def grad_context_of(chain, g, packed, wide):
    count, width = g.shape
    tile = count // 4
    at = packed.shape[1] // wide - 1
    return chain.run(
        context_kernel,
        (g, packed),
        grid=(count // tile,),
        ins=[pl.BlockSpec((tile, width), lambda i: (i, 0)), pl.BlockSpec((width, wide), lambda i: (0, at))],
        outs=[pl.BlockSpec((tile, wide), lambda i: (i, 0))],
        shapes=[array((count, wide))],
        name="grad_context",
    )[0]


def forward_kernel(spots, part, me_ref, n_ref, bias_ref, *refs):
    ups, (act_ref, slope_ref, up_ref) = refs[: len(spots)], refs[len(spots) :]
    me = me_ref[0]

    @pl.when(pl.program_id(1) == 0)
    def _():
        for (r, low), ref in zip(spots, ups):
            up_ref[slot_of(r, me, part, low, ref.shape[0]), :] = ref[...]

    h = dot(n_ref[...], up_ref[...]) + bias_ref[...]
    z = jnp.abs(h)
    e = jnp.exp(-0.5 * (h * h))
    t = 1.0 / (1.0 + TAIL_P * z)
    q = jnp.full_like(t, TAIL[0])
    for co in TAIL[1:]:
        q = q * t + co
    low = e * (t * q)
    cdf = jnp.where(h >= 0.0, 1.0 - low, low)
    act_ref[...] = (h * cdf).astype(bf16)
    slope_ref[...] = (cdf + h * (e * PEAK)).astype(bf16)


def spots_of(slots):
    spots, pieces = [], []
    for r, slot in enumerate(slots):
        low = 0
        for piece in slot:
            spots.append((r, low))
            pieces.append(piece)
            low += piece.shape[0]
    return spots, pieces


def ff_forward(chain, me, norm_two, ups, bias, rows):
    count, width = norm_two.shape
    spots, pieces = spots_of(ups)
    part, hidden = ups[0][0].shape
    cols = min(512, hidden)
    out = pl.BlockSpec((rows, cols), lambda c, r, _: (r, c))
    return chain.run(
        functools.partial(forward_kernel, spots, part),
        (me, norm_two, bias, *pieces),
        scalars=1,
        grid=(hidden // cols, count // rows),
        ins=[
            pl.BlockSpec((rows, width), lambda c, r, _: (r, 0)),
            pl.BlockSpec((1, cols), lambda c, r, _: (0, c)),
        ]
        + [pl.BlockSpec((p.shape[0], cols), lambda c, r, _: (0, c)) for p in pieces],
        outs=[out, out],
        shapes=[array((count, hidden))] * 2,
        scratch=[pltpu.VMEM((width, cols), bf16)],
        name="ff_forward",
    )


def stack_kernel(spots, *refs):
    o_ref = refs[-1]
    for (r, low), ref in zip(spots, refs):
        o_ref[r, low : low + ref.shape[0], :] = ref[...]


def stack(chain, slots):
    spots, pieces = spots_of(slots)
    part, hidden = slots[0][0].shape
    cols = min(512, hidden)
    return chain.run(
        functools.partial(stack_kernel, spots),
        tuple(pieces),
        grid=(hidden // cols,),
        ins=[pl.BlockSpec((p.shape[0], cols), lambda c: (0, c)) for p in pieces],
        outs=[pl.BlockSpec((len(slots), part, cols), lambda c: (0, 0, c))],
        shapes=[array((len(slots), part, hidden))],
        name="stack",
    )[0]


def backward_kernel(g_ref, down_ref, slope_ref, grad_ref, rows_ref):
    blocks, _, part = down_ref.shape

    @pl.when(pl.program_id(1) == 0)
    def _():
        for j in range(blocks):
            rows_ref[:, j * part : (j + 1) * part] = down_ref[j]

    ga = dot(g_ref[...], rows_ref[...], NT)
    grad_ref[...] = (ga * slope_ref[...].astype(f32)).astype(bf16)


def ff_backward(chain, g, down, slope, rows):
    count, width = g.shape
    blocks, hidden, part = down.shape
    cols = min(1024, hidden)
    out = pl.BlockSpec((rows, cols), lambda c, r: (r, c))
    return chain.run(
        backward_kernel,
        (g, down, slope),
        grid=(hidden // cols, count // rows),
        ins=[
            pl.BlockSpec((rows, width), lambda c, r: (r, 0)),
            pl.BlockSpec((blocks, cols, part), lambda c, r: (0, c, 0)),
            out,
        ],
        outs=[out],
        shapes=[array((count, hidden))],
        scratch=[pltpu.VMEM((cols, width), bf16)],
        name="ff_backward",
    )[0]


def mix_kernel(act_ref, ctx_ref, down_ref, dense_ref, *o_refs):
    total = dot(act_ref[...], down_ref[...])
    total += dot(ctx_ref[...], dense_ref[...], NT)
    size = total.shape[0] // len(o_refs)
    for i, ref in enumerate(o_refs):
        ref[...] = total[i * size : (i + 1) * size].astype(bf16)


def mix(chain, act, context, down, packed, rows, index, pieces):
    hidden = act.shape[1]
    wide = context.shape[1]
    blocks, _, part = down.shape
    size = rows // pieces
    at = packed.shape[1] // wide - 1
    return chain.run(
        mix_kernel,
        (act, context, down, packed),
        grid=(blocks,),
        ins=[
            pl.BlockSpec((rows, hidden), lambda j: (index, 0)),
            pl.BlockSpec((rows, wide), lambda j: (index, 0)),
            pl.BlockSpec((None, hidden, part), lambda j: (j, 0, 0)),
            pl.BlockSpec((part, wide), lambda j: (j, at)),
        ],
        outs=[pl.BlockSpec((size, part), lambda j: (0, j))] * pieces,
        shapes=[array((size, blocks * part))] * pieces,
        name="mix",
        key="mix%d" % min(index, 1),
    )


def second_grad_kernel(act_ref, ctx_ref, g_ref, o_ref):
    hidden = act_ref.shape[1]
    o_ref[:hidden, :] = dot(act_ref[...], g_ref[...], TN).astype(bf16)
    o_ref[hidden:, :] = dot(ctx_ref[...], g_ref[...], TN).astype(bf16)


def second_grads(chain, act, context, g, blocks):
    count, hidden = act.shape
    wide = context.shape[1]
    part = g.shape[1] // blocks
    return chain.run(
        second_grad_kernel,
        (act, context, g),
        grid=(blocks,),
        ins=[
            pl.BlockSpec((count, hidden), lambda j: (0, 0)),
            pl.BlockSpec((count, wide), lambda j: (0, 0)),
            pl.BlockSpec((count, part), lambda j: (0, j)),
        ],
        outs=[pl.BlockSpec((None, hidden + wide, part), lambda j: (j, 0, 0))],
        shapes=[array((blocks, hidden + wide, part))],
        name="second_grads",
    )[0]


def norm_grad_kernel(me_ref, gj_ref, gh_ref, wj_ref, wu_ref, x_ref, mean_ref, inv_ref, g1_ref, g2_ref, *outs):
    *o_refs, stat_ref, sum_ref = outs

    @pl.when(pl.program_id(0) == 0)
    def _():
        sum_ref[...] = jnp.sum(gj_ref[...].astype(f32), axis=0, keepdims=True)

    one = dot(gj_ref[...], wj_ref[...], NT)
    two = dot(gh_ref[...], wu_ref[...], NT)
    normed = (x_ref[...].astype(f32) - mean_ref[...]) * inv_ref[...]
    total = one * g1_ref[...] + two * g2_ref[...]
    size = total.shape[0] // len(o_refs)
    for i, ref in enumerate(o_refs):
        ref[...] = total[i * size : (i + 1) * size].astype(bf16)
    for i, term in enumerate((one * normed, one, two * normed, two)):
        stat_ref[i : i + 1, :] = jnp.sum(term, axis=0, keepdims=True)


def norm_grads(chain, me, grad_joined, grad_hidden, packed, up, x, mean, inverse, gain_one, gain_two, rows, index, pieces):
    width = x.shape[1]
    wide, hidden = grad_joined.shape[1], grad_hidden.shape[1]
    blocks, part, _ = up.shape
    size = rows // pieces
    column = pl.BlockSpec((rows, 1), lambda c, _: (index, 0))
    gain = pl.BlockSpec((1, part), lambda c, _: (0, c))
    return chain.run(
        norm_grad_kernel,
        (me, grad_joined, grad_hidden, packed, up, x, mean, inverse, gain_one, gain_two),
        scalars=1,
        grid=(blocks,),
        ins=[
            pl.BlockSpec((rows, wide), lambda c, _: (index, 0)),
            pl.BlockSpec((rows, hidden), lambda c, _: (index, 0)),
            pl.BlockSpec((part, wide), lambda c, _: (c, 0)),
            pl.BlockSpec((None, part, hidden), lambda c, me: (lax.bitwise_xor(c, me[0]), 0, 0)),
            pl.BlockSpec((rows, part), lambda c, _: (index, c)),
            column, column, gain, gain,
        ],
        outs=[pl.BlockSpec((size, part), lambda c, _: (0, c))] * pieces
        + [pl.BlockSpec((8, part), lambda c, _: (0, c)), pl.BlockSpec((1, wide), lambda c, _: (0, 0))],
        shapes=[array((size, width))] * pieces + [array((8, width), f32), array((1, wide), f32)],
        name="norm_grads",
        key="norm_grads%d" % min(index, 1),
    )


def prompt_kernel(keep_ref, got_ref, cos_ref, sin_ref, _, o_ref):
    total = keep_ref[...].astype(f32) + got_ref[...].astype(f32)

    @pl.when(pl.program_id(2) == 0)
    def _():
        first = rotated_back(total[:, :LANES], cos_ref[...], sin_ref[...], kernel_roll)
        o_ref[:, :LANES] = first.astype(bf16)
        o_ref[:, LANES:] = total[:, LANES:].astype(bf16)

    @pl.when(pl.program_id(2) == 1)
    def _():
        o_ref[...] = total.astype(bf16)


def put_prompt(chain, grad_joined, kept, got, cosine, signed):
    _, _, micro, heads, own, _ = kept.shape
    part = pl.BlockSpec((None, None, None, None, own, HEAD_DIM), lambda m, h, i: (0, i, m, h, 0, 0))
    table = pl.BlockSpec((None, own, LANES), lambda m, h, i: (m, 0, 0))
    return chain.run(
        prompt_kernel,
        (kept, got, cosine, signed, grad_joined),
        grid=(micro, heads, 2),
        ins=[part, part, table, table, ANY],
        outs=[pl.BlockSpec((None, own, HEAD_DIM), lambda m, h, i: (m, 0, 3 * h + 1 + i))],
        shapes=[array(grad_joined.shape)],
        aliases={4: 0},
        name="put_prompt",
    )[0]


def pair_kernel(a_ref, b_ref, o_ref):
    o_ref[...] = (a_ref[...].astype(f32) + b_ref[...].astype(f32)).astype(bf16)


def add_pair(chain, a, b, low, size):
    width = a.shape[1]
    tile = size // 2
    row = pl.BlockSpec((tile, width), lambda i: (low // tile + i, 0))
    return chain.run(
        pair_kernel,
        (a, b),
        grid=(size // tile,),
        ins=[row, row],
        outs=[pl.BlockSpec((tile, width), lambda i: (i, 0))],
        shapes=[array((size, width))],
        name="add_pair",
    )[0]


def output_kernel(a_ref, b_ref, x_ref, dense_ref, down_ref, o_ref):
    total = a_ref[...].astype(f32) + b_ref[...].astype(f32)
    o_ref[...] = (x_ref[...].astype(f32) + total + dense_ref[...] + down_ref[...]).astype(bf16)


def input_kernel(a_ref, b_ref, x_ref, g_ref, mean_ref, inv_ref, o_ref):
    total = a_ref[...].astype(f32) + b_ref[...].astype(f32)
    inverse = inv_ref[...]
    normed = (x_ref[...].astype(f32) - mean_ref[...]) * inverse
    centred = (
        total
        - jnp.mean(total, axis=-1, keepdims=True)
        - normed * jnp.mean(total * normed, axis=-1, keepdims=True)
    )
    o_ref[...] = (g_ref[...].astype(f32) + inverse * centred).astype(bf16)


def finish(chain, a, b, start, rows, columns=(), vectors=()):
    size, width = a.shape
    tile = size // 2
    at = start // tile
    here = pl.BlockSpec((tile, width), lambda i: (i, 0))
    there = pl.BlockSpec((tile, width), lambda i: (at + i, 0))
    column = pl.BlockSpec((tile, 1), lambda i: (at + i, 0))
    vector = pl.BlockSpec((1, width), lambda i: (0, 0))
    return chain.run(
        input_kernel if columns else output_kernel,
        (a, b, *rows, *columns, *vectors),
        grid=(size // tile,),
        ins=[here, here] + [there] * len(rows) + [column] * len(columns) + [vector] * len(vectors),
        outs=[here],
        shapes=[array((size, width))],
        name="finish",
    )[0]


def swap(value, axis, bit):
    size = lax.axis_size(axis)
    return lax.ppermute(value, axis, [(i, i ^ (1 << bit)) for i in range(size)])


def bits_of(axis):
    return lax.axis_size(axis).bit_length() - 1


def send_xor(value, axis, offset):
    size = lax.axis_size(axis)
    return lax.ppermute(value, axis, [(i, i ^ offset) for i in range(size)])


def join(*values):
    return lax.optimization_barrier(values)


class Gather:
    def __init__(self, value, axis):
        self.axis, self.size = axis, lax.axis_size(axis)
        self.direct = self.size != 8
        offsets = range(2, self.size, 2) if self.direct else (2, 4)
        self.slots = [None] * self.size
        self.slots[0] = [value]
        self.slots[1] = [send_xor(value, axis, 1)]
        for r in offsets:
            self.slots[r] = [send_xor(value, axis, r)]

    def first(self, *others):
        here = [r for r in range(self.size) if r and self.slots[r]]
        values = join(*[self.slots[r][0] for r in here], *others)
        for r, value in zip(here, values):
            self.slots[r] = [value]
        self.fresh = []
        if not self.direct:
            near, far = self.slots[2][0], self.slots[4][0]
            half = near.shape[0] // 2
            self.fresh = [send_xor(near[:half], self.axis, 4), send_xor(far[half:], self.axis, 2)]
        self.twins = [r for r in here if r > 1]
        self.fresh += [send_xor(self.slots[r][0], self.axis, 1) for r in self.twins]
        return values[len(here) :]

    def second(self, *others):
        values = join(*self.fresh, *others)
        if not self.direct:
            self.slots[6] = list(values[:2])
            self.slots[7] = [send_xor(piece, self.axis, 1) for piece in self.slots[6]]
        for r, value in zip(self.twins, values[len(self.fresh) - len(self.twins) :]):
            self.slots[r + 1] = [value]
        return values[len(self.fresh) :]


def gather_ordered(value, axis):
    index = lax.axis_index(axis)
    held = value[None]
    for bit in range(bits_of(axis)):
        other = swap(held, axis, bit)
        low = ((index >> bit) & 1) == 0
        held = jnp.concatenate([jnp.where(low, held, other), jnp.where(low, other, held)], 0)
    return held


def add_up(value, axis):
    for bit in range(bits_of(axis)):
        value = value + swap(value, axis, bit)
    return value


def own_rows(value, start, count):
    return lax.dynamic_slice_in_dim(value, start, count, 0)


def sum_rows(partial, axis):
    index = lax.axis_index(axis)
    held, start = partial, jnp.int32(0)
    for bit in range(bits_of(axis)):
        mine = (index >> bit) & 1
        half = held.shape[0] // 2
        other = swap(own_rows(held, (1 - mine) * half, half).astype(bf16), axis, bit)
        held = own_rows(held, mine * half, half).astype(f32) + other.astype(f32)
        start = start + mine * half
    return held, start


def spread_rows(share, axis):
    index = lax.axis_index(axis)
    held = share
    for bit in reversed(range(bits_of(axis))):
        mine = (index >> bit) & 1
        other = swap(held, axis, bit)
        held = jnp.where(
            mine == 0, jnp.concatenate([held, other], 0), jnp.concatenate([other, held], 0)
        )
    return held


TO_MIDDLE = [(0, 1), (3, 2)]
ACROSS = [(1, 2), (2, 1)]
TO_ENDS = [(1, 0), (2, 3)]


class Piece:
    def __init__(self, chain, partial, first, low, size, axis, closing):
        self.chain, self.axis, self.closing = chain, axis, closing
        self.partial, self.first, self.low, self.size = partial, first, low, size

    def cross(self):
        self.pair = add_pair(self.chain, self.partial, self.first, self.low, self.size)
        self.second = lax.ppermute(self.pair, self.axis, ACROSS)

    def close(self):
        self.own = self.closing(self.pair, self.second)
        self.third = lax.ppermute(self.own, self.axis, TO_ENDS)


def local(
    tokens,
    cont_lengths,
    first_gain,
    first_bias,
    second_gain,
    second_bias,
    joined_weight,
    joined_bias,
    dense_weight,
    dense_bias,
    up_weight,
    up_bias,
    down_weight,
    down_bias,
    cotangent,
):
    blocks, ranks = lax.axis_size("dp"), lax.axis_size("tensor")
    me = lax.axis_index("dp").astype(jnp.int32)
    micro, _, rows, width = tokens.shape
    count = micro * rows
    own = PROMPT // blocks
    tail = rows - own
    part = width // blocks
    heads = joined_weight.shape[1] // (3 * HEAD_DIM)
    wide = heads * HEAD_DIM
    hidden = up_weight.shape[1]
    x = tokens.reshape(count, width)
    g = cotangent.reshape(count, width)
    here = me.reshape(1)

    chain = Chain()
    packed, first_gain = join(pack(chain, joined_weight, dense_weight), first_gain)
    packed = lax.all_gather(packed, "dp", axis=0, tiled=True)
    down = lax.all_gather(down_weight, "dp", axis=0, tiled=False)

    vectors = (first_gain, first_bias, second_gain, second_bias, dense_bias, down_bias)
    small = jnp.concatenate([v.reshape(-1) for v in vectors + (joined_bias, up_bias)])
    small = gather_ordered(small, "dp")
    up_here, small = join(up_weight, small)
    ups = Gather(up_here, "dp")

    small = small.astype(f32)
    full = [small[:, i * part : (i + 1) * part].reshape(1, width) for i in range(6)]
    gain_one, bias_one, gain_two, bias_two, dense_add, down_add = full

    def by_head(start, like):
        piece = small[:, start : start + like.size].reshape((blocks,) + like.shape)
        return jnp.transpose(piece, (1, 0, 2)).reshape(1, -1)

    joined_add = by_head(6 * part, joined_bias)
    up_add = by_head(6 * part + joined_bias.size, up_bias)

    seg_ends = jnp.cumsum(cont_lengths[:, 0], axis=1)
    slots = jnp.arange(tail, dtype=jnp.int32)
    passed = (slots[None, :, None] >= seg_ends[:, None, :]).astype(jnp.int32)
    first = jnp.sum(passed * cont_lengths[:, 0][:, None, :], axis=2)
    prompt_pos = jnp.broadcast_to(me * own + jnp.arange(own, dtype=jnp.int32), (micro, own))
    positions = jnp.concatenate([prompt_pos, PROMPT + slots[None] - first], axis=1)
    cosine, signed = rope_tables(positions)

    norm_one, norm_two, mean, inverse, upstream_sum = norms(chain, x, g, gain_one, bias_one, gain_two, bias_two)
    norm_one, cosine, signed, packed = ups.first(norm_one, cosine, signed, packed)

    q, k, v, prompt = qkv(chain, norm_one.reshape(micro, rows, width), packed, joined_add, cosine, signed, own)
    (prompt,) = ups.second(prompt)
    prompts = Gather(prompt, "dp")
    act, slope = ff_forward(chain, here, norm_two, ups.slots, up_add, rows)
    (slope,) = prompts.first(slope)
    grad_context = grad_context_of(chain, g, packed, wide)
    (grad_context,) = prompts.second(grad_context)
    prompts, ups = prompts.slots, ups.slots

    line = ranks == 4
    pieces = 2
    size = rows // pieces
    context, grad_joined, kept, sent = attention(
        chain, here, q, k, v, prompts, grad_context, first[..., None], cosine, signed
    )
    got = send_xor(sent, "dp", 1)

    def close_output(start):
        return lambda a, b: finish(chain, a, b, start, (x,), vectors=(dense_add, down_add))

    def close_input(start):
        return lambda a, b: finish(chain, a, b, start, (x, g), columns=(mean, inverse))

    rank = lax.axis_index("tensor")
    end = ((rank == 0) | (rank == 3)).astype(jnp.int32).reshape(1)
    have = {"kept": kept, "got": got, "bit": 1, "joined": grad_joined, "stats": [], "joined_sums": [], "results": [None, None]}
    partials, sums = [None] * (2 * micro), []

    def along_rows(value, like):
        lead, span = like.shape
        value = jnp.transpose(value.reshape(lead, blocks, span), (1, 0, 2)).reshape(blocks, lead * span)
        return jnp.pad(value, ((0, 0), (0, part - lead * span))).reshape(1, width)

    def sums_of_all():
        stats = functools.reduce(jnp.add, have["stats"])
        joined_sums = functools.reduce(jnp.add, have["joined_sums"])
        rows_of = [stats, upstream_sum, along_rows(have["up_sums"], up_bias), along_rows(joined_sums, joined_bias)]
        return jnp.concatenate(rows_of + [jnp.zeros((1, width), f32)], 0)

    def scattered(value):
        return lax.psum_scatter(value, "dp", scatter_dimension=0, tiled=value.ndim == 2)

    def step(what, *which):
        if what == "mix":
            partials[which[0]] = mix(chain, act, context, down, packed, rows, which[0], 1 if which[0] in MERGED else pieces)
        elif what == "go":
            stage, i, *behind = which
            partial, start = partials[stage][i], (stage % micro) * rows + i * size
            if line:
                if behind:
                    piece = sums[behind[0]]
                    partial, piece.pair = join(partial, piece.pair)
                got = lax.ppermute(partial, "tensor", TO_MIDDLE)
                for low in range(0, partial.shape[0], size):
                    closing = (close_output, close_input)[stage // micro](start + low)
                    sums.append(Piece(chain, partial, got, low, size, "tensor", closing))
        elif what == "fold":
            for _ in range(1 if line or have["bit"] == 1 else bits_of("dp") - 2):
                kept, sent = fold(chain, have["kept"], have["got"])
                have["kept"], have["got"] = kept, send_xor(sent, "dp", 1 << have["bit"])
                have["bit"] += 1
        elif what == "ffb":
            have["hidden"] = ff_backward(chain, g, down, slope, rows)
        elif what == "up":
            have["up"], have["up_sums"] = outer(chain, norm_two, have["hidden"], "outer0")
        elif what == "stack":
            have["ups"] = stack(chain, ups)
        elif what == "second":
            have["second"] = second_grads(chain, act, context, g, blocks)
        elif what == "joined":
            have["joined_grad"] = outer_more(chain, norm_one, have["joined"], sums_of_all(), "outer1")
        elif what == "send":
            if line and len(which) > 1:
                piece = sums[which[1]]
                piece.pair, have[which[0]] = join(piece.pair, have[which[0]])
            have[which[0]] = scattered(have[which[0]])
        elif what == "prompt":
            put = put_prompt(chain, have["joined"], have["kept"], have["got"], cosine, signed)
            have["joined"] = put.reshape(count, 3 * wide)
        elif what == "norm":
            m = which[0]
            *parts, stat, joined_sums = norm_grads(
                chain, here, have["joined"], have["hidden"], packed, have["ups"], x, mean, inverse, gain_one, gain_two,
                rows, m, 1 if micro + m in MERGED else pieces,
            )
            partials[micro + m] = parts
            have["stats"].append(stat[:4])
            have["joined_sums"].append(joined_sums)
        elif not line:
            pass
        elif what == "cross":
            sums[which[0]].cross()
        elif what == "close":
            k = which[0]
            if 1 <= k < BACK:
                sums[k].pair, sums[k - 1].third = join(sums[k].pair, sums[k - 1].third)
            sums[k].close()
            if k == END_TIE:
                sums[k].own, have["joined_grad"] = join(sums[k].own, have["joined_grad"])
        elif what == "place":
            low, high = which
            kind = low // (2 * pieces)
            have["results"][kind] = place(chain, have["results"][kind], end, sums[low:high], low * size % count, count)
        elif what == "tie":
            piece = sums[which[1]]
            piece.pair, have[which[0]] = join(piece.pair, have[which[0]])

    for one in PLAN:
        step(*one)
    up_out, second_out, joined_out = have["up"], have["second"], have["joined_grad"]
    joined_out = joined_out.astype(f32)
    vector = joined_out[:, 3 * wide : 3 * wide + 8].T
    joined_out = joined_out[:, : 3 * wide]
    gains = vector[:4]
    if line:
        have["results"][1], gains = join(have["results"][1], gains)
        output, input_grad = [r.reshape(micro, rows, width) for r in have["results"]]
    gains = add_up(gains, "tensor")
    if not line:
        outputs, inputs = [], []
        for m in range(micro):
            share, start = sum_rows(jnp.concatenate(partials[m]), "tensor")
            span = share.shape[0]
            mine = own_rows(x, m * rows + start, span).astype(f32)
            outputs.append(spread_rows((mine + share + dense_add + down_add).astype(bf16), "tensor"))
            share, start = sum_rows(jnp.concatenate(partials[micro + m]), "tensor")
            start = m * rows + start
            row_inverse = own_rows(inverse, start, span)
            row_normed = (own_rows(x, start, span).astype(f32) - own_rows(mean, start, span)) * row_inverse
            centred = (
                share
                - jnp.mean(share, axis=-1, keepdims=True)
                - row_normed * jnp.mean(share * row_normed, axis=-1, keepdims=True)
            )
            result = own_rows(g, start, span).astype(f32) + row_inverse * centred
            inputs.append(spread_rows(result.astype(bf16), "tensor"))
        output, input_grad = jnp.stack(outputs), jnp.stack(inputs)

    return (
        output[:, None],
        input_grad[:, None],
        gains[0],
        gains[1],
        gains[2],
        gains[3],
        joined_out,
        vector[6, : joined_bias.size].reshape(joined_bias.shape),
        second_out[hidden:].astype(f32),
        vector[4],
        up_out.astype(f32),
        vector[5, : up_bias.size].reshape(up_bias.shape),
        second_out[:hidden].astype(f32),
        vector[4],
    )


def solution(mesh):
    placed = (
        P(None, "dp", None, None),
        P(None, "dp", None),
        P("dp"),
        P("dp"),
        P("dp"),
        P("dp"),
        P("dp", "tensor"),
        P("tensor", "dp"),
        P("tensor", "dp"),
        P("dp"),
        P("dp", "tensor"),
        P("tensor", "dp"),
        P("tensor", "dp"),
        P("dp"),
        P(None, "dp", None, None),
    )
    return jax.shard_map(
        local,
        mesh=mesh,
        in_specs=placed,
        out_specs=(
            P(None, "dp", None, None),
            P(None, "dp", None, None),
            P("dp"),
            P("dp"),
            P("dp"),
            P("dp"),
            P("dp", "tensor"),
            P("tensor", "dp"),
            P("tensor", "dp"),
            P("dp"),
            P("dp", "tensor"),
            P("tensor", "dp"),
            P("tensor", "dp"),
            P("dp"),
        ),
        check_vma=False,
    )
```

```python
import functools

import jax
import jax.numpy as jnp
from jax import lax
from jax.experimental import pallas as pl
from jax.experimental.pallas import tpu as pltpu
from jax.sharding import PartitionSpec as P

HEAD_DIM = 256
ROT_DIMS = 64
PROMPT = 1024
LONGEST = 128

norm_eps = 1e-05
rope_base = 10000.0
masked_score = -1e30
scale = HEAD_DIM**-0.5
LANES = 128
VMEM = 60 << 20

f32, bf16 = jnp.float32, jnp.bfloat16
NN = (((1,), (0,)), ((), ()))
NT = (((1,), (1,)), ((), ()))
TN = (((0,), (0,)), ((), ()))

TAIL_P = 0.32
TAIL = (
    -0.02115197293220867,
    0.09575628590143809,
    -0.14740109756488956,
    0.06607995422323057,
    -0.0098602948578973,
    0.058840354546090344,
    0.08778712629904878,
    0.11462742044446793,
    0.12766067496581068,
    0.12766153278717104,
)
PEAK = 0.3989422804014327


def dot(a, b, dims=NN):
    return lax.dot_general(a, b, dims, preferred_element_type=f32)


TIMES = {
    "pack": 2.3,
    "norms": 12.4,
    "qkv": 14.0,
    "grad_context": 7.0,
    "ff_forward": 28.0,
    "attention": 25.0,
    "mix0": 13.0,
    "mix1": 13.0,
    "second_grads": 20.0,
    "fold": 3.5,
    "add_pair": 3.0,
    "finish": 40.0,
    "ff_backward": 18.5,
    "put_prompt": 5.4,
    "norm_grads0": 16.0,
    "norm_grads1": 16.0,
    "stack": 8.0,
    "outer0": 17.0,
    "outer1": 13.0,
    "place": 4.5,
}
FLOPS = 1.15e9
SHARE = 2.0
BACK = 5
END_TIE = 7
PLAN = (('mix', 0), ('go', 0, 0), ('go', 0, 1), ('mix', 1), ('fold',), ('ffb',), ('cross', 0), ('go', 1, 0, 0), ('up',), ('cross', 1), ('go', 1, 1, 1), ('send', 'up', 1), ('stack',), ('fold',), ('close', 0), ('second',), ('cross', 2), ('send', 'second', 2), ('close', 1), ('prompt',), ('norm', 0), ('go', 2, 0, 2), ('cross', 3), ('go', 2, 1, 3), ('close', 2), ('place', 0, 2), ('norm', 1), ('go', 3, 0, 3), ('cross', 4), ('go', 3, 1, 4), ('close', 3), ('joined',), ('cross', 5), ('send', 'joined_grad', 5), ('close', 4), ('place', 2, 4), ('cross', 6), ('close', 5), ('cross', 7), ('close', 6), ('place', 4, 6), ('tie', 'up', 7), ('tie', 'second', 7), ('close', 7), ('gains',), ('place', 6, 7), ('place', 7, 8))
MERGED = ()


def cost(name):
    return pl.CostEstimate(flops=int(TIMES[name] * FLOPS * SHARE), bytes_accessed=0, transcendentals=0)


ANY = pl.BlockSpec(memory_space=pl.ANY)


class Chain:
    def __init__(self):
        self.last = ()

    def run(self, kernel, args, *, grid, ins, outs, shapes, name, key=None, scalars=0, scratch=(), aliases=None):
        count, extra = len(args), tuple(e for e in self.last if all(e is not a for a in args))

        def body(*refs):
            kernel(*refs[:count], *refs[count + len(extra) :])

        results = pl.pallas_call(
            body,
            grid_spec=pltpu.PrefetchScalarGridSpec(
                num_scalar_prefetch=scalars,
                grid=grid,
                in_specs=list(ins) + [ANY] * len(extra),
                out_specs=outs,
                scratch_shapes=list(scratch),
            ),
            out_shape=shapes,
            input_output_aliases=aliases or {},
            compiler_params=pltpu.CompilerParams(vmem_limit_bytes=VMEM),
            cost_estimate=cost(key or name),
            name=name,
        )(*args, *extra)
        self.last = (results[0],)
        return results


def array(shape, dtype=bf16):
    return jax.ShapeDtypeStruct(tuple(shape), dtype)


def rope_tables(positions):
    half = ROT_DIMS // 2
    inverse = rope_base ** (-(2.0 * jnp.arange(half, dtype=f32)) / ROT_DIMS)
    angles = positions.astype(f32)[..., None] * inverse
    ones = jnp.ones(positions.shape + (LANES - ROT_DIMS,), f32)
    c, s = jnp.cos(angles), jnp.sin(angles)
    return jnp.concatenate([c, c, ones], -1), jnp.concatenate([-s, s, ones * 0.0], -1)


def swap_halves(u, roll):
    half = ROT_DIMS // 2
    lane = lax.broadcasted_iota(jnp.int32, u.shape, u.ndim - 1)
    up, down = roll(u, LANES - half), roll(u, half)
    return jnp.where(lane < half, up, jnp.where(lane < ROT_DIMS, down, 0.0))


def rotated(u, cosine, signed, roll):
    return u * cosine + swap_halves(u, roll) * signed


def rotated_back(y, cosine, signed, roll):
    return y * cosine + swap_halves(y * signed, roll)


def kernel_roll(u, by):
    return pltpu.roll(u, by, u.ndim - 1)


def plain_roll(u, by):
    return jnp.roll(u, by, -1)


def norm_kernel(x_ref, g_ref, g1_ref, b1_ref, g2_ref, b2_ref, n1_ref, n2_ref, mean_ref, inv_ref, sum_ref):
    x = x_ref[...].astype(f32)
    mean = jnp.mean(x, axis=-1, keepdims=True)
    centered = x - mean
    inverse = lax.rsqrt(jnp.mean(centered * centered, axis=-1, keepdims=True) + norm_eps)
    normed = centered * inverse
    n1_ref[...] = (normed * g1_ref[...] + b1_ref[...]).astype(bf16)
    n2_ref[...] = (normed * g2_ref[...] + b2_ref[...]).astype(bf16)
    mean_ref[...] = mean
    inv_ref[...] = inverse

    @pl.when(pl.program_id(0) == 0)
    def _():
        sum_ref[...] = jnp.zeros_like(sum_ref)

    sum_ref[...] += jnp.sum(g_ref[...].astype(f32), axis=0, keepdims=True)


def norms(chain, x, g, gain_one, bias_one, gain_two, bias_two):
    count, width = x.shape
    tile = count // 8
    row = pl.BlockSpec((tile, width), lambda i: (i, 0))
    vector = pl.BlockSpec((1, width), lambda i: (0, 0))
    column = pl.BlockSpec((tile, 1), lambda i: (i, 0))
    return chain.run(
        norm_kernel,
        (x, g, gain_one, bias_one, gain_two, bias_two),
        grid=(count // tile,),
        ins=[row, row] + [vector] * 4,
        outs=[row, row, column, column, vector],
        shapes=[array((count, width))] * 2 + [array((count, 1), f32)] * 2 + [array((1, width), f32)],
        name="norms",
    )


def outer_kernel(a_ref, b_ref, o_ref, sum_ref):
    o_ref[...] = dot(a_ref[...], b_ref[...], TN).astype(bf16)

    @pl.when(pl.program_id(0) == 0)
    def _():
        sum_ref[...] = jnp.sum(b_ref[...].astype(f32), axis=0, keepdims=True)


def outer(chain, a, b, key):
    count, width = a.shape
    cols = b.shape[1]
    tile = width // 4
    return chain.run(
        outer_kernel,
        (a, b),
        grid=(4,),
        ins=[pl.BlockSpec((count, tile), lambda i: (0, i)), pl.BlockSpec((count, cols), lambda i: (0, 0))],
        outs=[pl.BlockSpec((tile, cols), lambda i: (i, 0)), pl.BlockSpec((1, cols), lambda i: (0, 0))],
        shapes=[array((width, cols)), array((1, cols), f32)],
        name="outer",
        key=key,
    )


def outer_more_kernel(a_ref, b_ref, more_ref, o_ref):
    cols = b_ref.shape[1]
    o_ref[:, :cols] = dot(a_ref[...], b_ref[...], TN).astype(bf16)
    o_ref[:, cols:] = jnp.zeros((o_ref.shape[0], LANES), bf16)
    o_ref[:, cols : cols + more_ref.shape[0]] = more_ref[...].T.astype(bf16)


def outer_more(chain, a, b, more, key):
    count, width = a.shape
    cols = b.shape[1]
    tile = width // 4
    return chain.run(
        outer_more_kernel,
        (a, b, more),
        grid=(4,),
        ins=[
            pl.BlockSpec((count, tile), lambda i: (0, i)),
            pl.BlockSpec((count, cols), lambda i: (0, 0)),
            pl.BlockSpec((more.shape[0], tile), lambda i: (0, i)),
        ],
        outs=[pl.BlockSpec((tile, cols + LANES), lambda i: (i, 0))],
        shapes=[array((width, cols + LANES))],
        name="outer",
        key=key,
    )[0]


def place_kernel(flag_ref, *refs):
    o_ref = refs[-1]
    pieces = len(refs) // 2 if len(refs) % 2 else len(refs) // 2 - 1
    for i in range(pieces):
        for flag in (0, 1):

            @pl.when((flag_ref[0] == flag) & (pl.program_id(0) // 2 == i))
            def _():
                o_ref[...] = refs[2 * i + flag][...]


def place(chain, held, flag, pieces, start, total):
    size, width = pieces[0].own.shape
    tile = size // 2
    keep = () if held is None else (held,)
    ins, args = [], []
    for i, piece in enumerate(pieces):
        args += [piece.own, piece.third]
        ins += [
            pl.BlockSpec((tile, width), lambda j, flag, i=i: (jnp.clip(j - 2 * i, 0, 1) * (1 - flag[0]), 0)),
            pl.BlockSpec((tile, width), lambda j, flag, i=i: (jnp.clip(j - 2 * i, 0, 1) * flag[0], 0)),
        ]
    return chain.run(
        place_kernel,
        (flag, *args) + keep,
        scalars=1,
        grid=(2 * len(pieces),),
        ins=ins + [ANY] * len(keep),
        outs=[pl.BlockSpec((tile, width), lambda j, _: (start // tile + j, 0))],
        shapes=[array((total, width))],
        aliases={1 + len(args): 0} if keep else {},
        name="place",
    )[0]


def pack_kernel(joined_ref, dense_ref, o_ref):
    wide = joined_ref.shape[1]
    o_ref[:, :wide] = joined_ref[...]
    o_ref[:, wide:] = dense_ref[...].T


def pack(chain, joined, dense):
    part, wide = joined.shape
    total = wide + dense.shape[0]

    def whole(rows, columns):
        return pl.BlockSpec((rows, columns), lambda i: (0, 0))

    return chain.run(
        pack_kernel,
        (joined, dense),
        grid=(1,),
        ins=[whole(*joined.shape), whole(*dense.shape)],
        outs=[whole(part, total)],
        shapes=[array((part, total))],
        name="pack",
    )[0]


def qkv_kernel(x_ref, w_ref, bias_ref, cos_ref, sin_ref, q_ref, k_ref, v_ref, prompt_ref):
    joined = dot(x_ref[...], w_ref[...]) + bias_ref[...]
    c, s = cos_ref[...], sin_ref[...]
    for part, ref in ((0, q_ref), (1, k_ref)):
        base = part * HEAD_DIM
        head = joined[:, base : base + HEAD_DIM]
        ref[:, :LANES] = rotated(head[:, :LANES], c, s, kernel_roll).astype(bf16)
        ref[:, LANES:] = head[:, LANES:].astype(bf16)
    v_ref[...] = joined[:, 2 * HEAD_DIM :].astype(bf16)
    own = prompt_ref.shape[1]
    prompt_ref[0] = k_ref[:own, :]
    prompt_ref[1] = v_ref[:own, :]


def qkv(chain, norm_one, weight, bias, cosine, signed, own):
    micro, rows, width = norm_one.shape
    wide = 3 * HEAD_DIM
    heads = bias.shape[1] // wide
    head = pl.BlockSpec((None, None, rows, HEAD_DIM), lambda h, m: (m, h, 0, 0))
    table = pl.BlockSpec((None, rows, LANES), lambda h, m: (m, 0, 0))
    return chain.run(
        qkv_kernel,
        (norm_one, weight, bias, cosine, signed),
        grid=(heads, micro),
        ins=[
            pl.BlockSpec((None, rows, width), lambda h, m: (m, 0, 0)),
            pl.BlockSpec((width, wide), lambda h, m: (0, h)),
            pl.BlockSpec((1, wide), lambda h, m: (0, h)),
            table,
            table,
        ],
        outs=[head] * 3 + [pl.BlockSpec((2, None, None, own, HEAD_DIM), lambda h, m: (0, m, h, 0, 0))],
        shapes=[array((micro, heads, rows, HEAD_DIM))] * 3 + [array((2, micro, heads, own, HEAD_DIM))],
        name="qkv",
    )


def attention_kernel(layout, me_ref, q_ref, k_ref, v_ref, up_ref, first_ref, cos_ref, sin_ref, *refs):
    ctx_ref, grad_ref, keep_ref, send_ref, dk_acc, dv_acc = refs[-6:]
    blocks, own = len(layout), refs[0].shape[1]
    rows = q_ref.shape[0]
    tail = rows - own
    shared = blocks * own
    me = me_ref[0]
    pk = jnp.concatenate([refs[spots[0]][0] for spots in layout], 0)
    pv = jnp.concatenate([refs[spots[-1]][refs[spots[-1]].shape[0] - 1] for spots in layout], 0)
    ck, cv = k_ref[own:, :], v_ref[own:, :]
    dk_acc[...] = jnp.zeros_like(dk_acc)
    dv_acc[...] = jnp.zeros_like(dv_acc)

    def chunk(start, count, low, high):
        here = slice(start, start + count)
        q, up = q_ref[here, :], up_ref[here, :]
        sp = dot(q, pk, NT) * scale
        parts = []
        if high > low:
            wk, wv = ck[low:high], cv[low:high]
            sw = dot(q, wk, NT) * scale
            key = lax.broadcasted_iota(jnp.int32, sw.shape, 1) + low
            slot = lax.broadcasted_iota(jnp.int32, sw.shape, 0) + (start - own)
            first = first_ref[start - own : start - own + count, :]
            sw = jnp.where((key >= first) & (key <= slot), sw, masked_score)
            parts = [(sp, pk, pv, 0), (sw, wk, wv, shared + low)]
        else:
            spot = lax.broadcasted_iota(jnp.int32, sp.shape, 1)
            key = lax.bitwise_xor(spot // own, me) * own + spot % own
            slot = lax.broadcasted_iota(jnp.int32, sp.shape, 0) + (me * own + start)
            parts = [(jnp.where(key <= slot, sp, masked_score), pk, pv, 0)]
        highest = functools.reduce(jnp.maximum, [jnp.max(s, -1, keepdims=True) for s, *_ in parts])
        raised = [jnp.exp(s - highest) for s, *_ in parts]
        total = functools.reduce(jnp.add, [jnp.sum(r, -1, keepdims=True) for r in raised])
        inverse = 1.0 / total
        probs = [r * inverse for r in raised]
        lows = [p.astype(bf16) for p in probs]
        ctx = functools.reduce(jnp.add, [dot(p, v) for p, (_, _, v, _) in zip(lows, parts)])
        ctx_ref[here, :] = ctx.astype(bf16)
        dps = [dot(up, v, NT) for _, _, v, _ in parts]
        delta = functools.reduce(
            jnp.add, [jnp.sum(p * d, -1, keepdims=True) for p, d in zip(probs, dps)]
        )
        dss = [(p * (d - delta)).astype(bf16) for p, d in zip(probs, dps)]
        dq = functools.reduce(jnp.add, [dot(d, k) for d, (_, k, _, _) in zip(dss, parts)]) * scale
        c, s = cos_ref[here, :], sin_ref[here, :]
        grad_ref[here, :LANES] = rotated_back(dq[:, :LANES], c, s, kernel_roll).astype(bf16)
        grad_ref[here, LANES:HEAD_DIM] = dq[:, LANES:].astype(bf16)
        for p, d, (_, k, _, base) in zip(lows, dss, parts):
            there = slice(base, base + k.shape[0])
            dv_acc[there, :] += dot(p, up, TN)
            dk_acc[there, :] += dot(d, q, TN)

    chunk(0, own, 0, 0)
    step = 4 * LONGEST
    for at in range(0, tail, step):
        size = min(step, tail - at)
        chunk(own + at, size, max(0, at - LONGEST), at + size)

    for r in range(blocks):
        ref, there = (keep_ref, send_ref)[r % 2], slice(r * own, (r + 1) * own)
        ref[r // 2, 0] = (dk_acc[there, :] * scale).astype(bf16)
        ref[r // 2, 1] = dv_acc[there, :].astype(bf16)
    dk = dk_acc[shared:, :] * scale
    c, s = cos_ref[own:, :], sin_ref[own:, :]
    grad_ref[:own, HEAD_DIM:] = jnp.zeros((own, 2 * HEAD_DIM), bf16)
    grad_ref[own:, HEAD_DIM : HEAD_DIM + LANES] = rotated_back(
        dk[:, :LANES], c, s, kernel_roll
    ).astype(bf16)
    grad_ref[own:, HEAD_DIM + LANES : 2 * HEAD_DIM] = dk[:, LANES:].astype(bf16)
    grad_ref[own:, 2 * HEAD_DIM :] = dv_acc[shared:, :].astype(bf16)


def attention(chain, me, q, k, v, prompts, grad_context, first, cosine, signed):
    micro, heads, rows, _ = q.shape
    blocks = len(prompts)
    pieces = [piece for slot in prompts for piece in slot]
    own = pieces[0].shape[3]
    layout, at = [], 0
    for slot in prompts:
        layout.append(tuple(range(at, at + len(slot))))
        at += len(slot)
    shared, tail = blocks * own, rows - own
    head = pl.BlockSpec((None, None, rows, HEAD_DIM), lambda m, h, _: (m, h, 0, 0))
    prompt = [pl.BlockSpec((p.shape[0], None, None, own, HEAD_DIM), lambda m, h, _: (0, m, h, 0, 0)) for p in pieces]
    half = pl.BlockSpec((blocks // 2, 2, None, None, own, HEAD_DIM), lambda m, h, _: (0, 0, m, h, 0, 0))
    flat = pl.BlockSpec((rows, HEAD_DIM), lambda m, h, _: (m, h))
    table = pl.BlockSpec((None, rows, LANES), lambda m, h, _: (m, 0, 0))
    return chain.run(
        functools.partial(attention_kernel, layout),
        (me, q, k, v, grad_context, first, cosine, signed, *pieces),
        scalars=1,
        grid=(micro, heads),
        ins=[head, head, head, flat, pl.BlockSpec((None, tail, 1), lambda m, h, _: (m, 0, 0)), table, table] + prompt,
        outs=[flat, pl.BlockSpec((None, rows, 3 * HEAD_DIM), lambda m, h, _: (m, 0, h)), half, half],
        shapes=[array((micro * rows, heads * HEAD_DIM)), array((micro, rows, heads * 3 * HEAD_DIM))]
        + [array((blocks // 2, 2, micro, heads, own, HEAD_DIM))] * 2,
        scratch=[pltpu.VMEM((shared + tail, HEAD_DIM), f32)] * 2,
        name="attention",
    )


def fold_kernel(a_ref, b_ref, keep_ref, send_ref):
    for i, ref in enumerate((keep_ref, send_ref)):
        ref[0] = (a_ref[i].astype(f32) + b_ref[i].astype(f32)).astype(bf16)


def fold(chain, kept, got):
    slots, shape = kept.shape[0], kept.shape[1:]
    count = kept.size // (slots * HEAD_DIM)
    one = pl.BlockSpec((1, count, HEAD_DIM), lambda i: (i, 0, 0))
    two = pl.BlockSpec((2, count, HEAD_DIM), lambda i: (i, 0, 0))
    keep, send = chain.run(
        fold_kernel,
        (kept.reshape(slots, count, HEAD_DIM), got.reshape(slots, count, HEAD_DIM)),
        grid=(slots // 2,),
        ins=[two, two],
        outs=[one, one],
        shapes=[array((slots // 2, count, HEAD_DIM))] * 2,
        name="fold",
    )
    return keep.reshape((slots // 2,) + shape), send.reshape((slots // 2,) + shape)


def slot_of(j, me, part, low, size):
    return pl.ds(pl.multiple_of(lax.bitwise_xor(jnp.int32(j), me) * part + low, LANES), size)


def context_kernel(g_ref, w_ref, o_ref):
    o_ref[...] = dot(g_ref[...], w_ref[...]).astype(bf16)


def grad_context_of(chain, g, packed, wide):
    count, width = g.shape
    tile = count // 4
    at = packed.shape[1] // wide - 1
    return chain.run(
        context_kernel,
        (g, packed),
        grid=(count // tile,),
        ins=[pl.BlockSpec((tile, width), lambda i: (i, 0)), pl.BlockSpec((width, wide), lambda i: (0, at))],
        outs=[pl.BlockSpec((tile, wide), lambda i: (i, 0))],
        shapes=[array((count, wide))],
        name="grad_context",
    )[0]


def forward_kernel(spots, part, me_ref, n_ref, bias_ref, *refs):
    ups, (act_ref, slope_ref, up_ref) = refs[: len(spots)], refs[len(spots) :]
    me = me_ref[0]

    @pl.when(pl.program_id(1) == 0)
    def _():
        for (r, low), ref in zip(spots, ups):
            up_ref[slot_of(r, me, part, low, ref.shape[0]), :] = ref[...]

    h = dot(n_ref[...], up_ref[...]) + bias_ref[...]
    z = jnp.abs(h)
    e = jnp.exp(-0.5 * (h * h))
    t = 1.0 / (1.0 + TAIL_P * z)
    q = jnp.full_like(t, TAIL[0])
    for co in TAIL[1:]:
        q = q * t + co
    low = e * (t * q)
    cdf = jnp.where(h >= 0.0, 1.0 - low, low)
    act_ref[...] = (h * cdf).astype(bf16)
    slope_ref[...] = (cdf + h * (e * PEAK)).astype(bf16)


def spots_of(slots):
    spots, pieces = [], []
    for r, slot in enumerate(slots):
        low = 0
        for piece in slot:
            spots.append((r, low))
            pieces.append(piece)
            low += piece.shape[0]
    return spots, pieces


def ff_forward(chain, me, norm_two, ups, bias, rows):
    count, width = norm_two.shape
    spots, pieces = spots_of(ups)
    part, hidden = ups[0][0].shape
    cols = min(512, hidden)
    out = pl.BlockSpec((rows, cols), lambda c, r, _: (r, c))
    return chain.run(
        functools.partial(forward_kernel, spots, part),
        (me, norm_two, bias, *pieces),
        scalars=1,
        grid=(hidden // cols, count // rows),
        ins=[
            pl.BlockSpec((rows, width), lambda c, r, _: (r, 0)),
            pl.BlockSpec((1, cols), lambda c, r, _: (0, c)),
        ]
        + [pl.BlockSpec((p.shape[0], cols), lambda c, r, _: (0, c)) for p in pieces],
        outs=[out, out],
        shapes=[array((count, hidden))] * 2,
        scratch=[pltpu.VMEM((width, cols), bf16)],
        name="ff_forward",
    )


def stack_kernel(spots, *refs):
    o_ref = refs[-1]
    for (r, low), ref in zip(spots, refs):
        o_ref[r, low : low + ref.shape[0], :] = ref[...]


def stack(chain, slots):
    spots, pieces = spots_of(slots)
    part, hidden = slots[0][0].shape
    cols = min(512, hidden)
    return chain.run(
        functools.partial(stack_kernel, spots),
        tuple(pieces),
        grid=(hidden // cols,),
        ins=[pl.BlockSpec((p.shape[0], cols), lambda c: (0, c)) for p in pieces],
        outs=[pl.BlockSpec((len(slots), part, cols), lambda c: (0, 0, c))],
        shapes=[array((len(slots), part, hidden))],
        name="stack",
    )[0]


def backward_kernel(g_ref, down_ref, slope_ref, grad_ref, rows_ref):
    blocks, _, part = down_ref.shape

    @pl.when(pl.program_id(1) == 0)
    def _():
        for j in range(blocks):
            rows_ref[:, j * part : (j + 1) * part] = down_ref[j]

    ga = dot(g_ref[...], rows_ref[...], NT)
    grad_ref[...] = (ga * slope_ref[...].astype(f32)).astype(bf16)


def ff_backward(chain, g, down, slope, rows):
    count, width = g.shape
    blocks, hidden, part = down.shape
    cols = min(1024, hidden)
    out = pl.BlockSpec((rows, cols), lambda c, r: (r, c))
    return chain.run(
        backward_kernel,
        (g, down, slope),
        grid=(hidden // cols, count // rows),
        ins=[
            pl.BlockSpec((rows, width), lambda c, r: (r, 0)),
            pl.BlockSpec((blocks, cols, part), lambda c, r: (0, c, 0)),
            out,
        ],
        outs=[out],
        shapes=[array((count, hidden))],
        scratch=[pltpu.VMEM((cols, width), bf16)],
        name="ff_backward",
    )[0]


def mix_kernel(act_ref, ctx_ref, down_ref, dense_ref, *o_refs):
    total = dot(act_ref[...], down_ref[...])
    total += dot(ctx_ref[...], dense_ref[...], NT)
    size = total.shape[0] // len(o_refs)
    for i, ref in enumerate(o_refs):
        ref[...] = total[i * size : (i + 1) * size].astype(bf16)


def mix(chain, act, context, down, packed, rows, index, pieces):
    hidden = act.shape[1]
    wide = context.shape[1]
    blocks, _, part = down.shape
    size = rows // pieces
    at = packed.shape[1] // wide - 1
    return chain.run(
        mix_kernel,
        (act, context, down, packed),
        grid=(blocks,),
        ins=[
            pl.BlockSpec((rows, hidden), lambda j: (index, 0)),
            pl.BlockSpec((rows, wide), lambda j: (index, 0)),
            pl.BlockSpec((None, hidden, part), lambda j: (j, 0, 0)),
            pl.BlockSpec((part, wide), lambda j: (j, at)),
        ],
        outs=[pl.BlockSpec((size, part), lambda j: (0, j))] * pieces,
        shapes=[array((size, blocks * part))] * pieces,
        name="mix",
        key="mix%d" % min(index, 1),
    )


def second_grad_kernel(act_ref, ctx_ref, g_ref, o_ref):
    hidden = act_ref.shape[1]
    o_ref[:hidden, :] = dot(act_ref[...], g_ref[...], TN).astype(bf16)
    o_ref[hidden:, :] = dot(ctx_ref[...], g_ref[...], TN).astype(bf16)


def second_grads(chain, act, context, g, blocks):
    count, hidden = act.shape
    wide = context.shape[1]
    part = g.shape[1] // blocks
    return chain.run(
        second_grad_kernel,
        (act, context, g),
        grid=(blocks,),
        ins=[
            pl.BlockSpec((count, hidden), lambda j: (0, 0)),
            pl.BlockSpec((count, wide), lambda j: (0, 0)),
            pl.BlockSpec((count, part), lambda j: (0, j)),
        ],
        outs=[pl.BlockSpec((None, hidden + wide, part), lambda j: (j, 0, 0))],
        shapes=[array((blocks, hidden + wide, part))],
        name="second_grads",
    )[0]


def norm_grad_kernel(me_ref, gj_ref, gh_ref, wj_ref, wu_ref, x_ref, mean_ref, inv_ref, g1_ref, g2_ref, *outs):
    *o_refs, stat_ref, sum_ref = outs

    @pl.when(pl.program_id(0) == 0)
    def _():
        sum_ref[...] = jnp.sum(gj_ref[...].astype(f32), axis=0, keepdims=True)

    one = dot(gj_ref[...], wj_ref[...], NT)
    two = dot(gh_ref[...], wu_ref[...], NT)
    normed = (x_ref[...].astype(f32) - mean_ref[...]) * inv_ref[...]
    total = one * g1_ref[...] + two * g2_ref[...]
    size = total.shape[0] // len(o_refs)
    for i, ref in enumerate(o_refs):
        ref[...] = total[i * size : (i + 1) * size].astype(bf16)
    for i, term in enumerate((one * normed, one, two * normed, two)):
        stat_ref[i : i + 1, :] = jnp.sum(term, axis=0, keepdims=True)


def norm_grads(chain, me, grad_joined, grad_hidden, packed, up, x, mean, inverse, gain_one, gain_two, rows, index, pieces):
    width = x.shape[1]
    wide, hidden = grad_joined.shape[1], grad_hidden.shape[1]
    blocks, part, _ = up.shape
    size = rows // pieces
    column = pl.BlockSpec((rows, 1), lambda c, _: (index, 0))
    gain = pl.BlockSpec((1, part), lambda c, _: (0, c))
    return chain.run(
        norm_grad_kernel,
        (me, grad_joined, grad_hidden, packed, up, x, mean, inverse, gain_one, gain_two),
        scalars=1,
        grid=(blocks,),
        ins=[
            pl.BlockSpec((rows, wide), lambda c, _: (index, 0)),
            pl.BlockSpec((rows, hidden), lambda c, _: (index, 0)),
            pl.BlockSpec((part, wide), lambda c, _: (c, 0)),
            pl.BlockSpec((None, part, hidden), lambda c, me: (lax.bitwise_xor(c, me[0]), 0, 0)),
            pl.BlockSpec((rows, part), lambda c, _: (index, c)),
            column, column, gain, gain,
        ],
        outs=[pl.BlockSpec((size, part), lambda c, _: (0, c))] * pieces
        + [pl.BlockSpec((8, part), lambda c, _: (0, c)), pl.BlockSpec((1, wide), lambda c, _: (0, 0))],
        shapes=[array((size, width))] * pieces + [array((8, width), f32), array((1, wide), f32)],
        name="norm_grads",
        key="norm_grads%d" % min(index, 1),
    )


def prompt_kernel(keep_ref, got_ref, cos_ref, sin_ref, _, o_ref):
    total = keep_ref[...].astype(f32) + got_ref[...].astype(f32)

    @pl.when(pl.program_id(2) == 0)
    def _():
        first = rotated_back(total[:, :LANES], cos_ref[...], sin_ref[...], kernel_roll)
        o_ref[:, :LANES] = first.astype(bf16)
        o_ref[:, LANES:] = total[:, LANES:].astype(bf16)

    @pl.when(pl.program_id(2) == 1)
    def _():
        o_ref[...] = total.astype(bf16)


def put_prompt(chain, grad_joined, kept, got, cosine, signed):
    _, _, micro, heads, own, _ = kept.shape
    part = pl.BlockSpec((None, None, None, None, own, HEAD_DIM), lambda m, h, i: (0, i, m, h, 0, 0))
    table = pl.BlockSpec((None, own, LANES), lambda m, h, i: (m, 0, 0))
    return chain.run(
        prompt_kernel,
        (kept, got, cosine, signed, grad_joined),
        grid=(micro, heads, 2),
        ins=[part, part, table, table, ANY],
        outs=[pl.BlockSpec((None, own, HEAD_DIM), lambda m, h, i: (m, 0, 3 * h + 1 + i))],
        shapes=[array(grad_joined.shape)],
        aliases={4: 0},
        name="put_prompt",
    )[0]


def pair_kernel(a_ref, b_ref, o_ref):
    o_ref[...] = (a_ref[...].astype(f32) + b_ref[...].astype(f32)).astype(bf16)


def add_pair(chain, a, b, low, size):
    width = a.shape[1]
    tile = size // 2
    row = pl.BlockSpec((tile, width), lambda i: (low // tile + i, 0))
    return chain.run(
        pair_kernel,
        (a, b),
        grid=(size // tile,),
        ins=[row, row],
        outs=[pl.BlockSpec((tile, width), lambda i: (i, 0))],
        shapes=[array((size, width))],
        name="add_pair",
    )[0]


def output_kernel(a_ref, b_ref, x_ref, dense_ref, down_ref, o_ref):
    total = a_ref[...].astype(f32) + b_ref[...].astype(f32)
    o_ref[...] = (x_ref[...].astype(f32) + total + dense_ref[...] + down_ref[...]).astype(bf16)


def input_kernel(a_ref, b_ref, x_ref, g_ref, mean_ref, inv_ref, o_ref):
    total = a_ref[...].astype(f32) + b_ref[...].astype(f32)
    inverse = inv_ref[...]
    normed = (x_ref[...].astype(f32) - mean_ref[...]) * inverse
    centred = (
        total
        - jnp.mean(total, axis=-1, keepdims=True)
        - normed * jnp.mean(total * normed, axis=-1, keepdims=True)
    )
    o_ref[...] = (g_ref[...].astype(f32) + inverse * centred).astype(bf16)


def finish(chain, a, b, start, rows, columns=(), vectors=()):
    size, width = a.shape
    tile = size // 2
    at = start // tile
    here = pl.BlockSpec((tile, width), lambda i: (i, 0))
    there = pl.BlockSpec((tile, width), lambda i: (at + i, 0))
    column = pl.BlockSpec((tile, 1), lambda i: (at + i, 0))
    vector = pl.BlockSpec((1, width), lambda i: (0, 0))
    return chain.run(
        input_kernel if columns else output_kernel,
        (a, b, *rows, *columns, *vectors),
        grid=(size // tile,),
        ins=[here, here] + [there] * len(rows) + [column] * len(columns) + [vector] * len(vectors),
        outs=[here],
        shapes=[array((size, width))],
        name="finish",
    )[0]


def swap(value, axis, bit):
    size = lax.axis_size(axis)
    return lax.ppermute(value, axis, [(i, i ^ (1 << bit)) for i in range(size)])


def bits_of(axis):
    return lax.axis_size(axis).bit_length() - 1


def send_xor(value, axis, offset):
    size = lax.axis_size(axis)
    return lax.ppermute(value, axis, [(i, i ^ offset) for i in range(size)])


def join(*values):
    return lax.optimization_barrier(values)


class Gather:
    def __init__(self, value, axis):
        self.axis, self.size = axis, lax.axis_size(axis)
        self.direct = self.size != 8
        offsets = range(2, self.size, 2) if self.direct else (2, 4)
        self.slots = [None] * self.size
        self.slots[0] = [value]
        self.slots[1] = [send_xor(value, axis, 1)]
        for r in offsets:
            self.slots[r] = [send_xor(value, axis, r)]

    def first(self, *others):
        here = [r for r in range(self.size) if r and self.slots[r]]
        values = join(*[self.slots[r][0] for r in here], *others)
        for r, value in zip(here, values):
            self.slots[r] = [value]
        self.fresh = []
        if not self.direct:
            near, far = self.slots[2][0], self.slots[4][0]
            half = near.shape[0] // 2
            self.fresh = [send_xor(near[:half], self.axis, 4), send_xor(far[half:], self.axis, 2)]
        self.twins = [r for r in here if r > 1]
        self.fresh += [send_xor(self.slots[r][0], self.axis, 1) for r in self.twins]
        return values[len(here) :]

    def second(self, *others):
        values = join(*self.fresh, *others)
        if not self.direct:
            self.slots[6] = list(values[:2])
            self.slots[7] = [send_xor(piece, self.axis, 1) for piece in self.slots[6]]
        for r, value in zip(self.twins, values[len(self.fresh) - len(self.twins) :]):
            self.slots[r + 1] = [value]
        return values[len(self.fresh) :]


def gather_ordered(value, axis):
    index = lax.axis_index(axis)
    held = value[None]
    for bit in range(bits_of(axis)):
        other = swap(held, axis, bit)
        low = ((index >> bit) & 1) == 0
        held = jnp.concatenate([jnp.where(low, held, other), jnp.where(low, other, held)], 0)
    return held


def add_up(value, axis):
    for bit in range(bits_of(axis)):
        value = value + swap(value, axis, bit)
    return value


def own_rows(value, start, count):
    return lax.dynamic_slice_in_dim(value, start, count, 0)


def sum_rows(partial, axis):
    index = lax.axis_index(axis)
    held, start = partial, jnp.int32(0)
    for bit in range(bits_of(axis)):
        mine = (index >> bit) & 1
        half = held.shape[0] // 2
        other = swap(own_rows(held, (1 - mine) * half, half).astype(bf16), axis, bit)
        held = own_rows(held, mine * half, half).astype(f32) + other.astype(f32)
        start = start + mine * half
    return held, start


def spread_rows(share, axis):
    index = lax.axis_index(axis)
    held = share
    for bit in reversed(range(bits_of(axis))):
        mine = (index >> bit) & 1
        other = swap(held, axis, bit)
        held = jnp.where(
            mine == 0, jnp.concatenate([held, other], 0), jnp.concatenate([other, held], 0)
        )
    return held


TO_MIDDLE = [(0, 1), (3, 2)]
ACROSS = [(1, 2), (2, 1)]
TO_ENDS = [(1, 0), (2, 3)]


class Piece:
    def __init__(self, chain, partial, first, low, size, axis, closing):
        self.chain, self.axis, self.closing = chain, axis, closing
        self.partial, self.first, self.low, self.size = partial, first, low, size

    def cross(self):
        self.pair = add_pair(self.chain, self.partial, self.first, self.low, self.size)
        self.second = lax.ppermute(self.pair, self.axis, ACROSS)

    def close(self):
        self.own = self.closing(self.pair, self.second)
        self.third = lax.ppermute(self.own, self.axis, TO_ENDS)


def local(
    tokens,
    cont_lengths,
    first_gain,
    first_bias,
    second_gain,
    second_bias,
    joined_weight,
    joined_bias,
    dense_weight,
    dense_bias,
    up_weight,
    up_bias,
    down_weight,
    down_bias,
    cotangent,
):
    blocks, ranks = lax.axis_size("dp"), lax.axis_size("tensor")
    me = lax.axis_index("dp").astype(jnp.int32)
    micro, _, rows, width = tokens.shape
    count = micro * rows
    own = PROMPT // blocks
    tail = rows - own
    part = width // blocks
    heads = joined_weight.shape[1] // (3 * HEAD_DIM)
    wide = heads * HEAD_DIM
    hidden = up_weight.shape[1]
    x = tokens.reshape(count, width)
    g = cotangent.reshape(count, width)
    here = me.reshape(1)

    chain = Chain()
    packed, first_gain = join(pack(chain, joined_weight, dense_weight), first_gain)
    packed = lax.all_gather(packed, "dp", axis=0, tiled=True)
    down = lax.all_gather(down_weight, "dp", axis=0, tiled=False)

    vectors = (first_gain, first_bias, second_gain, second_bias, dense_bias, down_bias)
    small = jnp.concatenate([v.reshape(-1) for v in vectors + (joined_bias, up_bias)])
    small = gather_ordered(small, "dp")
    up_here, small = join(up_weight, small)
    ups = Gather(up_here, "dp")

    small = small.astype(f32)
    full = [small[:, i * part : (i + 1) * part].reshape(1, width) for i in range(6)]
    gain_one, bias_one, gain_two, bias_two, dense_add, down_add = full

    def by_head(start, like):
        piece = small[:, start : start + like.size].reshape((blocks,) + like.shape)
        return jnp.transpose(piece, (1, 0, 2)).reshape(1, -1)

    joined_add = by_head(6 * part, joined_bias)
    up_add = by_head(6 * part + joined_bias.size, up_bias)

    seg_ends = jnp.cumsum(cont_lengths[:, 0], axis=1)
    slots = jnp.arange(tail, dtype=jnp.int32)
    passed = (slots[None, :, None] >= seg_ends[:, None, :]).astype(jnp.int32)
    first = jnp.sum(passed * cont_lengths[:, 0][:, None, :], axis=2)
    prompt_pos = jnp.broadcast_to(me * own + jnp.arange(own, dtype=jnp.int32), (micro, own))
    positions = jnp.concatenate([prompt_pos, PROMPT + slots[None] - first], axis=1)
    cosine, signed = rope_tables(positions)

    norm_one, norm_two, mean, inverse, upstream_sum = norms(chain, x, g, gain_one, bias_one, gain_two, bias_two)
    norm_one, cosine, signed, packed = ups.first(norm_one, cosine, signed, packed)

    q, k, v, prompt = qkv(chain, norm_one.reshape(micro, rows, width), packed, joined_add, cosine, signed, own)
    (prompt,) = ups.second(prompt)
    prompts = Gather(prompt, "dp")
    act, slope = ff_forward(chain, here, norm_two, ups.slots, up_add, rows)
    (slope,) = prompts.first(slope)
    grad_context = grad_context_of(chain, g, packed, wide)
    (grad_context,) = prompts.second(grad_context)
    prompts, ups = prompts.slots, ups.slots

    line = ranks == 4
    pieces = 2
    size = rows // pieces
    context, grad_joined, kept, sent = attention(
        chain, here, q, k, v, prompts, grad_context, first[..., None], cosine, signed
    )
    got = send_xor(sent, "dp", 1)

    def close_output(start):
        return lambda a, b: finish(chain, a, b, start, (x,), vectors=(dense_add, down_add))

    def close_input(start):
        return lambda a, b: finish(chain, a, b, start, (x, g), columns=(mean, inverse))

    rank = lax.axis_index("tensor")
    end = ((rank == 0) | (rank == 3)).astype(jnp.int32).reshape(1)
    have = {"kept": kept, "got": got, "bit": 1, "joined": grad_joined, "stats": [], "joined_sums": [], "results": [None, None]}
    partials, sums = [None] * (2 * micro), []

    def along_rows(value, like):
        lead, span = like.shape
        value = jnp.transpose(value.reshape(lead, blocks, span), (1, 0, 2)).reshape(blocks, lead * span)
        return jnp.pad(value, ((0, 0), (0, part - lead * span))).reshape(1, width)

    def sums_of_all():
        stats = functools.reduce(jnp.add, have["stats"])
        joined_sums = functools.reduce(jnp.add, have["joined_sums"])
        rows_of = [stats, upstream_sum, along_rows(have["up_sums"], up_bias), along_rows(joined_sums, joined_bias)]
        return jnp.concatenate(rows_of + [jnp.zeros((1, width), f32)], 0)

    def scattered(value):
        return lax.psum_scatter(value, "dp", scatter_dimension=0, tiled=value.ndim == 2)

    def step(what, *which):
        if what == "mix":
            partials[which[0]] = mix(chain, act, context, down, packed, rows, which[0], 1 if which[0] in MERGED else pieces)
        elif what == "go":
            stage, i, *behind = which
            partial, start = partials[stage][i], (stage % micro) * rows + i * size
            if line:
                if behind:
                    piece = sums[behind[0]]
                    partial, piece.pair = join(partial, piece.pair)
                got = lax.ppermute(partial, "tensor", TO_MIDDLE)
                for low in range(0, partial.shape[0], size):
                    closing = (close_output, close_input)[stage // micro](start + low)
                    sums.append(Piece(chain, partial, got, low, size, "tensor", closing))
        elif what == "fold":
            for _ in range(1 if line or have["bit"] == 1 else bits_of("dp") - 2):
                kept, sent = fold(chain, have["kept"], have["got"])
                have["kept"], have["got"] = kept, send_xor(sent, "dp", 1 << have["bit"])
                have["bit"] += 1
        elif what == "ffb":
            have["hidden"] = ff_backward(chain, g, down, slope, rows)
        elif what == "up":
            have["up"], have["up_sums"] = outer(chain, norm_two, have["hidden"], "outer0")
        elif what == "stack":
            have["ups"] = stack(chain, ups)
        elif what == "second":
            have["second"] = second_grads(chain, act, context, g, blocks)
        elif what == "joined":
            have["joined_grad"] = outer_more(chain, norm_one, have["joined"], sums_of_all(), "outer1")
        elif what == "send":
            if line and len(which) > 1:
                piece = sums[which[1]]
                piece.pair, have[which[0]] = join(piece.pair, have[which[0]])
            have[which[0]] = scattered(have[which[0]])
        elif what == "prompt":
            put = put_prompt(chain, have["joined"], have["kept"], have["got"], cosine, signed)
            have["joined"] = put.reshape(count, 3 * wide)
        elif what == "norm":
            m = which[0]
            *parts, stat, joined_sums = norm_grads(
                chain, here, have["joined"], have["hidden"], packed, have["ups"], x, mean, inverse, gain_one, gain_two,
                rows, m, 1 if micro + m in MERGED else pieces,
            )
            partials[micro + m] = parts
            have["stats"].append(stat[:4])
            have["joined_sums"].append(joined_sums)
        elif not line:
            pass
        elif what == "cross":
            sums[which[0]].cross()
        elif what == "close":
            k = which[0]
            if 1 <= k < BACK:
                sums[k].pair, sums[k - 1].third = join(sums[k].pair, sums[k - 1].third)
            sums[k].close()
            if k == END_TIE:
                sums[k].own, have["joined_grad"] = join(sums[k].own, have["joined_grad"])
        elif what == "gains":
            vector = have["joined_grad"][:, 3 * wide : 3 * wide + 8].astype(f32).T
            sums[6].own, have["gains"] = join(sums[6].own, add_up(vector[:4], "tensor"))
        elif what == "place":
            low, high = which
            kind = low // (2 * pieces)
            have["results"][kind] = place(chain, have["results"][kind], end, sums[low:high], low * size % count, count)
        elif what == "tie":
            piece = sums[which[1]]
            piece.pair, have[which[0]] = join(piece.pair, have[which[0]])

    for one in PLAN:
        step(*one)
    up_out, second_out, joined_out = have["up"], have["second"], have["joined_grad"]
    joined_out = joined_out.astype(f32)
    vector = joined_out[:, 3 * wide : 3 * wide + 8].T
    joined_out = joined_out[:, : 3 * wide]
    if line:
        gains = have["gains"]
        output, input_grad = [r.reshape(micro, rows, width) for r in have["results"]]
    else:
        gains = add_up(vector[:4], "tensor")
    if not line:
        outputs, inputs = [], []
        for m in range(micro):
            share, start = sum_rows(jnp.concatenate(partials[m]), "tensor")
            span = share.shape[0]
            mine = own_rows(x, m * rows + start, span).astype(f32)
            outputs.append(spread_rows((mine + share + dense_add + down_add).astype(bf16), "tensor"))
            share, start = sum_rows(jnp.concatenate(partials[micro + m]), "tensor")
            start = m * rows + start
            row_inverse = own_rows(inverse, start, span)
            row_normed = (own_rows(x, start, span).astype(f32) - own_rows(mean, start, span)) * row_inverse
            centred = (
                share
                - jnp.mean(share, axis=-1, keepdims=True)
                - row_normed * jnp.mean(share * row_normed, axis=-1, keepdims=True)
            )
            result = own_rows(g, start, span).astype(f32) + row_inverse * centred
            inputs.append(spread_rows(result.astype(bf16), "tensor"))
        output, input_grad = jnp.stack(outputs), jnp.stack(inputs)

    return (
        output[:, None],
        input_grad[:, None],
        gains[0],
        gains[1],
        gains[2],
        gains[3],
        joined_out,
        vector[6, : joined_bias.size].reshape(joined_bias.shape),
        second_out[hidden:].astype(f32),
        vector[4],
        up_out.astype(f32),
        vector[5, : up_bias.size].reshape(up_bias.shape),
        second_out[:hidden].astype(f32),
        vector[4],
    )


def solution(mesh):
    placed = (
        P(None, "dp", None, None),
        P(None, "dp", None),
        P("dp"),
        P("dp"),
        P("dp"),
        P("dp"),
        P("dp", "tensor"),
        P("tensor", "dp"),
        P("tensor", "dp"),
        P("dp"),
        P("dp", "tensor"),
        P("tensor", "dp"),
        P("tensor", "dp"),
        P("dp"),
        P(None, "dp", None, None),
    )
    return jax.shard_map(
        local,
        mesh=mesh,
        in_specs=placed,
        out_specs=(
            P(None, "dp", None, None),
            P(None, "dp", None, None),
            P("dp"),
            P("dp"),
            P("dp"),
            P("dp"),
            P("dp", "tensor"),
            P("tensor", "dp"),
            P("tensor", "dp"),
            P("dp"),
            P("dp", "tensor"),
            P("tensor", "dp"),
            P("tensor", "dp"),
            P("dp"),
        ),
        check_vma=False,
    )
```

```python
import functools

import jax
import jax.numpy as jnp
from jax import lax
from jax.experimental import pallas as pl
from jax.experimental.pallas import tpu as pltpu
from jax.sharding import PartitionSpec as P

HEAD_DIM = 256
ROT_DIMS = 64
PROMPT = 1024
LONGEST = 128

norm_eps = 1e-05
rope_base = 10000.0
masked_score = -1e30
scale = HEAD_DIM**-0.5
LANES = 128
VMEM = 60 << 20

f32, bf16 = jnp.float32, jnp.bfloat16
NN = (((1,), (0,)), ((), ()))
NT = (((1,), (1,)), ((), ()))
TN = (((0,), (0,)), ((), ()))

TAIL_P = 0.32
TAIL = (
    -0.02115197293220867,
    0.09575628590143809,
    -0.14740109756488956,
    0.06607995422323057,
    -0.0098602948578973,
    0.058840354546090344,
    0.08778712629904878,
    0.11462742044446793,
    0.12766067496581068,
    0.12766153278717104,
)
PEAK = 0.3989422804014327


def dot(a, b, dims=NN):
    return lax.dot_general(a, b, dims, preferred_element_type=f32)


TIMES = {
    "pack": 2.3,
    "norms": 12.4,
    "qkv": 14.0,
    "grad_context": 7.0,
    "ff_forward": 28.0,
    "attention": 25.0,
    "mix0": 13.0,
    "mix1": 13.0,
    "second_grads": 20.0,
    "fold": 3.5,
    "add_pair": 3.0,
    "finish": 40.0,
    "ff_backward": 18.5,
    "put_prompt": 5.4,
    "norm_grads0": 16.0,
    "norm_grads1": 16.0,
    "stack": 8.0,
    "outer0": 17.0,
    "outer1": 13.0,
    "place": 4.5,
}
FLOPS = 1.15e9
SHARE = 2.0
BACK = 5
END_TIE = 7
PLAN = (('mix', 0), ('go', 0, 0), ('go', 0, 1), ('mix', 1), ('fold',), ('ffb',), ('cross', 0), ('go', 1, 0, 0), ('up',), ('cross', 1), ('go', 1, 1, 1), ('send', 'up', 1), ('stack',), ('fold',), ('close', 0), ('second',), ('cross', 2), ('send', 'second', 2), ('close', 1), ('prompt',), ('norm', 0), ('go', 2, 0, 2), ('cross', 3), ('go', 2, 1, 3), ('close', 2), ('place', 0, 2), ('norm', 1), ('go', 3, 0, 3), ('cross', 4), ('go', 3, 1, 4), ('close', 3), ('joined',), ('cross', 5), ('send', 'joined_grad', 5), ('close', 4), ('place', 2, 4), ('cross', 6), ('close', 5), ('cross', 7), ('close', 6), ('place', 4, 6), ('tie', 'up', 7), ('tie', 'second', 7), ('close', 7), ('place', 6, 7), ('gains',), ('place', 7, 8))
MERGED = ()


def cost(name):
    return pl.CostEstimate(flops=int(TIMES[name] * FLOPS * SHARE), bytes_accessed=0, transcendentals=0)


ANY = pl.BlockSpec(memory_space=pl.ANY)


class Chain:
    def __init__(self):
        self.last = ()

    def run(self, kernel, args, *, grid, ins, outs, shapes, name, key=None, scalars=0, scratch=(), aliases=None):
        count, extra = len(args), tuple(e for e in self.last if all(e is not a for a in args))

        def body(*refs):
            kernel(*refs[:count], *refs[count + len(extra) :])

        results = pl.pallas_call(
            body,
            grid_spec=pltpu.PrefetchScalarGridSpec(
                num_scalar_prefetch=scalars,
                grid=grid,
                in_specs=list(ins) + [ANY] * len(extra),
                out_specs=outs,
                scratch_shapes=list(scratch),
            ),
            out_shape=shapes,
            input_output_aliases=aliases or {},
            compiler_params=pltpu.CompilerParams(vmem_limit_bytes=VMEM),
            cost_estimate=cost(key or name),
            name=name,
        )(*args, *extra)
        self.last = (results[0],)
        return results


def array(shape, dtype=bf16):
    return jax.ShapeDtypeStruct(tuple(shape), dtype)


def rope_tables(positions):
    half = ROT_DIMS // 2
    inverse = rope_base ** (-(2.0 * jnp.arange(half, dtype=f32)) / ROT_DIMS)
    angles = positions.astype(f32)[..., None] * inverse
    ones = jnp.ones(positions.shape + (LANES - ROT_DIMS,), f32)
    c, s = jnp.cos(angles), jnp.sin(angles)
    return jnp.concatenate([c, c, ones], -1), jnp.concatenate([-s, s, ones * 0.0], -1)


def swap_halves(u, roll):
    half = ROT_DIMS // 2
    lane = lax.broadcasted_iota(jnp.int32, u.shape, u.ndim - 1)
    up, down = roll(u, LANES - half), roll(u, half)
    return jnp.where(lane < half, up, jnp.where(lane < ROT_DIMS, down, 0.0))


def rotated(u, cosine, signed, roll):
    return u * cosine + swap_halves(u, roll) * signed


def rotated_back(y, cosine, signed, roll):
    return y * cosine + swap_halves(y * signed, roll)


def kernel_roll(u, by):
    return pltpu.roll(u, by, u.ndim - 1)


def plain_roll(u, by):
    return jnp.roll(u, by, -1)


def norm_kernel(x_ref, g_ref, g1_ref, b1_ref, g2_ref, b2_ref, n1_ref, n2_ref, mean_ref, inv_ref, sum_ref):
    x = x_ref[...].astype(f32)
    mean = jnp.mean(x, axis=-1, keepdims=True)
    centered = x - mean
    inverse = lax.rsqrt(jnp.mean(centered * centered, axis=-1, keepdims=True) + norm_eps)
    normed = centered * inverse
    n1_ref[...] = (normed * g1_ref[...] + b1_ref[...]).astype(bf16)
    n2_ref[...] = (normed * g2_ref[...] + b2_ref[...]).astype(bf16)
    mean_ref[...] = mean
    inv_ref[...] = inverse

    @pl.when(pl.program_id(0) == 0)
    def _():
        sum_ref[...] = jnp.zeros_like(sum_ref)

    sum_ref[...] += jnp.sum(g_ref[...].astype(f32), axis=0, keepdims=True)


def norms(chain, x, g, gain_one, bias_one, gain_two, bias_two):
    count, width = x.shape
    tile = count // 8
    row = pl.BlockSpec((tile, width), lambda i: (i, 0))
    vector = pl.BlockSpec((1, width), lambda i: (0, 0))
    column = pl.BlockSpec((tile, 1), lambda i: (i, 0))
    return chain.run(
        norm_kernel,
        (x, g, gain_one, bias_one, gain_two, bias_two),
        grid=(count // tile,),
        ins=[row, row] + [vector] * 4,
        outs=[row, row, column, column, vector],
        shapes=[array((count, width))] * 2 + [array((count, 1), f32)] * 2 + [array((1, width), f32)],
        name="norms",
    )


def outer_kernel(a_ref, b_ref, o_ref, sum_ref):
    o_ref[...] = dot(a_ref[...], b_ref[...], TN).astype(bf16)

    @pl.when(pl.program_id(0) == 0)
    def _():
        sum_ref[...] = jnp.sum(b_ref[...].astype(f32), axis=0, keepdims=True)


def outer(chain, a, b, key):
    count, width = a.shape
    cols = b.shape[1]
    tile = width // 4
    return chain.run(
        outer_kernel,
        (a, b),
        grid=(4,),
        ins=[pl.BlockSpec((count, tile), lambda i: (0, i)), pl.BlockSpec((count, cols), lambda i: (0, 0))],
        outs=[pl.BlockSpec((tile, cols), lambda i: (i, 0)), pl.BlockSpec((1, cols), lambda i: (0, 0))],
        shapes=[array((width, cols)), array((1, cols), f32)],
        name="outer",
        key=key,
    )


def outer_more_kernel(a_ref, b_ref, more_ref, o_ref):
    cols = b_ref.shape[1]
    o_ref[:, :cols] = dot(a_ref[...], b_ref[...], TN).astype(bf16)
    o_ref[:, cols:] = jnp.zeros((o_ref.shape[0], LANES), bf16)
    o_ref[:, cols : cols + more_ref.shape[0]] = more_ref[...].T.astype(bf16)


def outer_more(chain, a, b, more, key):
    count, width = a.shape
    cols = b.shape[1]
    tile = width // 4
    return chain.run(
        outer_more_kernel,
        (a, b, more),
        grid=(4,),
        ins=[
            pl.BlockSpec((count, tile), lambda i: (0, i)),
            pl.BlockSpec((count, cols), lambda i: (0, 0)),
            pl.BlockSpec((more.shape[0], tile), lambda i: (0, i)),
        ],
        outs=[pl.BlockSpec((tile, cols + LANES), lambda i: (i, 0))],
        shapes=[array((width, cols + LANES))],
        name="outer",
        key=key,
    )[0]


def place_kernel(flag_ref, *refs):
    o_ref = refs[-1]
    pieces = len(refs) // 2 if len(refs) % 2 else len(refs) // 2 - 1
    for i in range(pieces):
        for flag in (0, 1):

            @pl.when((flag_ref[0] == flag) & (pl.program_id(0) // 2 == i))
            def _():
                o_ref[...] = refs[2 * i + flag][...]


def place(chain, held, flag, pieces, start, total):
    size, width = pieces[0].own.shape
    tile = size // 2
    keep = () if held is None else (held,)
    ins, args = [], []
    for i, piece in enumerate(pieces):
        args += [piece.own, piece.third]
        ins += [
            pl.BlockSpec((tile, width), lambda j, flag, i=i: (jnp.clip(j - 2 * i, 0, 1) * (1 - flag[0]), 0)),
            pl.BlockSpec((tile, width), lambda j, flag, i=i: (jnp.clip(j - 2 * i, 0, 1) * flag[0], 0)),
        ]
    return chain.run(
        place_kernel,
        (flag, *args) + keep,
        scalars=1,
        grid=(2 * len(pieces),),
        ins=ins + [ANY] * len(keep),
        outs=[pl.BlockSpec((tile, width), lambda j, _: (start // tile + j, 0))],
        shapes=[array((total, width))],
        aliases={1 + len(args): 0} if keep else {},
        name="place",
    )[0]


def pack_kernel(joined_ref, dense_ref, o_ref):
    wide = joined_ref.shape[1]
    o_ref[:, :wide] = joined_ref[...]
    o_ref[:, wide:] = dense_ref[...].T


def pack(chain, joined, dense):
    part, wide = joined.shape
    total = wide + dense.shape[0]

    def whole(rows, columns):
        return pl.BlockSpec((rows, columns), lambda i: (0, 0))

    return chain.run(
        pack_kernel,
        (joined, dense),
        grid=(1,),
        ins=[whole(*joined.shape), whole(*dense.shape)],
        outs=[whole(part, total)],
        shapes=[array((part, total))],
        name="pack",
    )[0]


def qkv_kernel(x_ref, w_ref, bias_ref, cos_ref, sin_ref, q_ref, k_ref, v_ref, prompt_ref):
    joined = dot(x_ref[...], w_ref[...]) + bias_ref[...]
    c, s = cos_ref[...], sin_ref[...]
    for part, ref in ((0, q_ref), (1, k_ref)):
        base = part * HEAD_DIM
        head = joined[:, base : base + HEAD_DIM]
        ref[:, :LANES] = rotated(head[:, :LANES], c, s, kernel_roll).astype(bf16)
        ref[:, LANES:] = head[:, LANES:].astype(bf16)
    v_ref[...] = joined[:, 2 * HEAD_DIM :].astype(bf16)
    own = prompt_ref.shape[1]
    prompt_ref[0] = k_ref[:own, :]
    prompt_ref[1] = v_ref[:own, :]


def qkv(chain, norm_one, weight, bias, cosine, signed, own):
    micro, rows, width = norm_one.shape
    wide = 3 * HEAD_DIM
    heads = bias.shape[1] // wide
    head = pl.BlockSpec((None, None, rows, HEAD_DIM), lambda h, m: (m, h, 0, 0))
    table = pl.BlockSpec((None, rows, LANES), lambda h, m: (m, 0, 0))
    return chain.run(
        qkv_kernel,
        (norm_one, weight, bias, cosine, signed),
        grid=(heads, micro),
        ins=[
            pl.BlockSpec((None, rows, width), lambda h, m: (m, 0, 0)),
            pl.BlockSpec((width, wide), lambda h, m: (0, h)),
            pl.BlockSpec((1, wide), lambda h, m: (0, h)),
            table,
            table,
        ],
        outs=[head] * 3 + [pl.BlockSpec((2, None, None, own, HEAD_DIM), lambda h, m: (0, m, h, 0, 0))],
        shapes=[array((micro, heads, rows, HEAD_DIM))] * 3 + [array((2, micro, heads, own, HEAD_DIM))],
        name="qkv",
    )


def attention_kernel(layout, me_ref, q_ref, k_ref, v_ref, up_ref, first_ref, cos_ref, sin_ref, *refs):
    ctx_ref, grad_ref, keep_ref, send_ref, dk_acc, dv_acc = refs[-6:]
    blocks, own = len(layout), refs[0].shape[1]
    rows = q_ref.shape[0]
    tail = rows - own
    shared = blocks * own
    me = me_ref[0]
    pk = jnp.concatenate([refs[spots[0]][0] for spots in layout], 0)
    pv = jnp.concatenate([refs[spots[-1]][refs[spots[-1]].shape[0] - 1] for spots in layout], 0)
    ck, cv = k_ref[own:, :], v_ref[own:, :]
    dk_acc[...] = jnp.zeros_like(dk_acc)
    dv_acc[...] = jnp.zeros_like(dv_acc)

    def chunk(start, count, low, high):
        here = slice(start, start + count)
        q, up = q_ref[here, :], up_ref[here, :]
        sp = dot(q, pk, NT) * scale
        parts = []
        if high > low:
            wk, wv = ck[low:high], cv[low:high]
            sw = dot(q, wk, NT) * scale
            key = lax.broadcasted_iota(jnp.int32, sw.shape, 1) + low
            slot = lax.broadcasted_iota(jnp.int32, sw.shape, 0) + (start - own)
            first = first_ref[start - own : start - own + count, :]
            sw = jnp.where((key >= first) & (key <= slot), sw, masked_score)
            parts = [(sp, pk, pv, 0), (sw, wk, wv, shared + low)]
        else:
            spot = lax.broadcasted_iota(jnp.int32, sp.shape, 1)
            key = lax.bitwise_xor(spot // own, me) * own + spot % own
            slot = lax.broadcasted_iota(jnp.int32, sp.shape, 0) + (me * own + start)
            parts = [(jnp.where(key <= slot, sp, masked_score), pk, pv, 0)]
        highest = functools.reduce(jnp.maximum, [jnp.max(s, -1, keepdims=True) for s, *_ in parts])
        raised = [jnp.exp(s - highest) for s, *_ in parts]
        total = functools.reduce(jnp.add, [jnp.sum(r, -1, keepdims=True) for r in raised])
        inverse = 1.0 / total
        probs = [r * inverse for r in raised]
        lows = [p.astype(bf16) for p in probs]
        ctx = functools.reduce(jnp.add, [dot(p, v) for p, (_, _, v, _) in zip(lows, parts)])
        ctx_ref[here, :] = ctx.astype(bf16)
        dps = [dot(up, v, NT) for _, _, v, _ in parts]
        delta = functools.reduce(
            jnp.add, [jnp.sum(p * d, -1, keepdims=True) for p, d in zip(probs, dps)]
        )
        dss = [(p * (d - delta)).astype(bf16) for p, d in zip(probs, dps)]
        dq = functools.reduce(jnp.add, [dot(d, k) for d, (_, k, _, _) in zip(dss, parts)]) * scale
        c, s = cos_ref[here, :], sin_ref[here, :]
        grad_ref[here, :LANES] = rotated_back(dq[:, :LANES], c, s, kernel_roll).astype(bf16)
        grad_ref[here, LANES:HEAD_DIM] = dq[:, LANES:].astype(bf16)
        for p, d, (_, k, _, base) in zip(lows, dss, parts):
            there = slice(base, base + k.shape[0])
            dv_acc[there, :] += dot(p, up, TN)
            dk_acc[there, :] += dot(d, q, TN)

    chunk(0, own, 0, 0)
    step = 4 * LONGEST
    for at in range(0, tail, step):
        size = min(step, tail - at)
        chunk(own + at, size, max(0, at - LONGEST), at + size)

    for r in range(blocks):
        ref, there = (keep_ref, send_ref)[r % 2], slice(r * own, (r + 1) * own)
        ref[r // 2, 0] = (dk_acc[there, :] * scale).astype(bf16)
        ref[r // 2, 1] = dv_acc[there, :].astype(bf16)
    dk = dk_acc[shared:, :] * scale
    c, s = cos_ref[own:, :], sin_ref[own:, :]
    grad_ref[:own, HEAD_DIM:] = jnp.zeros((own, 2 * HEAD_DIM), bf16)
    grad_ref[own:, HEAD_DIM : HEAD_DIM + LANES] = rotated_back(
        dk[:, :LANES], c, s, kernel_roll
    ).astype(bf16)
    grad_ref[own:, HEAD_DIM + LANES : 2 * HEAD_DIM] = dk[:, LANES:].astype(bf16)
    grad_ref[own:, 2 * HEAD_DIM :] = dv_acc[shared:, :].astype(bf16)


def attention(chain, me, q, k, v, prompts, grad_context, first, cosine, signed):
    micro, heads, rows, _ = q.shape
    blocks = len(prompts)
    pieces = [piece for slot in prompts for piece in slot]
    own = pieces[0].shape[3]
    layout, at = [], 0
    for slot in prompts:
        layout.append(tuple(range(at, at + len(slot))))
        at += len(slot)
    shared, tail = blocks * own, rows - own
    head = pl.BlockSpec((None, None, rows, HEAD_DIM), lambda m, h, _: (m, h, 0, 0))
    prompt = [pl.BlockSpec((p.shape[0], None, None, own, HEAD_DIM), lambda m, h, _: (0, m, h, 0, 0)) for p in pieces]
    half = pl.BlockSpec((blocks // 2, 2, None, None, own, HEAD_DIM), lambda m, h, _: (0, 0, m, h, 0, 0))
    flat = pl.BlockSpec((rows, HEAD_DIM), lambda m, h, _: (m, h))
    table = pl.BlockSpec((None, rows, LANES), lambda m, h, _: (m, 0, 0))
    return chain.run(
        functools.partial(attention_kernel, layout),
        (me, q, k, v, grad_context, first, cosine, signed, *pieces),
        scalars=1,
        grid=(micro, heads),
        ins=[head, head, head, flat, pl.BlockSpec((None, tail, 1), lambda m, h, _: (m, 0, 0)), table, table] + prompt,
        outs=[flat, pl.BlockSpec((None, rows, 3 * HEAD_DIM), lambda m, h, _: (m, 0, h)), half, half],
        shapes=[array((micro * rows, heads * HEAD_DIM)), array((micro, rows, heads * 3 * HEAD_DIM))]
        + [array((blocks // 2, 2, micro, heads, own, HEAD_DIM))] * 2,
        scratch=[pltpu.VMEM((shared + tail, HEAD_DIM), f32)] * 2,
        name="attention",
    )


def fold_kernel(a_ref, b_ref, keep_ref, send_ref):
    for i, ref in enumerate((keep_ref, send_ref)):
        ref[0] = (a_ref[i].astype(f32) + b_ref[i].astype(f32)).astype(bf16)


def fold(chain, kept, got):
    slots, shape = kept.shape[0], kept.shape[1:]
    count = kept.size // (slots * HEAD_DIM)
    one = pl.BlockSpec((1, count, HEAD_DIM), lambda i: (i, 0, 0))
    two = pl.BlockSpec((2, count, HEAD_DIM), lambda i: (i, 0, 0))
    keep, send = chain.run(
        fold_kernel,
        (kept.reshape(slots, count, HEAD_DIM), got.reshape(slots, count, HEAD_DIM)),
        grid=(slots // 2,),
        ins=[two, two],
        outs=[one, one],
        shapes=[array((slots // 2, count, HEAD_DIM))] * 2,
        name="fold",
    )
    return keep.reshape((slots // 2,) + shape), send.reshape((slots // 2,) + shape)


def slot_of(j, me, part, low, size):
    return pl.ds(pl.multiple_of(lax.bitwise_xor(jnp.int32(j), me) * part + low, LANES), size)


def context_kernel(g_ref, w_ref, o_ref):
    o_ref[...] = dot(g_ref[...], w_ref[...]).astype(bf16)


def grad_context_of(chain, g, packed, wide):
    count, width = g.shape
    tile = count // 4
    at = packed.shape[1] // wide - 1
    return chain.run(
        context_kernel,
        (g, packed),
        grid=(count // tile,),
        ins=[pl.BlockSpec((tile, width), lambda i: (i, 0)), pl.BlockSpec((width, wide), lambda i: (0, at))],
        outs=[pl.BlockSpec((tile, wide), lambda i: (i, 0))],
        shapes=[array((count, wide))],
        name="grad_context",
    )[0]


def forward_kernel(spots, part, me_ref, n_ref, bias_ref, *refs):
    ups, (act_ref, slope_ref, up_ref) = refs[: len(spots)], refs[len(spots) :]
    me = me_ref[0]

    @pl.when(pl.program_id(1) == 0)
    def _():
        for (r, low), ref in zip(spots, ups):
            up_ref[slot_of(r, me, part, low, ref.shape[0]), :] = ref[...]

    h = dot(n_ref[...], up_ref[...]) + bias_ref[...]
    z = jnp.abs(h)
    e = jnp.exp(-0.5 * (h * h))
    t = 1.0 / (1.0 + TAIL_P * z)
    q = jnp.full_like(t, TAIL[0])
    for co in TAIL[1:]:
        q = q * t + co
    low = e * (t * q)
    cdf = jnp.where(h >= 0.0, 1.0 - low, low)
    act_ref[...] = (h * cdf).astype(bf16)
    slope_ref[...] = (cdf + h * (e * PEAK)).astype(bf16)


def spots_of(slots):
    spots, pieces = [], []
    for r, slot in enumerate(slots):
        low = 0
        for piece in slot:
            spots.append((r, low))
            pieces.append(piece)
            low += piece.shape[0]
    return spots, pieces


def ff_forward(chain, me, norm_two, ups, bias, rows):
    count, width = norm_two.shape
    spots, pieces = spots_of(ups)
    part, hidden = ups[0][0].shape
    cols = min(512, hidden)
    out = pl.BlockSpec((rows, cols), lambda c, r, _: (r, c))
    return chain.run(
        functools.partial(forward_kernel, spots, part),
        (me, norm_two, bias, *pieces),
        scalars=1,
        grid=(hidden // cols, count // rows),
        ins=[
            pl.BlockSpec((rows, width), lambda c, r, _: (r, 0)),
            pl.BlockSpec((1, cols), lambda c, r, _: (0, c)),
        ]
        + [pl.BlockSpec((p.shape[0], cols), lambda c, r, _: (0, c)) for p in pieces],
        outs=[out, out],
        shapes=[array((count, hidden))] * 2,
        scratch=[pltpu.VMEM((width, cols), bf16)],
        name="ff_forward",
    )


def stack_kernel(spots, *refs):
    o_ref = refs[-1]
    for (r, low), ref in zip(spots, refs):
        o_ref[r, low : low + ref.shape[0], :] = ref[...]


def stack(chain, slots):
    spots, pieces = spots_of(slots)
    part, hidden = slots[0][0].shape
    cols = min(512, hidden)
    return chain.run(
        functools.partial(stack_kernel, spots),
        tuple(pieces),
        grid=(hidden // cols,),
        ins=[pl.BlockSpec((p.shape[0], cols), lambda c: (0, c)) for p in pieces],
        outs=[pl.BlockSpec((len(slots), part, cols), lambda c: (0, 0, c))],
        shapes=[array((len(slots), part, hidden))],
        name="stack",
    )[0]


def backward_kernel(g_ref, down_ref, slope_ref, grad_ref, rows_ref):
    blocks, _, part = down_ref.shape

    @pl.when(pl.program_id(1) == 0)
    def _():
        for j in range(blocks):
            rows_ref[:, j * part : (j + 1) * part] = down_ref[j]

    ga = dot(g_ref[...], rows_ref[...], NT)
    grad_ref[...] = (ga * slope_ref[...].astype(f32)).astype(bf16)


def ff_backward(chain, g, down, slope, rows):
    count, width = g.shape
    blocks, hidden, part = down.shape
    cols = min(1024, hidden)
    out = pl.BlockSpec((rows, cols), lambda c, r: (r, c))
    return chain.run(
        backward_kernel,
        (g, down, slope),
        grid=(hidden // cols, count // rows),
        ins=[
            pl.BlockSpec((rows, width), lambda c, r: (r, 0)),
            pl.BlockSpec((blocks, cols, part), lambda c, r: (0, c, 0)),
            out,
        ],
        outs=[out],
        shapes=[array((count, hidden))],
        scratch=[pltpu.VMEM((cols, width), bf16)],
        name="ff_backward",
    )[0]


def mix_kernel(act_ref, ctx_ref, down_ref, dense_ref, *o_refs):
    total = dot(act_ref[...], down_ref[...])
    total += dot(ctx_ref[...], dense_ref[...], NT)
    size = total.shape[0] // len(o_refs)
    for i, ref in enumerate(o_refs):
        ref[...] = total[i * size : (i + 1) * size].astype(bf16)


def mix(chain, act, context, down, packed, rows, index, pieces):
    hidden = act.shape[1]
    wide = context.shape[1]
    blocks, _, part = down.shape
    size = rows // pieces
    at = packed.shape[1] // wide - 1
    return chain.run(
        mix_kernel,
        (act, context, down, packed),
        grid=(blocks,),
        ins=[
            pl.BlockSpec((rows, hidden), lambda j: (index, 0)),
            pl.BlockSpec((rows, wide), lambda j: (index, 0)),
            pl.BlockSpec((None, hidden, part), lambda j: (j, 0, 0)),
            pl.BlockSpec((part, wide), lambda j: (j, at)),
        ],
        outs=[pl.BlockSpec((size, part), lambda j: (0, j))] * pieces,
        shapes=[array((size, blocks * part))] * pieces,
        name="mix",
        key="mix%d" % min(index, 1),
    )


def second_grad_kernel(act_ref, ctx_ref, g_ref, o_ref):
    hidden = act_ref.shape[1]
    o_ref[:hidden, :] = dot(act_ref[...], g_ref[...], TN).astype(bf16)
    o_ref[hidden:, :] = dot(ctx_ref[...], g_ref[...], TN).astype(bf16)


def second_grads(chain, act, context, g, blocks):
    count, hidden = act.shape
    wide = context.shape[1]
    part = g.shape[1] // blocks
    return chain.run(
        second_grad_kernel,
        (act, context, g),
        grid=(blocks,),
        ins=[
            pl.BlockSpec((count, hidden), lambda j: (0, 0)),
            pl.BlockSpec((count, wide), lambda j: (0, 0)),
            pl.BlockSpec((count, part), lambda j: (0, j)),
        ],
        outs=[pl.BlockSpec((None, hidden + wide, part), lambda j: (j, 0, 0))],
        shapes=[array((blocks, hidden + wide, part))],
        name="second_grads",
    )[0]


def norm_grad_kernel(me_ref, gj_ref, gh_ref, wj_ref, wu_ref, x_ref, mean_ref, inv_ref, g1_ref, g2_ref, *outs):
    *o_refs, stat_ref, sum_ref = outs

    @pl.when(pl.program_id(0) == 0)
    def _():
        sum_ref[...] = jnp.sum(gj_ref[...].astype(f32), axis=0, keepdims=True)

    one = dot(gj_ref[...], wj_ref[...], NT)
    two = dot(gh_ref[...], wu_ref[...], NT)
    normed = (x_ref[...].astype(f32) - mean_ref[...]) * inv_ref[...]
    total = one * g1_ref[...] + two * g2_ref[...]
    size = total.shape[0] // len(o_refs)
    for i, ref in enumerate(o_refs):
        ref[...] = total[i * size : (i + 1) * size].astype(bf16)
    for i, term in enumerate((one * normed, one, two * normed, two)):
        stat_ref[i : i + 1, :] = jnp.sum(term, axis=0, keepdims=True)


def norm_grads(chain, me, grad_joined, grad_hidden, packed, up, x, mean, inverse, gain_one, gain_two, rows, index, pieces):
    width = x.shape[1]
    wide, hidden = grad_joined.shape[1], grad_hidden.shape[1]
    blocks, part, _ = up.shape
    size = rows // pieces
    column = pl.BlockSpec((rows, 1), lambda c, _: (index, 0))
    gain = pl.BlockSpec((1, part), lambda c, _: (0, c))
    return chain.run(
        norm_grad_kernel,
        (me, grad_joined, grad_hidden, packed, up, x, mean, inverse, gain_one, gain_two),
        scalars=1,
        grid=(blocks,),
        ins=[
            pl.BlockSpec((rows, wide), lambda c, _: (index, 0)),
            pl.BlockSpec((rows, hidden), lambda c, _: (index, 0)),
            pl.BlockSpec((part, wide), lambda c, _: (c, 0)),
            pl.BlockSpec((None, part, hidden), lambda c, me: (lax.bitwise_xor(c, me[0]), 0, 0)),
            pl.BlockSpec((rows, part), lambda c, _: (index, c)),
            column, column, gain, gain,
        ],
        outs=[pl.BlockSpec((size, part), lambda c, _: (0, c))] * pieces
        + [pl.BlockSpec((8, part), lambda c, _: (0, c)), pl.BlockSpec((1, wide), lambda c, _: (0, 0))],
        shapes=[array((size, width))] * pieces + [array((8, width), f32), array((1, wide), f32)],
        name="norm_grads",
        key="norm_grads%d" % min(index, 1),
    )


def prompt_kernel(keep_ref, got_ref, cos_ref, sin_ref, _, o_ref):
    total = keep_ref[...].astype(f32) + got_ref[...].astype(f32)

    @pl.when(pl.program_id(2) == 0)
    def _():
        first = rotated_back(total[:, :LANES], cos_ref[...], sin_ref[...], kernel_roll)
        o_ref[:, :LANES] = first.astype(bf16)
        o_ref[:, LANES:] = total[:, LANES:].astype(bf16)

    @pl.when(pl.program_id(2) == 1)
    def _():
        o_ref[...] = total.astype(bf16)


def put_prompt(chain, grad_joined, kept, got, cosine, signed):
    _, _, micro, heads, own, _ = kept.shape
    part = pl.BlockSpec((None, None, None, None, own, HEAD_DIM), lambda m, h, i: (0, i, m, h, 0, 0))
    table = pl.BlockSpec((None, own, LANES), lambda m, h, i: (m, 0, 0))
    return chain.run(
        prompt_kernel,
        (kept, got, cosine, signed, grad_joined),
        grid=(micro, heads, 2),
        ins=[part, part, table, table, ANY],
        outs=[pl.BlockSpec((None, own, HEAD_DIM), lambda m, h, i: (m, 0, 3 * h + 1 + i))],
        shapes=[array(grad_joined.shape)],
        aliases={4: 0},
        name="put_prompt",
    )[0]


def pair_kernel(a_ref, b_ref, o_ref):
    o_ref[...] = (a_ref[...].astype(f32) + b_ref[...].astype(f32)).astype(bf16)


def add_pair(chain, a, b, low, size):
    width = a.shape[1]
    tile = size // 2
    row = pl.BlockSpec((tile, width), lambda i: (low // tile + i, 0))
    return chain.run(
        pair_kernel,
        (a, b),
        grid=(size // tile,),
        ins=[row, row],
        outs=[pl.BlockSpec((tile, width), lambda i: (i, 0))],
        shapes=[array((size, width))],
        name="add_pair",
    )[0]


def output_kernel(a_ref, b_ref, x_ref, dense_ref, down_ref, o_ref):
    total = a_ref[...].astype(f32) + b_ref[...].astype(f32)
    o_ref[...] = (x_ref[...].astype(f32) + total + dense_ref[...] + down_ref[...]).astype(bf16)


def input_kernel(a_ref, b_ref, x_ref, g_ref, mean_ref, inv_ref, o_ref):
    total = a_ref[...].astype(f32) + b_ref[...].astype(f32)
    inverse = inv_ref[...]
    normed = (x_ref[...].astype(f32) - mean_ref[...]) * inverse
    centred = (
        total
        - jnp.mean(total, axis=-1, keepdims=True)
        - normed * jnp.mean(total * normed, axis=-1, keepdims=True)
    )
    o_ref[...] = (g_ref[...].astype(f32) + inverse * centred).astype(bf16)


def finish(chain, a, b, start, rows, columns=(), vectors=()):
    size, width = a.shape
    tile = size // 2
    at = start // tile
    here = pl.BlockSpec((tile, width), lambda i: (i, 0))
    there = pl.BlockSpec((tile, width), lambda i: (at + i, 0))
    column = pl.BlockSpec((tile, 1), lambda i: (at + i, 0))
    vector = pl.BlockSpec((1, width), lambda i: (0, 0))
    return chain.run(
        input_kernel if columns else output_kernel,
        (a, b, *rows, *columns, *vectors),
        grid=(size // tile,),
        ins=[here, here] + [there] * len(rows) + [column] * len(columns) + [vector] * len(vectors),
        outs=[here],
        shapes=[array((size, width))],
        name="finish",
    )[0]


def swap(value, axis, bit):
    size = lax.axis_size(axis)
    return lax.ppermute(value, axis, [(i, i ^ (1 << bit)) for i in range(size)])


def bits_of(axis):
    return lax.axis_size(axis).bit_length() - 1


def send_xor(value, axis, offset):
    size = lax.axis_size(axis)
    return lax.ppermute(value, axis, [(i, i ^ offset) for i in range(size)])


def join(*values):
    return lax.optimization_barrier(values)


class Gather:
    def __init__(self, value, axis):
        self.axis, self.size = axis, lax.axis_size(axis)
        self.direct = self.size != 8
        offsets = range(2, self.size, 2) if self.direct else (2, 4)
        self.slots = [None] * self.size
        self.slots[0] = [value]
        self.slots[1] = [send_xor(value, axis, 1)]
        for r in offsets:
            self.slots[r] = [send_xor(value, axis, r)]

    def first(self, *others):
        here = [r for r in range(self.size) if r and self.slots[r]]
        values = join(*[self.slots[r][0] for r in here], *others)
        for r, value in zip(here, values):
            self.slots[r] = [value]
        self.fresh = []
        if not self.direct:
            near, far = self.slots[2][0], self.slots[4][0]
            half = near.shape[0] // 2
            self.fresh = [send_xor(near[:half], self.axis, 4), send_xor(far[half:], self.axis, 2)]
        self.twins = [r for r in here if r > 1]
        self.fresh += [send_xor(self.slots[r][0], self.axis, 1) for r in self.twins]
        return values[len(here) :]

    def second(self, *others):
        values = join(*self.fresh, *others)
        if not self.direct:
            self.slots[6] = list(values[:2])
            self.slots[7] = [send_xor(piece, self.axis, 1) for piece in self.slots[6]]
        for r, value in zip(self.twins, values[len(self.fresh) - len(self.twins) :]):
            self.slots[r + 1] = [value]
        return values[len(self.fresh) :]


def gather_ordered(value, axis):
    index = lax.axis_index(axis)
    held = value[None]
    for bit in range(bits_of(axis)):
        other = swap(held, axis, bit)
        low = ((index >> bit) & 1) == 0
        held = jnp.concatenate([jnp.where(low, held, other), jnp.where(low, other, held)], 0)
    return held


def add_up(value, axis):
    for bit in range(bits_of(axis)):
        value = value + swap(value, axis, bit)
    return value


def own_rows(value, start, count):
    return lax.dynamic_slice_in_dim(value, start, count, 0)


def sum_rows(partial, axis):
    index = lax.axis_index(axis)
    held, start = partial, jnp.int32(0)
    for bit in range(bits_of(axis)):
        mine = (index >> bit) & 1
        half = held.shape[0] // 2
        other = swap(own_rows(held, (1 - mine) * half, half).astype(bf16), axis, bit)
        held = own_rows(held, mine * half, half).astype(f32) + other.astype(f32)
        start = start + mine * half
    return held, start


def spread_rows(share, axis):
    index = lax.axis_index(axis)
    held = share
    for bit in reversed(range(bits_of(axis))):
        mine = (index >> bit) & 1
        other = swap(held, axis, bit)
        held = jnp.where(
            mine == 0, jnp.concatenate([held, other], 0), jnp.concatenate([other, held], 0)
        )
    return held


TO_MIDDLE = [(0, 1), (3, 2)]
ACROSS = [(1, 2), (2, 1)]
TO_ENDS = [(1, 0), (2, 3)]


class Piece:
    def __init__(self, chain, partial, first, low, size, axis, closing):
        self.chain, self.axis, self.closing = chain, axis, closing
        self.partial, self.first, self.low, self.size = partial, first, low, size

    def cross(self):
        self.pair = add_pair(self.chain, self.partial, self.first, self.low, self.size)
        self.second = lax.ppermute(self.pair, self.axis, ACROSS)

    def close(self):
        self.own = self.closing(self.pair, self.second)
        self.third = lax.ppermute(self.own, self.axis, TO_ENDS)


def local(
    tokens,
    cont_lengths,
    first_gain,
    first_bias,
    second_gain,
    second_bias,
    joined_weight,
    joined_bias,
    dense_weight,
    dense_bias,
    up_weight,
    up_bias,
    down_weight,
    down_bias,
    cotangent,
):
    blocks, ranks = lax.axis_size("dp"), lax.axis_size("tensor")
    me = lax.axis_index("dp").astype(jnp.int32)
    micro, _, rows, width = tokens.shape
    count = micro * rows
    own = PROMPT // blocks
    tail = rows - own
    part = width // blocks
    heads = joined_weight.shape[1] // (3 * HEAD_DIM)
    wide = heads * HEAD_DIM
    hidden = up_weight.shape[1]
    x = tokens.reshape(count, width)
    g = cotangent.reshape(count, width)
    here = me.reshape(1)

    chain = Chain()
    packed, first_gain = join(pack(chain, joined_weight, dense_weight), first_gain)
    packed = lax.all_gather(packed, "dp", axis=0, tiled=True)
    down = lax.all_gather(down_weight, "dp", axis=0, tiled=False)

    vectors = (first_gain, first_bias, second_gain, second_bias, dense_bias, down_bias)
    small = jnp.concatenate([v.reshape(-1) for v in vectors + (joined_bias, up_bias)])
    small = gather_ordered(small, "dp")
    up_here, small = join(up_weight, small)
    ups = Gather(up_here, "dp")

    small = small.astype(f32)
    full = [small[:, i * part : (i + 1) * part].reshape(1, width) for i in range(6)]
    gain_one, bias_one, gain_two, bias_two, dense_add, down_add = full

    def by_head(start, like):
        piece = small[:, start : start + like.size].reshape((blocks,) + like.shape)
        return jnp.transpose(piece, (1, 0, 2)).reshape(1, -1)

    joined_add = by_head(6 * part, joined_bias)
    up_add = by_head(6 * part + joined_bias.size, up_bias)

    seg_ends = jnp.cumsum(cont_lengths[:, 0], axis=1)
    slots = jnp.arange(tail, dtype=jnp.int32)
    passed = (slots[None, :, None] >= seg_ends[:, None, :]).astype(jnp.int32)
    first = jnp.sum(passed * cont_lengths[:, 0][:, None, :], axis=2)
    prompt_pos = jnp.broadcast_to(me * own + jnp.arange(own, dtype=jnp.int32), (micro, own))
    positions = jnp.concatenate([prompt_pos, PROMPT + slots[None] - first], axis=1)
    cosine, signed = rope_tables(positions)

    norm_one, norm_two, mean, inverse, upstream_sum = norms(chain, x, g, gain_one, bias_one, gain_two, bias_two)
    norm_one, cosine, signed, packed = ups.first(norm_one, cosine, signed, packed)

    q, k, v, prompt = qkv(chain, norm_one.reshape(micro, rows, width), packed, joined_add, cosine, signed, own)
    (prompt,) = ups.second(prompt)
    prompts = Gather(prompt, "dp")
    act, slope = ff_forward(chain, here, norm_two, ups.slots, up_add, rows)
    (slope,) = prompts.first(slope)
    grad_context = grad_context_of(chain, g, packed, wide)
    (grad_context,) = prompts.second(grad_context)
    prompts, ups = prompts.slots, ups.slots

    line = ranks == 4
    pieces = 2
    size = rows // pieces
    context, grad_joined, kept, sent = attention(
        chain, here, q, k, v, prompts, grad_context, first[..., None], cosine, signed
    )
    got = send_xor(sent, "dp", 1)

    def close_output(start):
        return lambda a, b: finish(chain, a, b, start, (x,), vectors=(dense_add, down_add))

    def close_input(start):
        return lambda a, b: finish(chain, a, b, start, (x, g), columns=(mean, inverse))

    rank = lax.axis_index("tensor")
    end = ((rank == 0) | (rank == 3)).astype(jnp.int32).reshape(1)
    have = {"kept": kept, "got": got, "bit": 1, "joined": grad_joined, "stats": [], "joined_sums": [], "results": [None, None]}
    partials, sums = [None] * (2 * micro), []

    def along_rows(value, like):
        lead, span = like.shape
        value = jnp.transpose(value.reshape(lead, blocks, span), (1, 0, 2)).reshape(blocks, lead * span)
        return jnp.pad(value, ((0, 0), (0, part - lead * span))).reshape(1, width)

    def sums_of_all():
        stats = functools.reduce(jnp.add, have["stats"])
        joined_sums = functools.reduce(jnp.add, have["joined_sums"])
        rows_of = [stats, upstream_sum, along_rows(have["up_sums"], up_bias), along_rows(joined_sums, joined_bias)]
        return jnp.concatenate(rows_of + [jnp.zeros((1, width), f32)], 0)

    def scattered(value):
        return lax.psum_scatter(value, "dp", scatter_dimension=0, tiled=value.ndim == 2)

    def step(what, *which):
        if what == "mix":
            partials[which[0]] = mix(chain, act, context, down, packed, rows, which[0], 1 if which[0] in MERGED else pieces)
        elif what == "go":
            stage, i, *behind = which
            partial, start = partials[stage][i], (stage % micro) * rows + i * size
            if line:
                if behind:
                    piece = sums[behind[0]]
                    partial, piece.pair = join(partial, piece.pair)
                got = lax.ppermute(partial, "tensor", TO_MIDDLE)
                for low in range(0, partial.shape[0], size):
                    closing = (close_output, close_input)[stage // micro](start + low)
                    sums.append(Piece(chain, partial, got, low, size, "tensor", closing))
        elif what == "fold":
            for _ in range(1 if line or have["bit"] == 1 else bits_of("dp") - 2):
                kept, sent = fold(chain, have["kept"], have["got"])
                have["kept"], have["got"] = kept, send_xor(sent, "dp", 1 << have["bit"])
                have["bit"] += 1
        elif what == "ffb":
            have["hidden"] = ff_backward(chain, g, down, slope, rows)
        elif what == "up":
            have["up"], have["up_sums"] = outer(chain, norm_two, have["hidden"], "outer0")
        elif what == "stack":
            have["ups"] = stack(chain, ups)
        elif what == "second":
            have["second"] = second_grads(chain, act, context, g, blocks)
        elif what == "joined":
            have["joined_grad"] = outer_more(chain, norm_one, have["joined"], sums_of_all(), "outer1")
        elif what == "send":
            if line and len(which) > 1:
                piece = sums[which[1]]
                piece.pair, have[which[0]] = join(piece.pair, have[which[0]])
            have[which[0]] = scattered(have[which[0]])
        elif what == "prompt":
            put = put_prompt(chain, have["joined"], have["kept"], have["got"], cosine, signed)
            have["joined"] = put.reshape(count, 3 * wide)
        elif what == "norm":
            m = which[0]
            *parts, stat, joined_sums = norm_grads(
                chain, here, have["joined"], have["hidden"], packed, have["ups"], x, mean, inverse, gain_one, gain_two,
                rows, m, 1 if micro + m in MERGED else pieces,
            )
            partials[micro + m] = parts
            have["stats"].append(stat[:4])
            have["joined_sums"].append(joined_sums)
        elif not line:
            pass
        elif what == "cross":
            sums[which[0]].cross()
        elif what == "close":
            k = which[0]
            if 1 <= k < BACK:
                sums[k].pair, sums[k - 1].third = join(sums[k].pair, sums[k - 1].third)
            sums[k].close()
            if k == END_TIE:
                sums[k].own, have["joined_grad"] = join(sums[k].own, have["joined_grad"])
        elif what == "gains":
            vector = have["joined_grad"][:, 3 * wide : 3 * wide + 8].astype(f32).T
            half = vector[:4] + swap(vector[:4], "tensor", 0)
            sums[7].own, have["gains"] = join(sums[7].own, half)
        elif what == "place":
            low, high = which
            kind = low // (2 * pieces)
            have["results"][kind] = place(chain, have["results"][kind], end, sums[low:high], low * size % count, count)
        elif what == "tie":
            piece = sums[which[1]]
            piece.pair, have[which[0]] = join(piece.pair, have[which[0]])

    for one in PLAN:
        step(*one)
    up_out, second_out, joined_out = have["up"], have["second"], have["joined_grad"]
    joined_out = joined_out.astype(f32)
    vector = joined_out[:, 3 * wide : 3 * wide + 8].T
    joined_out = joined_out[:, : 3 * wide]
    if line:
        gains = have["gains"] + swap(have["gains"], "tensor", 1)
        output, input_grad = [r.reshape(micro, rows, width) for r in have["results"]]
    else:
        gains = add_up(vector[:4], "tensor")
    if not line:
        outputs, inputs = [], []
        for m in range(micro):
            share, start = sum_rows(jnp.concatenate(partials[m]), "tensor")
            span = share.shape[0]
            mine = own_rows(x, m * rows + start, span).astype(f32)
            outputs.append(spread_rows((mine + share + dense_add + down_add).astype(bf16), "tensor"))
            share, start = sum_rows(jnp.concatenate(partials[micro + m]), "tensor")
            start = m * rows + start
            row_inverse = own_rows(inverse, start, span)
            row_normed = (own_rows(x, start, span).astype(f32) - own_rows(mean, start, span)) * row_inverse
            centred = (
                share
                - jnp.mean(share, axis=-1, keepdims=True)
                - row_normed * jnp.mean(share * row_normed, axis=-1, keepdims=True)
            )
            result = own_rows(g, start, span).astype(f32) + row_inverse * centred
            inputs.append(spread_rows(result.astype(bf16), "tensor"))
        output, input_grad = jnp.stack(outputs), jnp.stack(inputs)

    return (
        output[:, None],
        input_grad[:, None],
        gains[0],
        gains[1],
        gains[2],
        gains[3],
        joined_out,
        vector[6, : joined_bias.size].reshape(joined_bias.shape),
        second_out[hidden:].astype(f32),
        vector[4],
        up_out.astype(f32),
        vector[5, : up_bias.size].reshape(up_bias.shape),
        second_out[:hidden].astype(f32),
        vector[4],
    )


def solution(mesh):
    placed = (
        P(None, "dp", None, None),
        P(None, "dp", None),
        P("dp"),
        P("dp"),
        P("dp"),
        P("dp"),
        P("dp", "tensor"),
        P("tensor", "dp"),
        P("tensor", "dp"),
        P("dp"),
        P("dp", "tensor"),
        P("tensor", "dp"),
        P("tensor", "dp"),
        P("dp"),
        P(None, "dp", None, None),
    )
    return jax.shard_map(
        local,
        mesh=mesh,
        in_specs=placed,
        out_specs=(
            P(None, "dp", None, None),
            P(None, "dp", None, None),
            P("dp"),
            P("dp"),
            P("dp"),
            P("dp"),
            P("dp", "tensor"),
            P("tensor", "dp"),
            P("tensor", "dp"),
            P("dp"),
            P("dp", "tensor"),
            P("tensor", "dp"),
            P("tensor", "dp"),
            P("dp"),
        ),
        check_vma=False,
    )
```
